32 devices in a mesh: seq: 8 (over z, y), head: 4 (over x, core).
Axes of the slice: x: 2, y: 2, z: 4, core: 2. Of those that a mesh axis runs over, the one named last changes fastest.
Arguments:
- x_in: bfloat16 [4096, 4096], P('seq', 'head'), may hold values from -160 to 160
- gate_in: bfloat16 [4096, 4096], P('seq', 'head'), may hold values from -6 to 6
- bc_in: bfloat16 [4096, 256], P('seq'), may hold values from -2.390625 to 2.390625
- step_in: float32 [4096, 64], P('seq', 'head'), may hold values from 0.005 to 0.05
- decay_code: int32 [2, 4096, 64], P(None, 'seq', 'head'), may hold values from 1 to 16384
- decay_rate: float32 [2, 64], P(None, 'head'), may hold values from 1.4648437e-05 to 0.012
- skip_gain: float32 [2, 64], P(None, 'head'), may hold values from 0.25 to 1.5
- norm_gain: float32 [4096], P('head'), may hold values from 0.1 to 1.9
- w_out: bfloat16 [4096, 4096], P('head', 'seq'), may hold values from -0.09375 to 0.09375
- resid_in: bfloat16 [4096, 4096], P('seq', 'head'), may hold values from -25 to 25
- resid_gain: float32 [4096], replicated, may hold values from 0.1 to 1.9
- w_in_x: bfloat16 [4096, 4096], P('seq', 'head'), may hold values from -1 to 1
- w_in_bc: bfloat16 [4096, 256], P('seq'), may hold values from -0.09375 to 0.09375
- w_in_dt: bfloat16 [4096, 64], P('seq', 'head'), may hold values from -0.09375 to 0.09375
- step_time_bias: float32 [64], P('head'), may hold values from -3 to -1
- conv_x: bfloat16 [4, 4096], P(None, 'head'), may hold values from -3 to 3
- conv_bc: bfloat16 [4, 256], replicated, may hold values from -3 to 3
Outputs:
- resid_out: bfloat16 [4096, 4096], P('seq', 'head')
- mixer_out: bfloat16 [4096, 4096], P('seq', 'head')
The draws below stay inside these ranges and needn't reach their ends.
All inputs are finite; a program needn't handle non-finite values.
Results may differ from the reference program's by a relative error of at most 0.007.
Values may be sent and summed in bfloat16 or wider, within the bound.
No kernel may reach another device: no remote copies, remote signals or barrier semaphores. Data moves between devices by JAX's collectives and lax.ppermute only.
A program may use at most 128 MiB of HBM per device.

```python
import math
import jax
import jax.numpy as jnp
from jax import lax

D = 4096
HEADS = 64
HEAD_CHANNELS = 64
STATE = 128
GROUP = 256
CONV = 4
INNER = 4096
SEQUENCE_TOKENS = 4096


def rough_scale(key, count, spread):
    return 10.0 ** jax.random.uniform(key, (count,), jnp.float32, -spread, spread)


def base_values(key, shape):
    return jax.random.truncated_normal(key, -4.0, 4.0, shape, jnp.float32)


def draw_x_in(key, part):
    keys = jax.random.split(key, 3)
    values = base_values(keys[0], (SEQUENCE_TOKENS, INNER))
    row_scale = rough_scale(keys[1], SEQUENCE_TOKENS, 0.5)
    rising = 3.0 ** (jnp.arange(INNER, dtype=jnp.float32) / (INNER - 1))
    column_factor = rough_scale(keys[2], INNER, 0.5) * rising
    values = values * row_scale[:, None] * column_factor[None, :]
    return jnp.clip(values, -160.0, 160.0).astype(jnp.bfloat16)


def draw_resid_in(key, part):
    keys = jax.random.split(key, 3)
    values = base_values(keys[0], (SEQUENCE_TOKENS, D))
    row_scale = rough_scale(keys[1], SEQUENCE_TOKENS, 0.5)
    rising = 3.0 ** (jnp.arange(D, dtype=jnp.float32) / (D - 1)) / 1.7
    column_factor = rough_scale(keys[2], D, 0.5) * rising
    values = values * row_scale[:, None] * column_factor[None, :]
    return jnp.clip(values, -25.0, 25.0).astype(jnp.bfloat16)


def draw_w_in_x(key, part):
    keys = jax.random.split(key, 2)
    values = base_values(keys[0], (D, INNER)) * D ** (-0.5)
    rising = 3.0 ** (jnp.arange(INNER, dtype=jnp.float32) / (INNER - 1))
    column_factor = rough_scale(keys[1], INNER, 0.5) * rising
    values = values * column_factor[None, :]
    return jnp.clip(values, -1.0, 1.0).astype(jnp.bfloat16)


def draw_decay_code(key, part):
    keys = jax.random.split(key, 3)
    block_count = SEQUENCE_TOKENS // GROUP
    level = jax.random.randint(keys[0], (2, block_count, 1), 1, 3) * 2
    level = jnp.repeat(level, GROUP, axis=1)
    decay_labels = jax.random.randint(keys[1], (2, SEQUENCE_TOKENS, HEADS), 1, 2 * level)
    device_spots = jax.random.randint(keys[2], (2, 2), 0, SEQUENCE_TOKENS)
    transfer_group = jnp.any(jnp.arange(SEQUENCE_TOKENS, dtype=jnp.int32)[None, None, :] == device_spots[:, :, None], axis=1)
    return jnp.where(transfer_group[:, :, None], 4 * SEQUENCE_TOKENS, decay_labels).astype(jnp.int32)


def draw_decay_rate(key, part):
    keys = jax.random.split(key, 3)
    share = 0.5
    slow_pick = jax.random.uniform(keys[0], (2, HEADS), jnp.float32) < share
    slow_rate = jnp.exp(jax.random.uniform(keys[1], (2, HEADS), jnp.float32, math.log(0.25), math.log(0.6))) / (4.0 * SEQUENCE_TOKENS)
    fast_rate = jnp.exp(jax.random.uniform(keys[2], (2, HEADS), jnp.float32, math.log(0.006), math.log(0.012)))
    return jnp.where(slow_pick, slow_rate, fast_rate).astype(jnp.float32)


def steps_of(rng, extent, cuts, smallest, largest):
    def one(position, blocks):
        draws = jax.random.uniform(jax.random.fold_in(jax.random.fold_in(rng, 6), position), (blocks,), jnp.float32, smallest / len(cuts), largest / len(cuts))
        return jnp.repeat(jnp.exp(draws), extent[position] // blocks).reshape((-1,) + (1,) * (len(extent) - position - 1))

    factor_of = one(*cuts[0])
    for cut in cuts[1:]:
        factor_of = factor_of * one(*cut)
    return factor_of


def bell_draw(rng, shape, scale, bound, pieces=(), held_as=jnp.bfloat16):
    drawn = scale * jax.random.normal(rng, shape, jnp.float32)
    if pieces:
        drawn = drawn * steps_of(rng, shape, pieces, -0.22, 0.18)
    return jnp.clip(drawn, -bound, bound).astype(held_as)


def setup_inputs(seed: int = 0) -> dict:
    arg_keys = jax.random.split(jax.random.key(seed), 18)
    return {
        "x_in": draw_x_in(jax.random.fold_in(arg_keys[17], 71), 0),
        "gate_in": bell_draw(arg_keys[1], (SEQUENCE_TOKENS, INNER), 1.0, 6.0, ((0, 8), (1, 4))),
        "bc_in": bell_draw(arg_keys[2], (SEQUENCE_TOKENS, 2 * STATE), 0.3, 2.390625, ((0, 8),)),
        "step_in": jnp.clip(jnp.exp(math.log(0.05) - 2.3025851 * jax.random.uniform(arg_keys[3], (SEQUENCE_TOKENS, HEADS), jnp.float32) ** steps_of(arg_keys[3], (SEQUENCE_TOKENS, HEADS), ((0, 8), (1, 4)), -0.2, 0.2)), 0.005, 0.05),
        "decay_code": draw_decay_code(jax.random.fold_in(arg_keys[17], 71), 0),
        "decay_rate": draw_decay_rate(jax.random.fold_in(arg_keys[17], 71), 0),
        "skip_gain": jnp.clip(0.25 + 1.25 * jax.random.uniform(arg_keys[6], (2, HEADS), jnp.float32) ** steps_of(arg_keys[6], (2, HEADS), ((1, 4),), -0.2, 0.2), 0.25, 1.5),
        "norm_gain": jnp.clip(1.0 + 0.18 * jax.random.normal(arg_keys[7], (INNER,), jnp.float32), 0.1, 1.9),
        "w_out": bell_draw(arg_keys[8], (INNER, D), INNER ** -0.5, 0.09375, ((0, 4), (1, 8))),
        "resid_in": draw_resid_in(jax.random.fold_in(arg_keys[17], 71), 0),
        "resid_gain": jnp.clip(1.0 + 0.18 * jax.random.normal(arg_keys[10], (D,), jnp.float32), 0.1, 1.9),
        "w_in_x": draw_w_in_x(jax.random.fold_in(arg_keys[17], 71), 0),
        "w_in_bc": bell_draw(arg_keys[12], (D, 2 * STATE), D ** -0.5, 0.09375, ((0, 8),)),
        "w_in_dt": bell_draw(arg_keys[13], (D, HEADS), D ** -0.5, 0.09375, ((0, 8), (1, 4))),
        "step_time_bias": jnp.clip(-3.0 + 2.0 * jax.random.uniform(arg_keys[14], (HEADS,), jnp.float32) ** steps_of(arg_keys[14], (HEADS,), ((0, 4),), -0.2, 0.2), -3.0, -1.0),
        "conv_x": bell_draw(arg_keys[15], (CONV, INNER), CONV ** -0.5, 3.0, ((1, 4),)),
        "conv_bc": bell_draw(arg_keys[16], (CONV, 2 * STATE), CONV ** -0.5, 3.0),
    }


def log_decay(decay_labels, rates):
    return -jnp.minimum(decay_labels.astype(jnp.float32) * rates[None, :], 20.0)

def group_terms(input_block, b_block, c_block, step_block, decay_block):
    length = input_block.shape[0]
    head_count = step_block.shape[1]
    input_heads = input_block.reshape(length, head_count, HEAD_CHANNELS)
    cumulative = jnp.cumsum(decay_block, axis=0)
    across = cumulative.T
    segment = across[:, :, None] - across[:, None, :]
    lower_mask = (lax.broadcasted_iota(jnp.int32, (length, length), 0) >= lax.broadcasted_iota(jnp.int32, (length, length), 1))[None, :, :]
    scores = jnp.dot(c_block, b_block.T, preferred_element_type=jnp.float32)
    weights_mix = (jnp.where(lower_mask, jnp.exp(jnp.minimum(segment, 0.0)), 0.0) * scores[None, :, :] * step_block.T[:, None, :]).astype(jnp.bfloat16)
    diag_part = jnp.einsum('hij,jhp->ihp', weights_mix.astype(jnp.float32), input_heads.astype(jnp.float32))
    end_weight = jnp.exp(cumulative[-1][None, :] - cumulative) * step_block
    scaled_input = (input_heads.astype(jnp.float32) * end_weight[:, :, None]).astype(jnp.bfloat16)
    local_state = jnp.einsum('jhp,jn->hpn', scaled_input.astype(jnp.float32), b_block.astype(jnp.float32))
    return (diag_part, cumulative, local_state, cumulative[-1])

def ssd_layer(inputs, bc_values, step_values, decay_values, skip_values):
    state_width = bc_values.shape[1] // 2
    head_count = step_values.shape[1]
    token_count = inputs.shape[0]
    block_count = token_count // GROUP

    def advance(carry_state, block_data):
        input_block, bc_block, step_block, decay_block = block_data
        c_block = bc_block[:, state_width:]
        diag_part, cumulative, local_state, total_decay = group_terms(input_block, bc_block[:, :state_width], c_block, step_block, decay_block)
        carried_part = jnp.einsum('in,hpn->ihp', c_block.astype(jnp.float32), carry_state, precision=lax.Precision.HIGH) * jnp.exp(cumulative)[:, :, None]
        next_state = jnp.exp(total_decay)[:, None, None] * carry_state + local_state
        return (next_state, diag_part + carried_part)
    blocks = (inputs.reshape(block_count, GROUP, inputs.shape[1]), bc_values.reshape(block_count, GROUP, bc_values.shape[1]), step_values.reshape(block_count, GROUP, head_count), decay_values.reshape(block_count, GROUP, head_count))
    initial = jnp.zeros((head_count, HEAD_CHANNELS, state_width), jnp.float32)
    final_state, outputs = lax.scan(advance, initial, blocks)
    mixed = outputs.reshape(token_count, head_count, HEAD_CHANNELS)
    mixed = mixed + skip_values[None, :, None] * inputs.reshape(token_count, head_count, HEAD_CHANNELS).astype(jnp.float32)
    return mixed.reshape(token_count, head_count * HEAD_CHANNELS)

def rms_scale(values):
    return lax.rsqrt(lax.optimization_barrier(jnp.mean(values * values, axis=1, keepdims=True)) + 1e-05)

def causal_conv(padded, kernel, length):
    total = padded[0:length].astype(jnp.float32) * kernel[0].astype(jnp.float32)[None, :]
    for tap_index in range(1, kernel.shape[0]):
        total = total + padded[tap_index:tap_index + length].astype(jnp.float32) * kernel[tap_index].astype(jnp.float32)[None, :]
    return total

def reference(x_in, gate_in, bc_in, step_in, decay_code, decay_rate, skip_gain, norm_gain, w_out, resid_in, resid_gain, w_in_x, w_in_bc, w_in_dt, step_time_bias, conv_x, conv_bc):
    token_count = x_in.shape[0]
    decay_one = log_decay(decay_code[0], decay_rate[0])
    mixed_one = ssd_layer(x_in, bc_in, step_in, decay_one, skip_gain[0])
    gated = mixed_one * jax.nn.silu(gate_in.astype(jnp.float32))
    normed = (gated * rms_scale(gated) * norm_gain[None, :]).astype(jnp.bfloat16)
    resid_out = (resid_in.astype(jnp.float32) + jnp.dot(normed, w_out, preferred_element_type=jnp.float32)).astype(jnp.bfloat16)
    hidden = resid_out.astype(jnp.float32)
    hidden_norm = (hidden * rms_scale(hidden) * resid_gain[None, :]).astype(jnp.bfloat16)
    x_pre = jnp.dot(hidden_norm, w_in_x, preferred_element_type=jnp.float32).astype(jnp.bfloat16)
    bc_pre = jnp.dot(hidden_norm, w_in_bc, preferred_element_type=jnp.float32).astype(jnp.bfloat16)
    step_two = jax.nn.softplus(jnp.dot(hidden_norm, w_in_dt, preferred_element_type=jnp.float32) + step_time_bias[None, :])
    conv_taps = conv_x.shape[0]
    x_padded = jnp.concatenate([jnp.zeros((conv_taps - 1, x_pre.shape[1]), jnp.bfloat16), x_pre], axis=0)
    bc_padded = jnp.concatenate([jnp.zeros((conv_taps - 1, bc_pre.shape[1]), jnp.bfloat16), bc_pre], axis=0)
    x_two = jax.nn.silu(causal_conv(x_padded, conv_x, token_count)).astype(jnp.bfloat16)
    bc_two = jax.nn.silu(causal_conv(bc_padded, conv_bc, token_count)).astype(jnp.bfloat16)
    decay_two = log_decay(decay_code[1], decay_rate[1])
    mixed_two = ssd_layer(x_two, bc_two, step_two, decay_two, skip_gain[1])
    mixer_out = (mixed_two * rms_scale(mixed_two)).astype(jnp.bfloat16)
    return (resid_out, mixer_out)
```

```python
import jax
import jax.numpy as jnp
from jax import lax
from jax.sharding import PartitionSpec as P

HEAD_CHANNELS = 64
GROUP = 256
HALO = 16
F32 = jnp.float32
BF16 = jnp.bfloat16


def z_shift(value, by):
    n = lax.axis_size("seq")
    pairs = [(i, i + 2 * by) for i in range(n) if 0 <= i + 2 * by < n]
    return lax.ppermute(value, "seq", pairs)


def flip(value, axis, bit):
    n = lax.axis_size(axis)
    return lax.ppermute(value, axis, [(i, i ^ bit) for i in range(n)])


def y_swap(value):
    return flip(value, "seq", 1)


def x_swap(value):
    return flip(value, "head", 2)


def c_swap(value):
    return flip(value, "head", 1)


def z_gather(value, place):
    size = lax.axis_size("seq") // 2
    if size == 4:
        up1, down1 = z_shift(value, 1), z_shift(value, -1)
        up2, down2 = z_shift(up1, 1), z_shift(down1, -1)
        up3, down3 = z_shift(up2, 1), z_shift(down2, -1)
        first = jnp.where(place >= 1, up1, down1)
        second = jnp.where(place >= 2, up2, down2)
        third = jnp.where(place == 0, down3, jnp.where(place == 3, up3, down1))
        return [
            (place, value),
            (jnp.where(place >= 1, place - 1, 1), first),
            ((place + 2) % 4, second),
            (jnp.where(place == 0, 3, jnp.where(place == 3, 0, place + 1)), third),
        ]
    groups = [[2 * i + y for i in range(size)] for y in range(2)]
    whole = lax.all_gather(value, "seq", axis_index_groups=groups)
    return [(i, whole[i]) for i in range(size)]


def log_decay(decay_labels, rates):
    return -jnp.minimum(decay_labels.astype(F32) * rates[None, :], 20.0)


def group_terms(input_block, b_block, c_block, step_block, decay_block):
    length = input_block.shape[0]
    head_count = step_block.shape[1]
    input_heads = input_block.reshape(length, head_count, HEAD_CHANNELS)
    cumulative = jnp.cumsum(decay_block, axis=0)
    across = cumulative.T
    segment = across[:, :, None] - across[:, None, :]
    lower_mask = (
        lax.broadcasted_iota(jnp.int32, (length, length), 0)
        >= lax.broadcasted_iota(jnp.int32, (length, length), 1)
    )[None, :, :]
    scores = jnp.dot(c_block, b_block.T, preferred_element_type=F32)
    weights_mix = (
        jnp.where(lower_mask, jnp.exp(jnp.minimum(segment, 0.0)), 0.0)
        * scores[None, :, :]
        * step_block.T[:, None, :]
    ).astype(BF16)
    diag_part = jnp.einsum("hij,jhp->ihp", weights_mix, input_heads, preferred_element_type=F32)
    end_weight = jnp.exp(cumulative[-1][None, :] - cumulative) * step_block
    scaled_input = (input_heads * end_weight[:, :, None]).astype(BF16)
    local_state = jnp.einsum("jhp,jn->hpn", scaled_input, b_block, preferred_element_type=F32)
    return (diag_part, cumulative, local_state, cumulative[-1])


def local_pass(inputs, bc_values, step_values, decay_values):
    state_width = bc_values.shape[1] // 2
    head_count = step_values.shape[1]
    pieces = []
    end_state = jnp.zeros((head_count, HEAD_CHANNELS, state_width), F32)
    end_decay = jnp.zeros((head_count,), F32)
    for first_row in range(0, inputs.shape[0], GROUP):
        last_row = first_row + GROUP
        terms = group_terms(
            inputs[first_row:last_row],
            bc_values[first_row:last_row, :state_width],
            bc_values[first_row:last_row, state_width:],
            step_values[first_row:last_row],
            decay_values[first_row:last_row],
        )
        pieces.append(terms)
        end_state = jnp.exp(terms[3])[:, None, None] * end_state + terms[2]
        end_decay = end_decay + terms[3]
    return (pieces, end_state, end_decay)


def coarse(value):
    return lax.reduce_precision(value, 8, 7)


def pack(state, decay):
    heads, channels, width = state.shape
    high = coarse(decay)
    middle = coarse(decay - high)
    low = decay - high - middle
    tail = jnp.zeros((16, width), F32).at[:3, :heads].set(jnp.stack([high, middle, low]))
    return jnp.concatenate([state.reshape(heads * channels, width), tail], axis=0).astype(BF16)


def unpack(payload, heads):
    width = payload.shape[1]
    rows = payload.shape[0] - 16
    values = payload.astype(F32)
    tail = values[rows : rows + 3, :heads]
    return values[:rows].reshape(heads, rows // heads, width), tail[0] + tail[1] + tail[2]


def decayed(decay, state):
    return jnp.exp(decay)[:, None, None] * state


def carried_in(state, decay, y):
    heads = decay.shape[0]
    other_state, other_decay = unpack(y_swap(pack(state, decay)), heads)
    first = y == 0
    early_state = jnp.where(first, state, other_state)
    early_decay = jnp.where(first, decay, other_decay)
    late_state = jnp.where(first, other_state, state)
    late_decay = jnp.where(first, other_decay, decay)
    window, window_decay = decayed(late_decay, early_state) + late_state, early_decay + late_decay
    before, before_decay = jnp.zeros_like(state), jnp.zeros_like(decay)
    reach = 1
    size = lax.axis_size("seq") // 2
    while reach < size:
        far, far_decay = unpack(z_shift(pack(window, window_decay), reach), heads)
        before = before + decayed(before_decay, far)
        before_decay = before_decay + far_decay
        window = window + decayed(window_decay, far)
        window_decay = window_decay + far_decay
        reach *= 2
    return jnp.where(first, before, decayed(early_decay, before) + early_state)


def finish_pass(pieces, inputs, bc_values, skip_values, carried):
    state_width = bc_values.shape[1] // 2
    head_count = skip_values.shape[0]
    token_count = inputs.shape[0]
    carry_state = carried
    outputs = []
    for block_position in range(len(pieces)):
        diag_part, cumulative, local_state, total_decay = pieces[block_position]
        first_row = block_position * GROUP
        c_block = bc_values[first_row : first_row + GROUP, state_width:]
        carried_part = (
            jnp.einsum(
                "in,hpn->ihp",
                c_block.astype(F32),
                carry_state,
                precision=lax.Precision.HIGH,
            )
            * jnp.exp(cumulative)[:, :, None]
        )
        outputs.append(diag_part + carried_part)
        carry_state = decayed(total_decay, carry_state) + local_state
    mixed = jnp.concatenate(outputs, axis=0)
    mixed = mixed + skip_values[None, :, None] * inputs.reshape(
        token_count, head_count, HEAD_CHANNELS
    ).astype(F32)
    return mixed.reshape(token_count, head_count * HEAD_CHANNELS)


def causal_conv(padded, kernel, length):
    first = padded.shape[0] - length - kernel.shape[0] + 1
    total = 0.0
    for tap_index in range(kernel.shape[0]):
        start = first + tap_index
        total = (
            total
            + padded[start : start + length].astype(F32) * kernel[tap_index].astype(F32)[None, :]
        )
    return total


def pick(stack, index):
    return lax.dynamic_index_in_dim(stack, index, 0, False)


def on_device(
    x_in,
    gate_in,
    bc_in,
    step_in,
    decay_code,
    decay_rate,
    skip_gain,
    norm_gain,
    w_out,
    resid_in,
    resid_gain,
    w_in_x,
    w_in_bc,
    w_in_dt,
    step_time_bias,
    conv_x,
    conv_bc,
):
    tokens, width = x_in.shape
    seq_size, head_size = lax.axis_size("seq"), lax.axis_size("head")
    z_size = seq_size // 2
    seq_place, head = lax.axis_index("seq"), lax.axis_index("head")
    z, y = seq_place // 2, seq_place % 2
    x_bit, c_bit = head // 2, head % 2
    inner_count = width * head_size
    pair_tokens = 2 * tokens
    block = w_out.shape[1]
    half = width // 2
    per_head = z_size // head_size
    first = y == 0

    share = w_in_bc.shape[1] // head_size
    bc_weight = lax.dynamic_slice_in_dim(w_in_bc, head * share, share, 1)
    w_in = jnp.concatenate([w_in_x, bc_weight, w_in_dt], axis=1)
    out_blocks = z_gather(w_out, z)
    in_blocks = z_gather(w_in, z)

    parts = resid_in.reshape(tokens, per_head, 2, block)
    resid_own = lax.dynamic_index_in_dim(parts, y, 2, False).reshape(tokens, half)
    resid_far = y_swap(lax.dynamic_index_in_dim(parts, 1 - y, 2, False).reshape(tokens, half))

    decay_one = log_decay(decay_code[0], decay_rate[0])
    pieces_one, state_one, total_one = local_pass(x_in, bc_in, step_in, decay_one)
    carried_one = carried_in(state_one, total_one, y)
    mixed_one = finish_pass(pieces_one, x_in, bc_in, skip_gain[0], carried_one)
    gated = mixed_one * jax.nn.silu(gate_in.astype(F32))
    scaled = (gated * norm_gain[None, :]).astype(BF16)
    scaled_far = y_swap(scaled)
    square_own = lax.psum(jnp.sum(gated * gated, axis=1), "head")
    square_far = y_swap(square_own)
    both = jnp.concatenate(
        [jnp.where(first, scaled, scaled_far), jnp.where(first, scaled_far, scaled)], axis=0
    )
    square_one = jnp.concatenate(
        [jnp.where(first, square_own, square_far), jnp.where(first, square_far, square_own)]
    )
    resid = jnp.concatenate(
        [jnp.where(first, resid_own, resid_far), jnp.where(first, resid_far, resid_own)], axis=0
    ).astype(F32)

    products = [
        jnp.dot(both, part, preferred_element_type=F32).astype(BF16) for _, part in out_blocks
    ]
    stack = jnp.stack(products)
    place_of = jnp.zeros((z_size,), jnp.int32)
    for slot in range(z_size):
        place_of = place_of.at[out_blocks[slot][0]].set(slot)

    def for_head(target):
        picks = [pick(stack, place_of[target * per_head + i]) for i in range(per_head)]
        return picks[0] if per_head == 1 else jnp.concatenate(picks, axis=1)

    kept = [for_head(2 * (x_bit ^ i) + c_bit) for i in range(2)]
    sent = c_swap(jnp.stack([for_head(2 * (x_bit ^ i) + (1 - c_bit)) for i in range(2)]))
    sums = [kept[i].astype(F32) + sent[i].astype(F32) for i in range(2)]
    partial_share = sums[0] + x_swap(sums[1].astype(BF16)).astype(F32)
    resid_new = (
        resid + partial_share * lax.rsqrt(square_one / inner_count + 1e-05)[:, None]
    ).astype(BF16)

    resid_rows = jnp.stack([resid_new[:tokens], resid_new[tokens:]])
    resid_back = y_swap(pick(resid_rows, 1 - y))
    resid_mine = pick(resid_rows, y)
    resid_out = jnp.stack(
        [
            jnp.where(first, resid_mine, resid_back).reshape(tokens, per_head, block),
            jnp.where(first, resid_back, resid_mine).reshape(tokens, per_head, block),
        ],
        axis=2,
    ).reshape(tokens, width)

    gains = resid_gain.reshape(z_size, 2, block)
    gain = lax.dynamic_slice_in_dim(
        lax.dynamic_index_in_dim(gains, y, 1, False), head * per_head, per_head, 0
    ).reshape(half)
    hidden_wide = resid_new.astype(F32)
    hidden = (hidden_wide * gain[None, :]).astype(BF16)
    across = x_swap(hidden)
    pair = jnp.stack([hidden, across])
    other = c_swap(pair)
    square_two = lax.psum(jnp.sum(hidden_wide * hidden_wide, axis=1), "head")
    square_two = square_two + y_swap(square_two)
    all_hidden = jnp.stack([pair[0], other[0], pair[1], other[1]])
    halo_hidden = z_shift(all_hidden[:, pair_tokens - HALO :], 1)
    halo_square = z_shift(square_two[pair_tokens - HALO :], 1)
    all_hidden = jnp.concatenate([halo_hidden, all_hidden], axis=1)
    scale_two = lax.rsqrt(jnp.concatenate([halo_square, square_two]) / inner_count + 1e-05)

    total = 0.0
    for index, part in in_blocks:
        source = pick(all_hidden, (index // per_head) ^ head)
        if per_head > 1:
            source = lax.dynamic_slice_in_dim(source, (index % per_head) * block, block, 1)
        total = total + jnp.dot(source, part, preferred_element_type=F32)
    reach = tokens + HALO
    keep_start = jnp.where(first, 0, tokens)
    mine = lax.dynamic_slice_in_dim(total, keep_start, reach, 0)
    theirs = lax.dynamic_slice_in_dim(total, tokens - keep_start, reach, 0).astype(BF16)
    scale_mine = lax.dynamic_slice_in_dim(scale_two, keep_start, reach, 0)
    projected = (mine + y_swap(theirs).astype(F32)) * scale_mine[:, None]
    x_pre = projected[:, :width].astype(BF16)
    bc_share = projected[:, width : width + share].astype(BF16)
    step_two = jax.nn.softplus(projected[HALO:, width + share :] + step_time_bias[None, :])
    bc_pair = jnp.stack([bc_share, x_swap(bc_share)])
    bc_other = c_swap(bc_pair)
    bc_stack = jnp.stack([bc_pair[0], bc_other[0], bc_pair[1], bc_other[1]])
    bc_pre = jnp.concatenate([pick(bc_stack, head ^ i) for i in range(head_size)], axis=1)

    x_two = jax.nn.silu(causal_conv(x_pre, conv_x, tokens)).astype(BF16)
    bc_two = jax.nn.silu(causal_conv(bc_pre, conv_bc, tokens)).astype(BF16)
    decay_two = log_decay(decay_code[1], decay_rate[1])
    pieces_two, state_two, total_two = local_pass(x_two, bc_two, step_two, decay_two)
    carried_two = carried_in(state_two, total_two, y)
    mixed_two = finish_pass(pieces_two, x_two, bc_two, skip_gain[1], carried_two)
    square_last = lax.psum(jnp.sum(mixed_two * mixed_two, axis=1), "head")
    mixer_out = (mixed_two * lax.rsqrt(square_last / inner_count + 1e-05)[:, None]).astype(BF16)
    return (resid_out, mixer_out)


def solution(mesh):
    in_specs = (
        P("seq", "head"),
        P("seq", "head"),
        P("seq", None),
        P("seq", "head"),
        P(None, "seq", "head"),
        P(None, "head"),
        P(None, "head"),
        P("head"),
        P("head", "seq"),
        P("seq", "head"),
        P(),
        P("seq", "head"),
        P("seq", None),
        P("seq", "head"),
        P("head"),
        P(None, "head"),
        P(),
    )
    out_specs = (P("seq", "head"), P("seq", "head"))
    return jax.shard_map(
        on_device, mesh=mesh, in_specs=in_specs, out_specs=out_specs, check_vma=False
    )
```

```python
import functools
import jax
import jax.numpy as jnp
from jax import lax
from jax.experimental import pallas as pl
from jax.experimental.pallas import tpu as pltpu
from jax.sharding import PartitionSpec as P

HEAD_CHANNELS = 64
GROUP = 256
HALO = 16
F32 = jnp.float32
BF16 = jnp.bfloat16


def z_shift(value, by):
    n = lax.axis_size("seq")
    pairs = [(i, i + 2 * by) for i in range(n) if 0 <= i + 2 * by < n]
    return lax.ppermute(value, "seq", pairs)


def flip(value, axis, bit):
    n = lax.axis_size(axis)
    return lax.ppermute(value, axis, [(i, i ^ bit) for i in range(n)])


def y_swap(value):
    return flip(value, "seq", 1)


def x_swap(value):
    return flip(value, "head", 2)


def c_swap(value):
    return flip(value, "head", 1)


def z_line(value):
    ups, downs = [value], [value]
    for _ in range(1, 4):
        ups.append(z_shift(ups[-1], 1))
        downs.append(z_shift(downs[-1], -1))
    return downs[:0:-1] + ups


def z_whole(value):
    size = lax.axis_size("seq") // 2
    groups = [[2 * i + y for i in range(size)] for y in range(2)]
    return lax.all_gather(value, "seq", axis_index_groups=groups)


HIGHEST = lax.Precision.HIGHEST
LOW = -1e30


def spread(heads):
    channels = heads * HEAD_CHANNELS
    row = lax.broadcasted_iota(jnp.int32, (heads, channels), 0)
    column = lax.broadcasted_iota(jnp.int32, (heads, channels), 1)
    return (column // HEAD_CHANNELS == row).astype(F32)


def exact_dot(a, b):
    return jnp.dot(a, b, precision=HIGHEST, preferred_element_type=F32)


def running_decay(code, rate):
    decay = -jnp.minimum(code.astype(F32) * rate, 20.0)
    rows = code.shape[0]
    lower = (
        lax.broadcasted_iota(jnp.int32, (rows, rows), 0)
        >= lax.broadcasted_iota(jnp.int32, (rows, rows), 1)
    ).astype(F32)
    return exact_dot(lower, decay)


def state_kernel(x_ref, b_ref, step_ref, code_ref, rate_ref, first_ref, end_ref, payload_ref):
    tokens, channels = x_ref.shape
    heads = channels // HEAD_CHANNELS
    table = spread(heads)
    end = None
    decay = jnp.zeros((1, heads), F32)
    for start in range(0, tokens, GROUP):
        rows = pl.ds(start, GROUP)
        total = running_decay(code_ref[rows, :], rate_ref[...])
        last = total[GROUP - 1 :, :]
        weight = exact_dot(jnp.exp(last - total) * step_ref[rows, :], table)
        v = (x_ref[rows, :].astype(F32) * weight).astype(BF16)
        term = lax.dot_general(
            b_ref[rows, :], v, (((0,), (0,)), ((), ())), preferred_element_type=F32
        )
        if end is None:
            first_ref[...] = term
            end = term
        else:
            end = end * exact_dot(jnp.exp(last), table) + term
        decay = decay + last
    end_ref[...] = end
    put_payload(payload_ref, end, exact_dot(decay, table))


def put_payload(payload_ref, state, wide):
    width, channels = state.shape
    payload_ref[:width, :] = state.astype(BF16)
    high = wide.astype(BF16)
    rest = wide - high.astype(F32)
    middle = rest.astype(BF16)
    low = rest - middle.astype(F32)
    row = lax.broadcasted_iota(jnp.int32, (16, channels), 0)
    tail = jnp.where(
        row == 0,
        high.astype(F32),
        jnp.where(row == 1, middle.astype(F32), jnp.where(row == 2, low, 0.0)),
    )
    payload_ref[width:, :] = tail.astype(BF16)


def get_payload(payload_ref):
    width = payload_ref.shape[0] - 16
    tail = payload_ref[width:, :].astype(F32)
    return payload_ref[:width, :].astype(F32), tail[0:1] + tail[1:2] + tail[2:3]


def pair_kernel(
    y_ref, end_ref, own_ref, far_ref, window_ref, payload_ref, early_ref, early_decay_ref
):
    first = y_ref[0] == 0
    own, own_decay = end_ref[...], get_payload(own_ref)[1]
    far, far_decay = get_payload(far_ref)
    early, early_decay = jnp.where(first, own, far), jnp.where(first, own_decay, far_decay)
    late, late_decay = jnp.where(first, far, own), jnp.where(first, far_decay, own_decay)
    window = jnp.exp(late_decay) * early + late
    window_ref[...] = window
    put_payload(payload_ref, window, early_decay + late_decay)
    early_ref[...] = early
    early_decay_ref[...] = early_decay


def step_kernel(
    window_ref, own_ref, far_ref, before_ref, decay_ref, *outs
):
    window_out, payload_ref, before_out, decay_out = outs
    far, far_decay = get_payload(far_ref)
    own_decay = get_payload(own_ref)[1]
    window = jnp.exp(own_decay) * far + window_ref[...]
    window_out[...] = window
    put_payload(payload_ref, window, own_decay + far_decay)
    before_out[...] = before_ref[...] + jnp.exp(decay_ref[...]) * far
    decay_out[...] = decay_ref[...] + far_decay


def start_kernel(window_ref, own_ref, far_ref, *outs):
    window_out, payload_ref, before_out, decay_out = outs
    far, far_decay = get_payload(far_ref)
    own_decay = get_payload(own_ref)[1]
    window = jnp.exp(own_decay) * far + window_ref[...]
    window_out[...] = window
    put_payload(payload_ref, window, own_decay + far_decay)
    before_out[...] = far
    decay_out[...] = far_decay


def entering(y_ref, early_ref, early_decay_ref, before_ref, decay_ref, far_ref):
    far, _ = get_payload(far_ref)
    before = before_ref[...] + jnp.exp(decay_ref[...]) * far
    late = jnp.exp(early_decay_ref[...]) * before + early_ref[...]
    return jnp.where(y_ref[0] == 0, before, late)


def within_kernel(x_ref, bc_ref, step_ref, code_ref, rate_ref, skip_ref, out_ref):
    rows, channels = x_ref.shape
    heads = channels // HEAD_CHANNELS
    width = bc_ref.shape[1] // 2
    half = rows // 2
    total = running_decay(code_ref[...], rate_ref[...])
    across = total.T
    step = step_ref[...].T
    scores = lax.dot_general(
        bc_ref[:, width:],
        bc_ref[:, :width],
        (((1,), (1,)), ((), ())),
        preferred_element_type=F32,
    )
    skip = exact_dot(skip_ref[...], spread(heads))
    keep = lax.broadcasted_iota(jnp.int32, (half, half), 0) >= lax.broadcasted_iota(
        jnp.int32, (half, half), 1
    )
    lane = lax.broadcasted_iota(jnp.int32, (rows, 2 * HEAD_CHANNELS), 1)
    for pair in range(heads // 2):
        columns = pl.ds(pair * 2 * HEAD_CHANNELS, 2 * HEAD_CHANNELS)
        u = x_ref[:, columns]
        halves = []
        for h in (2 * pair, 2 * pair + 1):
            column = total[:, h : h + 1]
            line = across[h : h + 1, :]
            weight = step[h : h + 1, :]
            top = jnp.exp(jnp.where(keep, column[:half] - line[:, :half], LOW))
            top = (top * scores[:half, :half] * weight[:, :half]).astype(BF16)
            left = jnp.exp(column[half:] - line[:, :half])
            left = (left * scores[half:, :half] * weight[:, :half]).astype(BF16)
            right = jnp.exp(jnp.where(keep, column[half:] - line[:, half:], LOW))
            right = (right * scores[half:, half:] * weight[:, half:]).astype(BF16)
            upper = jnp.dot(top, u[:half], preferred_element_type=F32)
            lower = jnp.dot(
                jnp.concatenate([left, right], axis=1), u, preferred_element_type=F32
            )
            halves.append(jnp.concatenate([upper, lower], axis=0))
        mixed = jnp.where(lane < HEAD_CHANNELS, halves[0], halves[1])
        out_ref[:, columns] = mixed + skip[:, pair * 128 : pair * 128 + 128] * u.astype(F32)


def finish_group(start, state, within_ref, c_ref, code_ref, rate_ref, table):
    rows = pl.ds(start, GROUP)
    total = running_decay(code_ref[rows, :], rate_ref[...])
    c = c_ref[rows, :]
    high = state.astype(BF16)
    low = (state - high.astype(F32)).astype(BF16)
    carried = jnp.dot(
        jnp.concatenate([c, c], axis=1),
        jnp.concatenate([high, low], axis=0),
        preferred_element_type=F32,
    )
    mixed = within_ref[rows, :] + carried * exact_dot(jnp.exp(total), table)
    return mixed, exact_dot(jnp.exp(total[GROUP - 1 :, :]), table)


def gated_kernel(
    y_ref,
    early_ref,
    early_decay_ref,
    before_ref,
    decay_ref,
    far_ref,
    first_ref,
    within_ref,
    c_ref,
    code_ref,
    rate_ref,
    gate_ref,
    gain_ref,
    out_ref,
    square_ref,
):
    tokens, channels = within_ref.shape
    table = spread(channels // HEAD_CHANNELS)
    state = entering(y_ref, early_ref, early_decay_ref, before_ref, decay_ref, far_ref)
    for start in range(0, tokens, GROUP):
        mixed, decay = finish_group(start, state, within_ref, c_ref, code_ref, rate_ref, table)
        state = state * decay + first_ref[...]
        gate = gate_ref[pl.ds(start, GROUP), :].astype(F32)
        gated = mixed * (gate / (1.0 + jnp.exp(-gate)))
        out_ref[pl.ds(start, GROUP), :] = (gated * gain_ref[...]).astype(BF16)
        square_ref[:, pl.ds(start, GROUP)] = jnp.sum(gated * gated, axis=1, keepdims=True).T


def last_kernel(
    y_ref,
    early_ref,
    early_decay_ref,
    before_ref,
    decay_ref,
    far_ref,
    first_ref,
    within_ref,
    c_ref,
    code_ref,
    rate_ref,
    out_ref,
    square_ref,
):
    tokens, channels = within_ref.shape
    table = spread(channels // HEAD_CHANNELS)
    state = entering(y_ref, early_ref, early_decay_ref, before_ref, decay_ref, far_ref)
    for start in range(0, tokens, GROUP):
        mixed, decay = finish_group(start, state, within_ref, c_ref, code_ref, rate_ref, table)
        state = state * decay + first_ref[...]
        out_ref[pl.ds(start, GROUP), :] = mixed
        square_ref[:, pl.ds(start, GROUP)] = jnp.sum(mixed * mixed, axis=1, keepdims=True).T


VMEM_SPEC = pl.BlockSpec(memory_space=pltpu.VMEM)
SMEM_SPEC = pl.BlockSpec(memory_space=pltpu.SMEM)
ANY_SPEC = pl.BlockSpec(memory_space=pl.ANY)


def whole_call(kernel, outs, flops, *args):
    moved = sum(a.size * a.dtype.itemsize for a in args)
    moved += sum(o.size * o.dtype.itemsize for o in outs)
    return pl.pallas_call(
        kernel,
        out_shape=outs,
        in_specs=[SMEM_SPEC if a.shape == (1,) else VMEM_SPEC for a in args],
        out_specs=[VMEM_SPEC] * len(outs),
        cost_estimate=pl.CostEstimate(flops=flops, bytes_accessed=moved, transcendentals=0),
        compiler_params=pltpu.CompilerParams(vmem_limit_bytes=48 * 2**20),
    )(*args)


def shape(dims, kind):
    return jax.ShapeDtypeStruct(dims, kind)


def chunk_states(x, b, step, code, rate):
    width, channels = b.shape[1], x.shape[1]
    return whole_call(
        state_kernel,
        [
            shape((width, channels), F32),
            shape((width, channels), F32),
            shape((width + 16, channels), BF16),
        ],
        4 * x.size * width,
        x,
        b,
        step,
        code,
        rate,
    )


def within_blocks(x, bc, step, code, rate, skip):
    tokens, channels = x.shape
    heads = step.shape[1]
    row = lambda cols: pl.BlockSpec((GROUP, cols), lambda i: (i, 0))
    one = pl.BlockSpec((1, heads), lambda i: (0, 0))
    return pl.pallas_call(
        within_kernel,
        name="within",
        grid=(tokens // GROUP,),
        out_shape=shape((tokens, channels), F32),
        in_specs=[row(channels), row(bc.shape[1]), row(heads), row(heads), one, one],
        out_specs=row(channels),
        cost_estimate=pl.CostEstimate(
            flops=16 * x.size * GROUP, bytes_accessed=8 * x.size, transcendentals=0
        ),
        compiler_params=pltpu.CompilerParams(vmem_limit_bytes=32 * 2**20),
    )(x, bc, step, code, rate, skip)


def conv_kernel(mine_ref, far_ref, scale_ref, taps_ref, bias_ref, x_ref, bc_ref, step_ref, pre_ref):
    rows = mine_ref.shape[0]
    tokens, width = x_ref.shape
    share = bc_ref.shape[1]
    scale = scale_ref[...]
    count = taps_ref.shape[0]

    def convolved(start, size):
        columns = pl.ds(start, size)
        pre = (mine_ref[:, columns] + far_ref[:, columns].astype(F32)) * scale
        pre_ref[:, :size] = pre.astype(BF16).astype(F32)
        total = None
        for tap in range(count):
            first = rows - tokens - count + 1 + tap
            part = pre_ref[pl.ds(first, tokens), :size] * taps_ref[tap : tap + 1, columns]
            total = part if total is None else total + part
        return (total / (1.0 + jnp.exp(-total))).astype(BF16)

    for start in range(0, width, 128):
        x_ref[:, pl.ds(start, 128)] = convolved(start, 128)
    bc_ref[...] = convolved(width, share)
    heads = step_ref.shape[1]
    columns = pl.ds(width + share, heads)
    raw = (mine_ref[:, columns] + far_ref[:, columns].astype(F32)) * scale
    raw = raw[rows - tokens :] + bias_ref[...]
    step_ref[...] = jnp.maximum(raw, 0.0) + jnp.log1p(jnp.exp(-jnp.abs(raw)))


def conv_call(mine, far, scale, taps, bias, tokens, width, share):
    rows = mine.shape[0]
    heads = bias.shape[1]
    return pl.pallas_call(
        conv_kernel,
        name="conv",
        out_shape=[
            shape((tokens, width), BF16),
            shape((tokens, share), BF16),
            shape((tokens, heads), F32),
        ],
        in_specs=[VMEM_SPEC] * 5,
        out_specs=[VMEM_SPEC] * 3,
        scratch_shapes=[pltpu.VMEM((rows, 128), F32)],
        cost_estimate=pl.CostEstimate(
            flops=16 * mine.size, bytes_accessed=8 * mine.size, transcendentals=mine.size
        ),
        compiler_params=pltpu.CompilerParams(vmem_limit_bytes=32 * 2**20),
    )(mine, far, scale, taps, bias)


def fetch(spot, sources, buffer, sem, start):
    reach = len(sources) // 2
    for k in range(len(sources)):

        @pl.when(spot == k - reach)
        def _():
            copy = pltpu.make_async_copy(sources[k], buffer, sem)
            if start:
                copy.start()
            else:
                copy.wait()


def out_kernel(count, where_ref, own_ref, far_ref, *refs):
    sources, outs, (buffers, sems) = refs[:7], refs[7:-2], refs[-2:]
    tokens = own_ref.shape[0]
    own_start = pl.multiple_of(where_ref[0] * tokens, tokens)
    far_start = pl.multiple_of((1 - where_ref[0]) * tokens, tokens)
    fetch(where_ref[1], sources, buffers.at[0], sems.at[0], True)
    for i in range(count):
        if i + 1 < count:
            slot = (i + 1) % 2
            fetch(where_ref[i + 2], sources, buffers.at[slot], sems.at[slot], True)
        fetch(where_ref[i + 1], sources, buffers.at[i % 2], sems.at[i % 2], False)
        weight = buffers[i % 2]
        for ref, start in ((own_ref, own_start), (far_ref, far_start)):
            product = jnp.dot(ref[...], weight, preferred_element_type=F32)
            if len(outs) == 1:
                outs[0][i, pl.ds(start, tokens), :] = product.astype(outs[0].dtype)
            else:
                outs[i][pl.ds(start, tokens), :] = product.astype(outs[i].dtype)


def in_kernel(count, where_ref, hidden_ref, *refs):
    sources, (out_ref, buffers, total, sems) = refs[:7], refs[7:]
    rows = out_ref.shape[0]
    window = pl.ds(pl.multiple_of(where_ref[0], HALO), rows)
    fetch(where_ref[1], sources, buffers.at[0], sems.at[0], True)
    for i in range(count):
        if i + 1 < count:
            slot = (i + 1) % 2
            fetch(where_ref[i + 2], sources, buffers.at[slot], sems.at[slot], True)
        fetch(where_ref[i + 1], sources, buffers.at[i % 2], sems.at[i % 2], False)
        hidden = hidden_ref[i, window, :]
        depth = hidden.shape[1]
        large = jnp.dot(hidden, buffers[i % 2, :depth, :], preferred_element_type=F32)
        packed = buffers[i % 2, depth:, :]
        small = lax.dot_general(
            hidden,
            jnp.concatenate([packed[:, :depth], packed[:, depth:]], axis=0),
            (((1,), (1,)), ((), ())),
            preferred_element_type=F32,
        )[:, : out_ref.shape[1] - large.shape[1]]
        for part, columns in (
            (large, slice(0, large.shape[1])),
            (small, slice(large.shape[1], out_ref.shape[1])),
        ):
            if i == 0:
                total[:, columns] = part
            elif i + 1 < count:
                total[:, columns] += part
            else:
                out_ref[:, columns] = (total[:, columns] + part).astype(out_ref.dtype)


def out_call(where, own, far, sources, outs):
    count = where.shape[0] - 1
    tokens, depth = own.shape
    block = sources[0].shape
    return pl.pallas_call(
        functools.partial(out_kernel, count),
        out_shape=outs,
        in_specs=[SMEM_SPEC, VMEM_SPEC, VMEM_SPEC] + [ANY_SPEC] * len(sources),
        out_specs=[VMEM_SPEC] * len(outs),
        scratch_shapes=[pltpu.VMEM((2,) + block, BF16), pltpu.SemaphoreType.DMA((2,))],
        cost_estimate=pl.CostEstimate(
            flops=4 * count * tokens * depth * block[1],
            bytes_accessed=4 * own.size + 2 * count * sources[0].size,
            transcendentals=0,
        ),
        compiler_params=pltpu.CompilerParams(vmem_limit_bytes=32 * 2**20),
    )(where, own, far, *sources)


def in_call(where, hidden, sources, rows, columns, kind):
    count, _, depth = hidden.shape
    block = sources[0].shape
    return pl.pallas_call(
        functools.partial(in_kernel, count),
        out_shape=shape((rows, columns), kind),
        in_specs=[SMEM_SPEC, VMEM_SPEC] + [ANY_SPEC] * len(sources),
        out_specs=VMEM_SPEC,
        scratch_shapes=[
            pltpu.VMEM((2,) + block, BF16),
            pltpu.VMEM((rows, columns), F32),
            pltpu.SemaphoreType.DMA((2,)),
        ],
        cost_estimate=pl.CostEstimate(
            flops=2 * count * rows * depth * block[1],
            bytes_accessed=2 * hidden.size + 2 * count * sources[0].size,
            transcendentals=0,
        ),
        compiler_params=pltpu.CompilerParams(vmem_limit_bytes=40 * 2**20),
    )(where, hidden, *sources)


def pick(stack, index):
    return lax.dynamic_index_in_dim(stack, index, 0, False)


def exchange_states(end, payload, y):
    full, packed = shape(end.shape, F32), shape(payload.shape, BF16)
    row = shape((1, end.shape[1]), F32)
    flag = y[None].astype(jnp.int32)
    far = y_swap(payload)
    window, payload, early, early_decay = whole_call(
        pair_kernel, [full, packed, full, row], end.size, flag, end, payload, far
    )
    parts = ()
    reach, size = 1, lax.axis_size("seq") // 2
    while 2 * reach < size:
        far = z_shift(payload, reach)
        window, payload, *parts = whole_call(
            step_kernel if parts else start_kernel,
            [full, packed, full, row],
            end.size,
            window,
            payload,
            far,
            *parts,
        )
        reach *= 2
    far = z_shift(payload, reach)
    return (flag, early, early_decay, *parts, far)


def on_device(
    x_in,
    gate_in,
    bc_in,
    step_in,
    decay_code,
    decay_rate,
    skip_gain,
    norm_gain,
    w_out,
    resid_in,
    resid_gain,
    w_in_x,
    w_in_bc,
    w_in_dt,
    step_time_bias,
    conv_x,
    conv_bc,
):
    tokens, width = x_in.shape
    seq_size, head_size = lax.axis_size("seq"), lax.axis_size("head")
    z_size = seq_size // 2
    seq_place, head = lax.axis_index("seq"), lax.axis_index("head")
    z, y = seq_place // 2, seq_place % 2
    x_bit, c_bit = head // 2, head % 2
    inner_count = width * head_size
    pair_tokens = 2 * tokens
    state_width = bc_in.shape[1] // 2
    block = w_out.shape[1]
    half = width // 2
    per_head = z_size // head_size
    first = y == 0
    line = z_size == 4 and per_head == 1

    share = w_in_bc.shape[1] // head_size
    bc_weight = lax.dynamic_slice_in_dim(w_in_bc, head * share, share, 1)
    small = share + w_in_dt.shape[1]
    if line:
        below = jnp.concatenate([bc_weight, w_in_dt], axis=1).T
        below = jnp.concatenate([below, jnp.zeros((-small % 32, block), BF16)], axis=0)
        below = below.reshape(2, below.shape[0] // 2, block)
        below = jnp.concatenate([below[0], below[1]], axis=1)
        out_blocks = z_line(w_out)
        in_blocks = z_line(jnp.concatenate([w_in_x, below], axis=0))
    else:
        w_in = jnp.concatenate([w_in_x, bc_weight, w_in_dt], axis=1)
        out_blocks, in_blocks = z_whole(w_out), z_whole(w_in)

    def parity(array, which):
        if per_head == 1:
            return lax.dynamic_slice_in_dim(array, which * block, block, 1)
        parts = array.reshape(tokens, per_head, 2, block)
        return lax.dynamic_index_in_dim(parts, which, 2, False).reshape(tokens, half)

    resid_own = parity(resid_in, y)
    resid_far = y_swap(parity(resid_in, 1 - y))

    code_one, rate_one = decay_code[0], decay_rate[0][None, :]
    first_one, end_one, payload_one = chunk_states(
        x_in, bc_in[:, :state_width], step_in, code_one, rate_one
    )
    within_one = within_blocks(x_in, bc_in, step_in, code_one, rate_one, skip_gain[0][None, :])
    carried_one = exchange_states(end_one, payload_one, y)
    scaled, square_own = whole_call(
        gated_kernel,
        [shape((tokens, width), BF16), shape((1, tokens), F32)],
        4 * x_in.size * state_width,
        *carried_one,
        first_one,
        within_one,
        bc_in[:, state_width:],
        code_one,
        rate_one,
        gate_in,
        norm_gain[None, :],
    )
    scaled_far = y_swap(scaled)
    square_own = square_own + c_swap(square_own)
    square_own = square_own + x_swap(square_own)
    square_far = y_swap(square_own)
    square_one = jnp.concatenate(
        [jnp.where(first, square_own, square_far), jnp.where(first, square_far, square_own)], axis=1
    )[0]
    resid = jnp.concatenate(
        [jnp.where(first, resid_own, resid_far), jnp.where(first, resid_far, resid_own)], axis=0
    ).astype(F32)

    keep_heads = [2 * (x_bit ^ i) + c_bit for i in range(2)]
    send_heads = [2 * (x_bit ^ i) + (1 - c_bit) for i in range(2)]
    if line:
        where = lambda heads: jnp.stack([y] + [z - h for h in heads]).astype(jnp.int32)
        (sends,) = out_call(
            where(send_heads),
            scaled,
            scaled_far,
            out_blocks,
            [shape((2, pair_tokens, block), BF16)],
        )
        keeps = out_call(
            where(keep_heads),
            scaled,
            scaled_far,
            out_blocks,
            [shape((pair_tokens, block), F32)] * 2,
        )
    else:
        both = jnp.concatenate(
            [jnp.where(first, scaled, scaled_far), jnp.where(first, scaled_far, scaled)], axis=0
        )
        by_head = out_blocks.reshape(head_size, per_head, width, block)
        by_head = by_head.transpose(0, 2, 1, 3).reshape(head_size, width, half)
        product = lambda h: jnp.dot(both, pick(by_head, h), preferred_element_type=F32)
        sends = jnp.stack([product(h) for h in send_heads]).astype(BF16)
        keeps = [product(h) for h in keep_heads]
    received = c_swap(sends)
    crossing = x_swap((keeps[1] + received[1].astype(F32)).astype(BF16))
    partial_share = keeps[0] + received[0].astype(F32) + crossing.astype(F32)
    resid_new = (
        resid + partial_share * lax.rsqrt(square_one / inner_count + 1e-05)[:, None]
    ).astype(BF16)

    resid_back = y_swap(lax.dynamic_slice_in_dim(resid_new, (1 - y) * tokens, tokens, 0))
    resid_mine = lax.dynamic_slice_in_dim(resid_new, y * tokens, tokens, 0)
    both = [jnp.where(first, resid_mine, resid_back), jnp.where(first, resid_back, resid_mine)]
    if per_head == 1:
        resid_out = jnp.concatenate(both, axis=1)
    else:
        both = [a.reshape(tokens, per_head, block) for a in both]
        resid_out = jnp.stack(both, axis=2).reshape(tokens, width)

    gains = resid_gain.reshape(z_size, 2, block)
    gain = lax.dynamic_slice_in_dim(
        lax.dynamic_index_in_dim(gains, y, 1, False), head * per_head, per_head, 0
    ).reshape(half)
    hidden_wide = resid_new.astype(F32)
    hidden = (hidden_wide * gain[None, :]).astype(BF16)
    pair = jnp.stack([hidden, x_swap(hidden)])
    other = c_swap(pair)
    square_two = jnp.sum(hidden_wide * hidden_wide, axis=1)
    square_two = square_two + x_swap(square_two)
    square_two = square_two + c_swap(square_two)
    square_two = square_two + y_swap(square_two)
    all_hidden = jnp.stack([pair[0], other[0], pair[1], other[1]])
    halo_hidden = z_shift(all_hidden[:, pair_tokens - HALO :], 1)
    halo_square = z_shift(square_two[pair_tokens - HALO :], 1)
    all_hidden = jnp.concatenate([halo_hidden, all_hidden], axis=1)
    scale_two = lax.rsqrt(jnp.concatenate([halo_square, square_two]) / inner_count + 1e-05)

    reach = tokens + HALO
    keep_start = jnp.where(first, 0, tokens)
    send_start = tokens - keep_start
    if line:
        spots = [z - (head ^ k) for k in range(4)]
        where = lambda start: jnp.stack([start] + spots).astype(jnp.int32)
        columns = width + small
        theirs = in_call(where(send_start), all_hidden, in_blocks, reach, columns, BF16)
        mine = in_call(where(keep_start), all_hidden, in_blocks, reach, columns, F32)
    else:
        wide = jnp.concatenate([pick(all_hidden, head ^ i) for i in range(head_size)], axis=1)
        total = jnp.dot(
            wide, in_blocks.reshape(z_size * block, w_in.shape[1]), preferred_element_type=F32
        )
        mine = lax.dynamic_slice_in_dim(total, keep_start, reach, 0)
        theirs = lax.dynamic_slice_in_dim(total, send_start, reach, 0).astype(BF16)
    scale_mine = lax.dynamic_slice_in_dim(scale_two, keep_start, reach, 0)
    taps = jnp.concatenate(
        [conv_x, lax.dynamic_slice_in_dim(conv_bc, head * share, share, 1)], axis=1
    ).astype(F32)
    x_two, bc_share, step_two = conv_call(
        mine,
        y_swap(theirs),
        scale_mine[:, None],
        taps,
        step_time_bias[None, :],
        tokens,
        width,
        share,
    )
    bc_pair = jnp.stack([bc_share, x_swap(bc_share)])
    bc_other = c_swap(bc_pair)
    bc_stack = jnp.stack([bc_pair[0], bc_other[0], bc_pair[1], bc_other[1]])
    bc_two = jnp.concatenate([pick(bc_stack, head ^ i) for i in range(head_size)], axis=1)

    code_two, rate_two = decay_code[1], decay_rate[1][None, :]
    first_two, end_two, payload_two = chunk_states(
        x_two, bc_two[:, :state_width], step_two, code_two, rate_two
    )
    within_two = within_blocks(x_two, bc_two, step_two, code_two, rate_two, skip_gain[1][None, :])
    carried_two = exchange_states(end_two, payload_two, y)
    mixed_two, square_last = whole_call(
        last_kernel,
        [shape((tokens, width), F32), shape((1, tokens), F32)],
        4 * x_in.size * state_width,
        *carried_two,
        first_two,
        within_two,
        bc_two[:, state_width:],
        code_two,
        rate_two,
    )
    square_last = lax.psum(square_last[0], "head")
    mixer_out = (mixed_two * lax.rsqrt(square_last / inner_count + 1e-05)[:, None]).astype(BF16)
    return (resid_out, mixer_out)


def solution(mesh):
    in_specs = (
        P("seq", "head"),
        P("seq", "head"),
        P("seq", None),
        P("seq", "head"),
        P(None, "seq", "head"),
        P(None, "head"),
        P(None, "head"),
        P("head"),
        P("head", "seq"),
        P("seq", "head"),
        P(),
        P("seq", "head"),
        P("seq", None),
        P("seq", "head"),
        P("head"),
        P(None, "head"),
        P(),
    )
    out_specs = (P("seq", "head"), P("seq", "head"))

    return jax.shard_map(
        on_device, mesh=mesh, in_specs=in_specs, out_specs=out_specs, check_vma=False
    )
```

```python
import functools
import jax
import jax.numpy as jnp
from jax import lax
from jax.experimental import pallas as pl
from jax.experimental.pallas import tpu as pltpu
from jax.sharding import PartitionSpec as P

HEAD_CHANNELS = 64
GROUP = 256
HALO = 16
ROWS = 256
F32 = jnp.float32
BF16 = jnp.bfloat16


def z_shift(value, by):
    n = lax.axis_size("seq")
    pairs = [(i, i + 2 * by) for i in range(n) if 0 <= i + 2 * by < n]
    return lax.ppermute(value, "seq", pairs)


def flip(value, axis, bit):
    n = lax.axis_size(axis)
    return lax.ppermute(value, axis, [(i, i ^ bit) for i in range(n)])


def y_swap(value):
    return flip(value, "seq", 1)


def x_swap(value):
    return flip(value, "head", 2)


def c_swap(value):
    return flip(value, "head", 1)


def z_line(value):
    ups, downs = [value], [value]
    for _ in range(1, 4):
        ups.append(z_shift(ups[-1], 1))
        downs.append(z_shift(downs[-1], -1))
    return downs[:0:-1] + ups


def z_whole(value):
    size = lax.axis_size("seq") // 2
    groups = [[2 * i + y for i in range(size)] for y in range(2)]
    return lax.all_gather(value, "seq", axis_index_groups=groups)


HIGHEST = lax.Precision.HIGHEST
LOW = -1e30


def spread(heads):
    channels = heads * HEAD_CHANNELS
    row = lax.broadcasted_iota(jnp.int32, (heads, channels), 0)
    column = lax.broadcasted_iota(jnp.int32, (heads, channels), 1)
    return (column // HEAD_CHANNELS == row).astype(F32)


def exact_dot(a, b):
    return jnp.dot(a, b, precision=HIGHEST, preferred_element_type=F32)


def running_decay(code, rate):
    decay = -jnp.minimum(code.astype(F32) * rate, 20.0)
    rows = code.shape[0]
    lower = (
        lax.broadcasted_iota(jnp.int32, (rows, rows), 0)
        >= lax.broadcasted_iota(jnp.int32, (rows, rows), 1)
    ).astype(F32)
    return exact_dot(lower, decay)


def state_kernel(x_ref, b_ref, step_ref, code_ref, rate_ref, first_ref, end_ref, payload_ref):
    tokens, channels = x_ref.shape
    heads = channels // HEAD_CHANNELS
    table = spread(heads)
    end = None
    decay = jnp.zeros((1, heads), F32)
    for start in range(0, tokens, GROUP):
        rows = pl.ds(start, GROUP)
        total = running_decay(code_ref[rows, :], rate_ref[...])
        last = total[GROUP - 1 :, :]
        weight = exact_dot(jnp.exp(last - total) * step_ref[rows, :], table)
        v = (x_ref[rows, :].astype(F32) * weight).astype(BF16)
        term = lax.dot_general(
            b_ref[rows, :], v, (((0,), (0,)), ((), ())), preferred_element_type=F32
        )
        if end is None:
            first_ref[...] = term
            end = term
        else:
            end = end * exact_dot(jnp.exp(last), table) + term
        decay = decay + last
    end_ref[...] = end
    put_payload(payload_ref, end, exact_dot(decay, table))


def put_payload(payload_ref, state, wide):
    width, channels = state.shape
    payload_ref[:width, :] = state.astype(BF16)
    high = wide.astype(BF16)
    rest = wide - high.astype(F32)
    middle = rest.astype(BF16)
    low = rest - middle.astype(F32)
    row = lax.broadcasted_iota(jnp.int32, (16, channels), 0)
    tail = jnp.where(
        row == 0,
        high.astype(F32),
        jnp.where(row == 1, middle.astype(F32), jnp.where(row == 2, low, 0.0)),
    )
    payload_ref[width:, :] = tail.astype(BF16)


def get_payload(payload_ref):
    width = payload_ref.shape[0] - 16
    tail = payload_ref[width:, :].astype(F32)
    return payload_ref[:width, :].astype(F32), tail[0:1] + tail[1:2] + tail[2:3]


def pair_kernel(
    y_ref, end_ref, own_ref, far_ref, window_ref, payload_ref, early_ref, early_decay_ref
):
    first = y_ref[0] == 0
    own, own_decay = end_ref[...], get_payload(own_ref)[1]
    far, far_decay = get_payload(far_ref)
    early, early_decay = jnp.where(first, own, far), jnp.where(first, own_decay, far_decay)
    late, late_decay = jnp.where(first, far, own), jnp.where(first, far_decay, own_decay)
    window = jnp.exp(late_decay) * early + late
    window_ref[...] = window
    put_payload(payload_ref, window, early_decay + late_decay)
    early_ref[...] = early
    early_decay_ref[...] = early_decay


def step_kernel(
    window_ref, own_ref, far_ref, before_ref, decay_ref, *outs
):
    window_out, payload_ref, before_out, decay_out = outs
    far, far_decay = get_payload(far_ref)
    own_decay = get_payload(own_ref)[1]
    window = jnp.exp(own_decay) * far + window_ref[...]
    window_out[...] = window
    put_payload(payload_ref, window, own_decay + far_decay)
    before_out[...] = before_ref[...] + jnp.exp(decay_ref[...]) * far
    decay_out[...] = decay_ref[...] + far_decay


def start_kernel(window_ref, own_ref, far_ref, *outs):
    window_out, payload_ref, before_out, decay_out = outs
    far, far_decay = get_payload(far_ref)
    own_decay = get_payload(own_ref)[1]
    window = jnp.exp(own_decay) * far + window_ref[...]
    window_out[...] = window
    put_payload(payload_ref, window, own_decay + far_decay)
    before_out[...] = far
    decay_out[...] = far_decay


def entering(y_ref, early_ref, early_decay_ref, before_ref, decay_ref, far_ref):
    far, _ = get_payload(far_ref)
    before = before_ref[...] + jnp.exp(decay_ref[...]) * far
    late = jnp.exp(early_decay_ref[...]) * before + early_ref[...]
    return jnp.where(y_ref[0] == 0, before, late)


def within_kernel(x_ref, bc_ref, step_ref, code_ref, rate_ref, skip_ref, out_ref):
    rows, channels = x_ref.shape
    heads = channels // HEAD_CHANNELS
    width = bc_ref.shape[1] // 2
    half = rows // 2
    total = running_decay(code_ref[...], rate_ref[...])
    across = total.T
    step = step_ref[...].T
    scores = lax.dot_general(
        bc_ref[:, width:],
        bc_ref[:, :width],
        (((1,), (1,)), ((), ())),
        preferred_element_type=F32,
    )
    skip = exact_dot(skip_ref[...], spread(heads))
    keep = lax.broadcasted_iota(jnp.int32, (half, half), 0) >= lax.broadcasted_iota(
        jnp.int32, (half, half), 1
    )
    lane = lax.broadcasted_iota(jnp.int32, (rows, 2 * HEAD_CHANNELS), 1)
    for pair in range(heads // 2):
        columns = pl.ds(pair * 2 * HEAD_CHANNELS, 2 * HEAD_CHANNELS)
        u = x_ref[:, columns]
        halves = []
        for h in (2 * pair, 2 * pair + 1):
            column = total[:, h : h + 1]
            line = across[h : h + 1, :]
            weight = step[h : h + 1, :]
            top = jnp.exp(jnp.where(keep, column[:half] - line[:, :half], LOW))
            top = (top * scores[:half, :half] * weight[:, :half]).astype(BF16)
            left = jnp.exp(column[half:] - line[:, :half])
            left = (left * scores[half:, :half] * weight[:, :half]).astype(BF16)
            right = jnp.exp(jnp.where(keep, column[half:] - line[:, half:], LOW))
            right = (right * scores[half:, half:] * weight[:, half:]).astype(BF16)
            upper = jnp.dot(top, u[:half], preferred_element_type=F32)
            lower = jnp.dot(
                jnp.concatenate([left, right], axis=1), u, preferred_element_type=F32
            )
            halves.append(jnp.concatenate([upper, lower], axis=0))
        mixed = jnp.where(lane < HEAD_CHANNELS, halves[0], halves[1])
        out_ref[:, columns] = mixed + skip[:, pair * 128 : pair * 128 + 128] * u.astype(F32)


def finish_group(start, state, within_ref, c_ref, code_ref, rate_ref, table):
    rows = pl.ds(start, GROUP)
    total = running_decay(code_ref[rows, :], rate_ref[...])
    c = c_ref[rows, :]
    high = state.astype(BF16)
    low = (state - high.astype(F32)).astype(BF16)
    carried = jnp.dot(
        jnp.concatenate([c, c], axis=1),
        jnp.concatenate([high, low], axis=0),
        preferred_element_type=F32,
    )
    mixed = within_ref[rows, :] + carried * exact_dot(jnp.exp(total), table)
    return mixed, exact_dot(jnp.exp(total[GROUP - 1 :, :]), table)


def gated_kernel(
    y_ref,
    early_ref,
    early_decay_ref,
    before_ref,
    decay_ref,
    far_ref,
    first_ref,
    within_ref,
    c_ref,
    code_ref,
    rate_ref,
    gate_ref,
    gain_ref,
    out_ref,
    square_ref,
):
    tokens, channels = within_ref.shape
    table = spread(channels // HEAD_CHANNELS)
    state = entering(y_ref, early_ref, early_decay_ref, before_ref, decay_ref, far_ref)
    for start in range(0, tokens, GROUP):
        mixed, decay = finish_group(start, state, within_ref, c_ref, code_ref, rate_ref, table)
        state = state * decay + first_ref[...]
        gate = gate_ref[pl.ds(start, GROUP), :].astype(F32)
        gated = mixed * (gate / (1.0 + jnp.exp(-gate)))
        out_ref[pl.ds(start, GROUP), :] = (gated * gain_ref[...]).astype(BF16)
        square_ref[:, pl.ds(start, GROUP)] = jnp.sum(gated * gated, axis=1, keepdims=True).T


def last_kernel(
    y_ref,
    early_ref,
    early_decay_ref,
    before_ref,
    decay_ref,
    far_ref,
    first_ref,
    within_ref,
    c_ref,
    code_ref,
    rate_ref,
    out_ref,
    square_ref,
):
    tokens, channels = within_ref.shape
    table = spread(channels // HEAD_CHANNELS)
    state = entering(y_ref, early_ref, early_decay_ref, before_ref, decay_ref, far_ref)
    for start in range(0, tokens, GROUP):
        mixed, decay = finish_group(start, state, within_ref, c_ref, code_ref, rate_ref, table)
        state = state * decay + first_ref[...]
        out_ref[pl.ds(start, GROUP), :] = mixed
        square_ref[:, pl.ds(start, GROUP)] = jnp.sum(mixed * mixed, axis=1, keepdims=True).T


VMEM_SPEC = pl.BlockSpec(memory_space=pltpu.VMEM)
SMEM_SPEC = pl.BlockSpec(memory_space=pltpu.SMEM)
HBM_SPEC = pl.BlockSpec(memory_space=pltpu.HBM)


def whole_call(kernel, outs, flops, *args):
    moved = sum(a.size * a.dtype.itemsize for a in args)
    moved += sum(o.size * o.dtype.itemsize for o in outs)
    return pl.pallas_call(
        kernel,
        out_shape=outs,
        in_specs=[SMEM_SPEC if a.shape == (1,) else VMEM_SPEC for a in args],
        out_specs=[VMEM_SPEC] * len(outs),
        cost_estimate=pl.CostEstimate(flops=flops, bytes_accessed=moved, transcendentals=0),
        compiler_params=pltpu.CompilerParams(vmem_limit_bytes=48 * 2**20),
    )(*args)


def shape(dims, kind):
    return jax.ShapeDtypeStruct(dims, kind)


def chunk_states(x, b, step, code, rate):
    width, channels = b.shape[1], x.shape[1]
    return whole_call(
        state_kernel,
        [
            shape((width, channels), F32),
            shape((width, channels), F32),
            shape((width + 16, channels), BF16),
        ],
        4 * x.size * width,
        x,
        b,
        step,
        code,
        rate,
    )


def within_blocks(x, bc, step, code, rate, skip):
    tokens, channels = x.shape
    heads = step.shape[1]
    row = lambda cols: pl.BlockSpec((GROUP, cols), lambda i: (i, 0))
    one = pl.BlockSpec((1, heads), lambda i: (0, 0))
    return pl.pallas_call(
        within_kernel,
        name="within",
        grid=(tokens // GROUP,),
        out_shape=shape((tokens, channels), F32),
        in_specs=[row(channels), row(bc.shape[1]), row(heads), row(heads), one, one],
        out_specs=row(channels),
        cost_estimate=pl.CostEstimate(
            flops=16 * x.size * GROUP, bytes_accessed=8 * x.size, transcendentals=0
        ),
        compiler_params=pltpu.CompilerParams(vmem_limit_bytes=32 * 2**20),
    )(x, bc, step, code, rate, skip)


def conv_kernel(mine_ref, far_ref, scale_ref, taps_ref, bias_ref, x_ref, bc_ref, step_ref, pre_ref):
    rows = mine_ref.shape[0]
    tokens, width = x_ref.shape
    share = bc_ref.shape[1]
    scale = scale_ref[...]
    count = taps_ref.shape[0]

    def convolved(start, size):
        columns = pl.ds(start, size)
        pre = (mine_ref[:, columns] + far_ref[:, columns].astype(F32)) * scale
        pre_ref[:, :size] = pre.astype(BF16).astype(F32)
        total = None
        for tap in range(count):
            first = rows - tokens - count + 1 + tap
            part = pre_ref[pl.ds(first, tokens), :size] * taps_ref[tap : tap + 1, columns]
            total = part if total is None else total + part
        return (total / (1.0 + jnp.exp(-total))).astype(BF16)

    for start in range(0, width, 128):
        x_ref[:, pl.ds(start, 128)] = convolved(start, 128)
    bc_ref[...] = convolved(width, share)
    heads = step_ref.shape[1]
    columns = pl.ds(width + share, heads)
    raw = (mine_ref[:, columns] + far_ref[:, columns].astype(F32)) * scale
    raw = raw[rows - tokens :] + bias_ref[...]
    step_ref[...] = jnp.maximum(raw, 0.0) + jnp.log1p(jnp.exp(-jnp.abs(raw)))


def conv_call(mine, far, scale, taps, bias, tokens, width, share):
    rows = mine.shape[0]
    heads = bias.shape[1]
    return pl.pallas_call(
        conv_kernel,
        name="conv",
        out_shape=[
            shape((tokens, width), BF16),
            shape((tokens, share), BF16),
            shape((tokens, heads), F32),
        ],
        in_specs=[VMEM_SPEC] * 5,
        out_specs=[VMEM_SPEC] * 3,
        scratch_shapes=[pltpu.VMEM((rows, 128), F32)],
        cost_estimate=pl.CostEstimate(
            flops=16 * mine.size, bytes_accessed=8 * mine.size, transcendentals=mine.size
        ),
        compiler_params=pltpu.CompilerParams(vmem_limit_bytes=32 * 2**20),
    )(mine, far, scale, taps, bias)


def fetch(spot, sources, buffer, sem, start):
    reach = len(sources) // 2
    for k in range(len(sources)):

        @pl.when(spot == k - reach)
        def _():
            copy = pltpu.make_async_copy(sources[k], buffer, sem)
            if start:
                copy.start()
            else:
                copy.wait()


def out_kernel(count, where_ref, own_ref, far_ref, *refs):
    sources, outs, (buffers, sems) = refs[:7], refs[7:-2], refs[-2:]
    tokens = own_ref.shape[0]
    own_start = pl.multiple_of(where_ref[0] * tokens, tokens)
    far_start = pl.multiple_of((1 - where_ref[0]) * tokens, tokens)
    fetch(where_ref[1], sources, buffers.at[0], sems.at[0], True)
    for i in range(count):
        if i + 1 < count:
            slot = (i + 1) % 2
            fetch(where_ref[i + 2], sources, buffers.at[slot], sems.at[slot], True)
        fetch(where_ref[i + 1], sources, buffers.at[i % 2], sems.at[i % 2], False)
        for ref, start in ((own_ref, own_start), (far_ref, far_start)):

            @pl.loop(0, tokens, step=ROWS)
            def _(row):
                row = pl.multiple_of(row, ROWS)
                product = jnp.dot(
                    ref[pl.ds(row, ROWS), :], buffers[i % 2], preferred_element_type=F32
                )
                if len(outs) == 1:
                    outs[0][i, pl.ds(start + row, ROWS), :] = product.astype(outs[0].dtype)
                else:
                    outs[i][pl.ds(start + row, ROWS), :] = product.astype(outs[i].dtype)


def in_kernel(count, where_ref, hidden_ref, *refs):
    sources, (out_ref, buffers, total, sems) = refs[:7], refs[7:]
    rows = out_ref.shape[0]
    fetch(where_ref[1], sources, buffers.at[0], sems.at[0], True)
    for i in range(count):
        if i + 1 < count:
            slot = (i + 1) % 2
            fetch(where_ref[i + 2], sources, buffers.at[slot], sems.at[slot], True)
        fetch(where_ref[i + 1], sources, buffers.at[i % 2], sems.at[i % 2], False)
        depth, wide = hidden_ref.shape[2], buffers.shape[2]
        packed = buffers[i % 2, depth:, :]
        below = jnp.concatenate([packed[:, :depth], packed[:, depth:]], axis=0)

        @pl.loop(0, rows, step=rows // 3)
        def _(row):
            here = pl.ds(pl.multiple_of(row, HALO), rows // 3)
            there = pl.ds(pl.multiple_of(where_ref[0] + row, HALO), rows // 3)
            hidden = hidden_ref[i, there, :]
            large = jnp.dot(hidden, buffers[i % 2, :depth, :], preferred_element_type=F32)
            small = lax.dot_general(
                hidden, below, (((1,), (1,)), ((), ())), preferred_element_type=F32
            )[:, : out_ref.shape[1] - wide]
            for part, columns in (
                (large, slice(0, wide)),
                (small, slice(wide, out_ref.shape[1])),
            ):
                if i == 0:
                    total[here, columns] = part
                elif i + 1 < count:
                    total[here, columns] += part
                else:
                    out_ref[here, columns] = (total[here, columns] + part).astype(out_ref.dtype)


def out_call(where, own, far, sources, outs):
    count = where.shape[0] - 1
    tokens, depth = own.shape
    block = sources[0].shape
    return pl.pallas_call(
        functools.partial(out_kernel, count),
        out_shape=outs,
        in_specs=[SMEM_SPEC, VMEM_SPEC, VMEM_SPEC] + [HBM_SPEC] * len(sources),
        out_specs=[VMEM_SPEC] * len(outs),
        scratch_shapes=[pltpu.VMEM((2,) + block, BF16), pltpu.SemaphoreType.DMA((2,))],
        cost_estimate=pl.CostEstimate(
            flops=4 * count * tokens * depth * block[1],
            bytes_accessed=4 * own.size + 2 * count * sources[0].size,
            transcendentals=0,
        ),
        compiler_params=pltpu.CompilerParams(vmem_limit_bytes=32 * 2**20),
    )(where, own, far, *sources)


def in_call(where, hidden, sources, rows, columns, kind):
    count, _, depth = hidden.shape
    block = sources[0].shape
    return pl.pallas_call(
        functools.partial(in_kernel, count),
        out_shape=shape((rows, columns), kind),
        in_specs=[SMEM_SPEC, VMEM_SPEC] + [HBM_SPEC] * len(sources),
        out_specs=VMEM_SPEC,
        scratch_shapes=[
            pltpu.VMEM((2,) + block, BF16),
            pltpu.VMEM((rows, columns), F32),
            pltpu.SemaphoreType.DMA((2,)),
        ],
        cost_estimate=pl.CostEstimate(
            flops=2 * count * rows * depth * block[1],
            bytes_accessed=2 * hidden.size + 2 * count * sources[0].size,
            transcendentals=0,
        ),
        compiler_params=pltpu.CompilerParams(vmem_limit_bytes=40 * 2**20),
    )(where, hidden, *sources)


def pick(stack, index):
    return lax.dynamic_index_in_dim(stack, index, 0, False)


def exchange_states(end, payload, y):
    full, packed = shape(end.shape, F32), shape(payload.shape, BF16)
    row = shape((1, end.shape[1]), F32)
    flag = y[None].astype(jnp.int32)
    far = y_swap(payload)
    window, payload, early, early_decay = whole_call(
        pair_kernel, [full, packed, full, row], end.size, flag, end, payload, far
    )
    parts = ()
    reach, size = 1, lax.axis_size("seq") // 2
    while 2 * reach < size:
        far = z_shift(payload, reach)
        window, payload, *parts = whole_call(
            step_kernel if parts else start_kernel,
            [full, packed, full, row],
            end.size,
            window,
            payload,
            far,
            *parts,
        )
        reach *= 2
    far = z_shift(payload, reach)
    return (flag, early, early_decay, *parts, far)


def on_device(
    x_in,
    gate_in,
    bc_in,
    step_in,
    decay_code,
    decay_rate,
    skip_gain,
    norm_gain,
    w_out,
    resid_in,
    resid_gain,
    w_in_x,
    w_in_bc,
    w_in_dt,
    step_time_bias,
    conv_x,
    conv_bc,
):
    tokens, width = x_in.shape
    seq_size, head_size = lax.axis_size("seq"), lax.axis_size("head")
    z_size = seq_size // 2
    seq_place, head = lax.axis_index("seq"), lax.axis_index("head")
    z, y = seq_place // 2, seq_place % 2
    x_bit, c_bit = head // 2, head % 2
    inner_count = width * head_size
    pair_tokens = 2 * tokens
    state_width = bc_in.shape[1] // 2
    block = w_out.shape[1]
    half = width // 2
    per_head = z_size // head_size
    first = y == 0
    line = z_size == 4 and per_head == 1

    share = w_in_bc.shape[1] // head_size
    bc_weight = lax.dynamic_slice_in_dim(w_in_bc, head * share, share, 1)
    small = share + w_in_dt.shape[1]
    if line:
        below = jnp.concatenate([bc_weight, w_in_dt], axis=1).T
        below = jnp.concatenate([below, jnp.zeros((-small % 32, block), BF16)], axis=0)
        below = below.reshape(2, below.shape[0] // 2, block)
        below = jnp.concatenate([below[0], below[1]], axis=1)
        out_blocks = z_line(w_out)
        in_blocks = z_line(jnp.concatenate([w_in_x, below], axis=0))
    else:
        w_in = jnp.concatenate([w_in_x, bc_weight, w_in_dt], axis=1)
        out_blocks, in_blocks = z_whole(w_out), z_whole(w_in)

    def parity(array, which):
        if per_head == 1:
            return lax.dynamic_slice_in_dim(array, which * block, block, 1)
        parts = array.reshape(tokens, per_head, 2, block)
        return lax.dynamic_index_in_dim(parts, which, 2, False).reshape(tokens, half)

    resid_own = parity(resid_in, y)
    resid_far = y_swap(parity(resid_in, 1 - y))

    code_one, rate_one = decay_code[0], decay_rate[0][None, :]
    first_one, end_one, payload_one = chunk_states(
        x_in, bc_in[:, :state_width], step_in, code_one, rate_one
    )
    within_one = within_blocks(x_in, bc_in, step_in, code_one, rate_one, skip_gain[0][None, :])
    carried_one = exchange_states(end_one, payload_one, y)
    scaled, square_own = whole_call(
        gated_kernel,
        [shape((tokens, width), BF16), shape((1, tokens), F32)],
        4 * x_in.size * state_width,
        *carried_one,
        first_one,
        within_one,
        bc_in[:, state_width:],
        code_one,
        rate_one,
        gate_in,
        norm_gain[None, :],
    )
    scaled_far = y_swap(scaled)
    square_own = square_own + c_swap(square_own)
    square_own = square_own + x_swap(square_own)
    square_far = y_swap(square_own)
    square_one = jnp.concatenate(
        [jnp.where(first, square_own, square_far), jnp.where(first, square_far, square_own)], axis=1
    )[0]
    resid = jnp.concatenate(
        [jnp.where(first, resid_own, resid_far), jnp.where(first, resid_far, resid_own)], axis=0
    ).astype(F32)

    keep_heads = [2 * (x_bit ^ i) + c_bit for i in range(2)]
    send_heads = [2 * (x_bit ^ i) + (1 - c_bit) for i in range(2)]
    if line:
        where = lambda heads: jnp.stack([y] + [z - h for h in heads]).astype(jnp.int32)
        (sends,) = out_call(
            where(send_heads),
            scaled,
            scaled_far,
            out_blocks,
            [shape((2, pair_tokens, block), BF16)],
        )
        keeps = out_call(
            where(keep_heads),
            scaled,
            scaled_far,
            out_blocks,
            [shape((pair_tokens, block), F32)] * 2,
        )
    else:
        both = jnp.concatenate(
            [jnp.where(first, scaled, scaled_far), jnp.where(first, scaled_far, scaled)], axis=0
        )
        by_head = out_blocks.reshape(head_size, per_head, width, block)
        by_head = by_head.transpose(0, 2, 1, 3).reshape(head_size, width, half)
        product = lambda h: jnp.dot(both, pick(by_head, h), preferred_element_type=F32)
        sends = jnp.stack([product(h) for h in send_heads]).astype(BF16)
        keeps = [product(h) for h in keep_heads]
    received = c_swap(sends)
    crossing = x_swap((keeps[1] + received[1].astype(F32)).astype(BF16))
    partial_share = keeps[0] + received[0].astype(F32) + crossing.astype(F32)
    resid_new = (
        resid + partial_share * lax.rsqrt(square_one / inner_count + 1e-05)[:, None]
    ).astype(BF16)

    resid_back = y_swap(lax.dynamic_slice_in_dim(resid_new, (1 - y) * tokens, tokens, 0))
    resid_mine = lax.dynamic_slice_in_dim(resid_new, y * tokens, tokens, 0)
    both = [jnp.where(first, resid_mine, resid_back), jnp.where(first, resid_back, resid_mine)]
    if per_head == 1:
        resid_out = jnp.concatenate(both, axis=1)
    else:
        both = [a.reshape(tokens, per_head, block) for a in both]
        resid_out = jnp.stack(both, axis=2).reshape(tokens, width)

    gains = resid_gain.reshape(z_size, 2, block)
    gain = lax.dynamic_slice_in_dim(
        lax.dynamic_index_in_dim(gains, y, 1, False), head * per_head, per_head, 0
    ).reshape(half)
    hidden_wide = resid_new.astype(F32)
    hidden = (hidden_wide * gain[None, :]).astype(BF16)
    pair = jnp.stack([hidden, x_swap(hidden)])
    other = c_swap(pair)
    square_two = jnp.sum(hidden_wide * hidden_wide, axis=1)
    square_two = square_two + x_swap(square_two)
    square_two = square_two + c_swap(square_two)
    square_two = square_two + y_swap(square_two)
    all_hidden = jnp.stack([pair[0], other[0], pair[1], other[1]])
    halo_hidden = z_shift(all_hidden[:, pair_tokens - HALO :], 1)
    halo_square = z_shift(square_two[pair_tokens - HALO :], 1)
    all_hidden = jnp.concatenate([halo_hidden, all_hidden], axis=1)
    scale_two = lax.rsqrt(jnp.concatenate([halo_square, square_two]) / inner_count + 1e-05)

    reach = tokens + HALO
    keep_start = jnp.where(first, 0, tokens)
    send_start = tokens - keep_start
    if line:
        spots = [z - (head ^ k) for k in range(4)]
        where = lambda start: jnp.stack([start] + spots).astype(jnp.int32)
        columns = width + small
        theirs = in_call(where(send_start), all_hidden, in_blocks, reach, columns, BF16)
        mine = in_call(where(keep_start), all_hidden, in_blocks, reach, columns, F32)
    else:
        wide = jnp.concatenate([pick(all_hidden, head ^ i) for i in range(head_size)], axis=1)
        total = jnp.dot(
            wide, in_blocks.reshape(z_size * block, w_in.shape[1]), preferred_element_type=F32
        )
        mine = lax.dynamic_slice_in_dim(total, keep_start, reach, 0)
        theirs = lax.dynamic_slice_in_dim(total, send_start, reach, 0).astype(BF16)
    scale_mine = lax.dynamic_slice_in_dim(scale_two, keep_start, reach, 0)
    taps = jnp.concatenate(
        [conv_x, lax.dynamic_slice_in_dim(conv_bc, head * share, share, 1)], axis=1
    ).astype(F32)
    x_two, bc_share, step_two = conv_call(
        mine,
        y_swap(theirs),
        scale_mine[:, None],
        taps,
        step_time_bias[None, :],
        tokens,
        width,
        share,
    )
    bc_pair = jnp.stack([bc_share, x_swap(bc_share)])
    bc_other = c_swap(bc_pair)
    bc_stack = jnp.stack([bc_pair[0], bc_other[0], bc_pair[1], bc_other[1]])
    bc_two = jnp.concatenate([pick(bc_stack, head ^ i) for i in range(head_size)], axis=1)

    code_two, rate_two = decay_code[1], decay_rate[1][None, :]
    first_two, end_two, payload_two = chunk_states(
        x_two, bc_two[:, :state_width], step_two, code_two, rate_two
    )
    within_two = within_blocks(x_two, bc_two, step_two, code_two, rate_two, skip_gain[1][None, :])
    carried_two = exchange_states(end_two, payload_two, y)
    mixed_two, square_last = whole_call(
        last_kernel,
        [shape((tokens, width), F32), shape((1, tokens), F32)],
        4 * x_in.size * state_width,
        *carried_two,
        first_two,
        within_two,
        bc_two[:, state_width:],
        code_two,
        rate_two,
    )
    square_last = lax.psum(square_last[0], "head")
    mixer_out = (mixed_two * lax.rsqrt(square_last / inner_count + 1e-05)[:, None]).astype(BF16)
    return (resid_out, mixer_out)


def solution(mesh):
    in_specs = (
        P("seq", "head"),
        P("seq", "head"),
        P("seq", None),
        P("seq", "head"),
        P(None, "seq", "head"),
        P(None, "head"),
        P(None, "head"),
        P("head"),
        P("head", "seq"),
        P("seq", "head"),
        P(),
        P("seq", "head"),
        P("seq", None),
        P("seq", "head"),
        P("head"),
        P(None, "head"),
        P(),
    )
    out_specs = (P("seq", "head"), P("seq", "head"))

    return jax.shard_map(
        on_device, mesh=mesh, in_specs=in_specs, out_specs=out_specs, check_vma=False
    )
```

```python
import functools
import jax
import jax.numpy as jnp
from jax import lax
from jax.experimental import pallas as pl
from jax.experimental.pallas import tpu as pltpu
from jax.sharding import PartitionSpec as P

HEAD_CHANNELS = 64
GROUP = 256
HALO = 16
ROWS = 256
F32 = jnp.float32
BF16 = jnp.bfloat16


def z_shift(value, by):
    n = lax.axis_size("seq")
    pairs = [(i, i + 2 * by) for i in range(n) if 0 <= i + 2 * by < n]
    return lax.ppermute(value, "seq", pairs)


def flip(value, axis, bit):
    n = lax.axis_size(axis)
    return lax.ppermute(value, axis, [(i, i ^ bit) for i in range(n)])


def y_swap(value):
    return flip(value, "seq", 1)


def x_swap(value):
    return flip(value, "head", 2)


def c_swap(value):
    return flip(value, "head", 1)


def z_line(value):
    ups, downs = [value], [value]
    for _ in range(1, 4):
        ups.append(z_shift(ups[-1], 1))
        downs.append(z_shift(downs[-1], -1))
    return downs[:0:-1] + ups


def z_whole(value):
    size = lax.axis_size("seq") // 2
    groups = [[2 * i + y for i in range(size)] for y in range(2)]
    return lax.all_gather(value, "seq", axis_index_groups=groups)


HIGHEST = lax.Precision.HIGHEST
LOW = -1e30


def spread(heads):
    channels = heads * HEAD_CHANNELS
    row = lax.broadcasted_iota(jnp.int32, (heads, channels), 0)
    column = lax.broadcasted_iota(jnp.int32, (heads, channels), 1)
    return (column // HEAD_CHANNELS == row).astype(F32)


def exact_dot(a, b):
    return jnp.dot(a, b, precision=HIGHEST, preferred_element_type=F32)


def running_decay(code, rate):
    decay = -jnp.minimum(code.astype(F32) * rate, 20.0)
    rows = code.shape[0]
    lower = (
        lax.broadcasted_iota(jnp.int32, (rows, rows), 0)
        >= lax.broadcasted_iota(jnp.int32, (rows, rows), 1)
    ).astype(F32)
    return exact_dot(lower, decay)


def state_kernel(x_ref, b_ref, step_ref, code_ref, rate_ref, first_ref, end_ref, payload_ref):
    tokens, channels = x_ref.shape
    heads = channels // HEAD_CHANNELS
    table = spread(heads)
    end = None
    decay = jnp.zeros((1, heads), F32)
    for start in range(0, tokens, GROUP):
        rows = pl.ds(start, GROUP)
        total = running_decay(code_ref[rows, :], rate_ref[...])
        last = total[GROUP - 1 :, :]
        weight = exact_dot(jnp.exp(last - total) * step_ref[rows, :], table)
        v = (x_ref[rows, :].astype(F32) * weight).astype(BF16)
        term = lax.dot_general(
            b_ref[rows, :], v, (((0,), (0,)), ((), ())), preferred_element_type=F32
        )
        if end is None:
            first_ref[...] = term
            end = term
        else:
            end = end * exact_dot(jnp.exp(last), table) + term
        decay = decay + last
    end_ref[...] = end
    put_payload(payload_ref, end, exact_dot(decay, table))


def put_payload(payload_ref, state, wide):
    width, channels = state.shape
    payload_ref[:width, :] = state.astype(BF16)
    high = wide.astype(BF16)
    rest = wide - high.astype(F32)
    middle = rest.astype(BF16)
    low = rest - middle.astype(F32)
    row = lax.broadcasted_iota(jnp.int32, (16, channels), 0)
    tail = jnp.where(
        row == 0,
        high.astype(F32),
        jnp.where(row == 1, middle.astype(F32), jnp.where(row == 2, low, 0.0)),
    )
    payload_ref[width:, :] = tail.astype(BF16)


def get_payload(payload_ref):
    width = payload_ref.shape[0] - 16
    tail = payload_ref[width:, :].astype(F32)
    return payload_ref[:width, :].astype(F32), tail[0:1] + tail[1:2] + tail[2:3]


def pair_kernel(
    y_ref, end_ref, own_ref, far_ref, window_ref, payload_ref, early_ref, early_decay_ref
):
    first = y_ref[0] == 0
    own, own_decay = end_ref[...], get_payload(own_ref)[1]
    far, far_decay = get_payload(far_ref)
    early, early_decay = jnp.where(first, own, far), jnp.where(first, own_decay, far_decay)
    late, late_decay = jnp.where(first, far, own), jnp.where(first, far_decay, own_decay)
    window = jnp.exp(late_decay) * early + late
    window_ref[...] = window
    put_payload(payload_ref, window, early_decay + late_decay)
    early_ref[...] = early
    early_decay_ref[...] = early_decay


def step_kernel(
    window_ref, own_ref, far_ref, before_ref, decay_ref, *outs
):
    window_out, payload_ref, before_out, decay_out = outs
    far, far_decay = get_payload(far_ref)
    own_decay = get_payload(own_ref)[1]
    window = jnp.exp(own_decay) * far + window_ref[...]
    window_out[...] = window
    put_payload(payload_ref, window, own_decay + far_decay)
    before_out[...] = before_ref[...] + jnp.exp(decay_ref[...]) * far
    decay_out[...] = decay_ref[...] + far_decay


def start_kernel(window_ref, own_ref, far_ref, *outs):
    window_out, payload_ref, before_out, decay_out = outs
    far, far_decay = get_payload(far_ref)
    own_decay = get_payload(own_ref)[1]
    window = jnp.exp(own_decay) * far + window_ref[...]
    window_out[...] = window
    put_payload(payload_ref, window, own_decay + far_decay)
    before_out[...] = far
    decay_out[...] = far_decay


def entering(y_ref, early_ref, early_decay_ref, before_ref, decay_ref, far_ref):
    far, _ = get_payload(far_ref)
    before = before_ref[...] + jnp.exp(decay_ref[...]) * far
    late = jnp.exp(early_decay_ref[...]) * before + early_ref[...]
    return jnp.where(y_ref[0] == 0, before, late)


def within_kernel(x_ref, bc_ref, step_ref, code_ref, rate_ref, skip_ref, out_ref):
    rows, channels = x_ref.shape
    heads = channels // HEAD_CHANNELS
    width = bc_ref.shape[1] // 2
    half = rows // 2
    total = running_decay(code_ref[...], rate_ref[...])
    across = total.T
    step = step_ref[...].T
    scores = lax.dot_general(
        bc_ref[:, width:],
        bc_ref[:, :width],
        (((1,), (1,)), ((), ())),
        preferred_element_type=F32,
    )
    skip = exact_dot(skip_ref[...], spread(heads))
    keep = lax.broadcasted_iota(jnp.int32, (half, half), 0) >= lax.broadcasted_iota(
        jnp.int32, (half, half), 1
    )
    lane = lax.broadcasted_iota(jnp.int32, (rows, 2 * HEAD_CHANNELS), 1)
    for pair in range(heads // 2):
        columns = pl.ds(pair * 2 * HEAD_CHANNELS, 2 * HEAD_CHANNELS)
        u = x_ref[:, columns]
        halves = []
        for h in (2 * pair, 2 * pair + 1):
            column = total[:, h : h + 1]
            line = across[h : h + 1, :]
            weight = step[h : h + 1, :]
            top = jnp.exp(jnp.where(keep, column[:half] - line[:, :half], LOW))
            top = (top * scores[:half, :half] * weight[:, :half]).astype(BF16)
            left = jnp.exp(column[half:] - line[:, :half])
            left = (left * scores[half:, :half] * weight[:, :half]).astype(BF16)
            right = jnp.exp(jnp.where(keep, column[half:] - line[:, half:], LOW))
            right = (right * scores[half:, half:] * weight[:, half:]).astype(BF16)
            upper = jnp.dot(top, u[:half], preferred_element_type=F32)
            lower = jnp.dot(
                jnp.concatenate([left, right], axis=1), u, preferred_element_type=F32
            )
            halves.append(jnp.concatenate([upper, lower], axis=0))
        mixed = jnp.where(lane < HEAD_CHANNELS, halves[0], halves[1])
        out_ref[:, columns] = mixed + skip[:, pair * 128 : pair * 128 + 128] * u.astype(F32)


def finish_group(start, state, within_ref, c_ref, code_ref, rate_ref, table):
    rows = pl.ds(start, GROUP)
    total = running_decay(code_ref[rows, :], rate_ref[...])
    c = c_ref[rows, :]
    high = state.astype(BF16)
    low = (state - high.astype(F32)).astype(BF16)
    carried = jnp.dot(
        jnp.concatenate([c, c], axis=1),
        jnp.concatenate([high, low], axis=0),
        preferred_element_type=F32,
    )
    mixed = within_ref[rows, :] + carried * exact_dot(jnp.exp(total), table)
    return mixed, exact_dot(jnp.exp(total[GROUP - 1 :, :]), table)


def gated_kernel(
    y_ref,
    early_ref,
    early_decay_ref,
    before_ref,
    decay_ref,
    far_ref,
    first_ref,
    within_ref,
    c_ref,
    code_ref,
    rate_ref,
    gate_ref,
    gain_ref,
    out_ref,
    square_ref,
):
    tokens, channels = within_ref.shape
    table = spread(channels // HEAD_CHANNELS)
    state = entering(y_ref, early_ref, early_decay_ref, before_ref, decay_ref, far_ref)
    for start in range(0, tokens, GROUP):
        mixed, decay = finish_group(start, state, within_ref, c_ref, code_ref, rate_ref, table)
        state = state * decay + first_ref[...]
        gate = gate_ref[pl.ds(start, GROUP), :].astype(F32)
        gated = mixed * (gate / (1.0 + jnp.exp(-gate)))
        out_ref[pl.ds(start, GROUP), :] = (gated * gain_ref[...]).astype(BF16)
        square_ref[:, pl.ds(start, GROUP)] = jnp.sum(gated * gated, axis=1, keepdims=True).T


def last_kernel(
    y_ref,
    early_ref,
    early_decay_ref,
    before_ref,
    decay_ref,
    far_ref,
    first_ref,
    within_ref,
    c_ref,
    code_ref,
    rate_ref,
    out_ref,
    square_ref,
):
    tokens, channels = within_ref.shape
    table = spread(channels // HEAD_CHANNELS)
    state = entering(y_ref, early_ref, early_decay_ref, before_ref, decay_ref, far_ref)
    for start in range(0, tokens, GROUP):
        mixed, decay = finish_group(start, state, within_ref, c_ref, code_ref, rate_ref, table)
        state = state * decay + first_ref[...]
        out_ref[pl.ds(start, GROUP), :] = mixed
        square_ref[:, pl.ds(start, GROUP)] = jnp.sum(mixed * mixed, axis=1, keepdims=True).T


VMEM_SPEC = pl.BlockSpec(memory_space=pltpu.VMEM)
SMEM_SPEC = pl.BlockSpec(memory_space=pltpu.SMEM)
HBM_SPEC = pl.BlockSpec(memory_space=pltpu.HBM)


def whole_call(kernel, outs, flops, *args):
    moved = sum(a.size * a.dtype.itemsize for a in args)
    moved += sum(o.size * o.dtype.itemsize for o in outs)
    return pl.pallas_call(
        kernel,
        out_shape=outs,
        in_specs=[SMEM_SPEC if a.shape == (1,) else VMEM_SPEC for a in args],
        out_specs=[VMEM_SPEC] * len(outs),
        cost_estimate=pl.CostEstimate(flops=flops, bytes_accessed=moved, transcendentals=0),
        compiler_params=pltpu.CompilerParams(vmem_limit_bytes=16 * 2**20),
    )(*args)


def shape(dims, kind):
    return jax.ShapeDtypeStruct(dims, kind)


def chunk_states(x, b, step, code, rate):
    width, channels = b.shape[1], x.shape[1]
    return whole_call(
        state_kernel,
        [
            shape((width, channels), F32),
            shape((width, channels), F32),
            shape((width + 16, channels), BF16),
        ],
        4 * x.size * width,
        x,
        b,
        step,
        code,
        rate,
    )


def within_blocks(x, bc, step, code, rate, skip):
    tokens, channels = x.shape
    heads = step.shape[1]
    row = lambda cols: pl.BlockSpec((GROUP, cols), lambda i: (i, 0))
    one = pl.BlockSpec((1, heads), lambda i: (0, 0))
    return pl.pallas_call(
        within_kernel,
        name="within",
        grid=(tokens // GROUP,),
        out_shape=shape((tokens, channels), F32),
        in_specs=[row(channels), row(bc.shape[1]), row(heads), row(heads), one, one],
        out_specs=row(channels),
        cost_estimate=pl.CostEstimate(
            flops=16 * x.size * GROUP, bytes_accessed=8 * x.size, transcendentals=0
        ),
        compiler_params=pltpu.CompilerParams(vmem_limit_bytes=12 * 2**20),
    )(x, bc, step, code, rate, skip)


def convolved(mine_ref, far_ref, scale, taps_ref, pre_ref, start, size, tokens):
    rows, count = mine_ref.shape[0], taps_ref.shape[0]
    columns = pl.ds(start, size)
    pre = (mine_ref[:, columns] + far_ref[:, columns].astype(F32)) * scale
    pre_ref[:, :size] = pre.astype(BF16).astype(F32)
    total = None
    for tap in range(count):
        first = rows - tokens - count + 1 + tap
        part = pre_ref[pl.ds(first, tokens), :size] * taps_ref[tap : tap + 1, columns]
        total = part if total is None else total + part
    return (total / (1.0 + jnp.exp(-total))).astype(BF16)


def conv_kernel(mine_ref, far_ref, scale_ref, taps_ref, *refs):
    if len(refs) == 2:
        x_ref, pre_ref = refs
    else:
        bias_ref, x_ref, bc_ref, step_ref, late_ref, pre_ref = refs
    tokens, width = x_ref.shape
    scale = scale_ref[...]

    @pl.loop(0, width, step=128)
    def _(start):
        start = pl.multiple_of(start, 128)
        x_ref[:, pl.ds(start, 128)] = convolved(
            mine_ref, far_ref, scale, taps_ref, pre_ref, start, 128, tokens
        )

    if len(refs) > 2:
        share, heads = bc_ref.shape[1], step_ref.shape[1]
        bc_ref[...] = convolved(mine_ref, far_ref, scale, taps_ref, pre_ref, width, share, tokens)
        columns = pl.ds(width + share, 2 * heads)
        raw = (mine_ref[:, columns] + far_ref[:, columns].astype(F32)) * scale
        raw = raw[mine_ref.shape[0] - tokens :] + bias_ref[...]
        steps = jnp.maximum(raw, 0.0) + jnp.log1p(jnp.exp(-jnp.abs(raw)))
        step_ref[...] = steps[:, :heads]
        late_ref[...] = steps[:, heads:]


def conv_call(outs, mine, *args):
    return pl.pallas_call(
        conv_kernel,
        out_shape=outs,
        in_specs=[VMEM_SPEC] * (1 + len(args)),
        out_specs=[VMEM_SPEC] * len(outs),
        scratch_shapes=[pltpu.VMEM((mine.shape[0], 128), F32)],
        cost_estimate=pl.CostEstimate(
            flops=16 * mine.size, bytes_accessed=8 * mine.size, transcendentals=mine.size
        ),
        compiler_params=pltpu.CompilerParams(vmem_limit_bytes=12 * 2**20),
    )(mine, *args)


def fetch(spot, sources, buffer, sem, start):
    reach = len(sources) // 2
    for k in range(len(sources)):

        @pl.when(spot == k - reach)
        def _():
            copy = pltpu.make_async_copy(sources[k], buffer, sem)
            if start:
                copy.start()
            else:
                copy.wait()


def out_kernel(count, where_ref, own_ref, far_ref, *refs):
    sources, outs, (buffers, sems) = refs[:7], refs[7:-2], refs[-2:]
    tokens = own_ref.shape[0]
    own_start = pl.multiple_of(where_ref[0] * tokens, tokens)
    far_start = pl.multiple_of((1 - where_ref[0]) * tokens, tokens)
    fetch(where_ref[1], sources, buffers.at[0], sems.at[0], True)
    for i in range(count):
        if i + 1 < count:
            slot = (i + 1) % 2
            fetch(where_ref[i + 2], sources, buffers.at[slot], sems.at[slot], True)
        fetch(where_ref[i + 1], sources, buffers.at[i % 2], sems.at[i % 2], False)
        for ref, start in ((own_ref, own_start), (far_ref, far_start)):

            @pl.loop(0, tokens, step=ROWS)
            def _(row):
                row = pl.multiple_of(row, ROWS)
                product = jnp.dot(
                    ref[pl.ds(row, ROWS), :], buffers[i % 2], preferred_element_type=F32
                )
                if len(outs) == 1:
                    outs[0][i, pl.ds(start + row, ROWS), :] = product.astype(outs[0].dtype)
                else:
                    outs[i][pl.ds(start + row, ROWS), :] = product.astype(outs[i].dtype)


def in_kernel(count, place, where_ref, hidden_ref, *refs):
    sources, (out_ref, buffers, total, sems) = refs[:7], refs[7:]
    rows = out_ref.shape[0]
    fetch(where_ref[1], sources, buffers.at[0], sems.at[0], True)
    for i in range(count):
        if i + 1 < count:
            slot = (i + 1) % 2
            fetch(where_ref[i + 2], sources, buffers.at[slot], sems.at[slot], True)
        fetch(where_ref[i + 1], sources, buffers.at[i % 2], sems.at[i % 2], False)
        depth, wide = hidden_ref.shape[2], buffers.shape[2] // 2
        packed = buffers[i % 2, depth:, :]
        below = jnp.concatenate([packed[:, :depth], packed[:, depth:]], axis=0)

        @pl.loop(0, rows, step=rows // 3)
        def _(row):
            here = pl.ds(pl.multiple_of(row, HALO), rows // 3)
            there = pl.ds(pl.multiple_of(where_ref[0] + row, HALO), rows // 3)
            hidden = hidden_ref[i, there, :]
            weight = buffers[i % 2, :depth, place * wide : (place + 1) * wide]
            products = [(jnp.dot(hidden, weight, preferred_element_type=F32), slice(0, wide))]
            if out_ref.shape[1] > wide:
                small = lax.dot_general(
                    hidden, below, (((1,), (1,)), ((), ())), preferred_element_type=F32
                )[:, : out_ref.shape[1] - wide]
                products.append((small, slice(wide, out_ref.shape[1])))
            for part, columns in products:
                if i == 0:
                    total[here, columns] = part
                elif i + 1 < count:
                    total[here, columns] += part
                else:
                    out_ref[here, columns] = (total[here, columns] + part).astype(out_ref.dtype)


def out_call(where, own, far, sources, outs):
    count = where.shape[0] - 1
    tokens, depth = own.shape
    block = sources[0].shape
    return pl.pallas_call(
        functools.partial(out_kernel, count),
        out_shape=outs,
        in_specs=[SMEM_SPEC, VMEM_SPEC, VMEM_SPEC] + [HBM_SPEC] * len(sources),
        out_specs=[VMEM_SPEC] * len(outs),
        scratch_shapes=[pltpu.VMEM((2,) + block, BF16), pltpu.SemaphoreType.DMA((2,))],
        cost_estimate=pl.CostEstimate(
            flops=4 * count * tokens * depth * block[1],
            bytes_accessed=4 * own.size + 2 * count * sources[0].size,
            transcendentals=0,
        ),
        compiler_params=pltpu.CompilerParams(vmem_limit_bytes=60 * 2**20),
    )(where, own, far, *sources)


def in_call(place, where, hidden, sources, rows, columns, kind):
    count, _, depth = hidden.shape
    block = sources[0].shape
    return pl.pallas_call(
        functools.partial(in_kernel, count, place),
        out_shape=shape((rows, columns), kind),
        in_specs=[SMEM_SPEC, VMEM_SPEC] + [HBM_SPEC] * len(sources),
        out_specs=VMEM_SPEC,
        scratch_shapes=[
            pltpu.VMEM((2,) + block, BF16),
            pltpu.VMEM((rows, columns), F32),
            pltpu.SemaphoreType.DMA((2,)),
        ],
        cost_estimate=pl.CostEstimate(
            flops=2 * count * rows * depth * block[1],
            bytes_accessed=2 * hidden.size + 2 * count * sources[0].size,
            transcendentals=0,
        ),
        compiler_params=pltpu.CompilerParams(vmem_limit_bytes=60 * 2**20),
    )(where, hidden, *sources)


def pick(stack, index):
    return lax.dynamic_index_in_dim(stack, index, 0, False)


def exchange_states(end, payload, y):
    full, packed = shape(end.shape, F32), shape(payload.shape, BF16)
    row = shape((1, end.shape[1]), F32)
    flag = y[None].astype(jnp.int32)
    far = y_swap(payload)
    window, payload, early, early_decay = whole_call(
        pair_kernel, [full, packed, full, row], end.size, flag, end, payload, far
    )
    parts = ()
    reach, size = 1, lax.axis_size("seq") // 2
    while 2 * reach < size:
        far = z_shift(payload, reach)
        window, payload, *parts = whole_call(
            step_kernel if parts else start_kernel,
            [full, packed, full, row],
            end.size,
            window,
            payload,
            far,
            *parts,
        )
        reach *= 2
    far = z_shift(payload, reach)
    return (flag, early, early_decay, *parts, far)


def on_device(
    x_in,
    gate_in,
    bc_in,
    step_in,
    decay_code,
    decay_rate,
    skip_gain,
    norm_gain,
    w_out,
    resid_in,
    resid_gain,
    w_in_x,
    w_in_bc,
    w_in_dt,
    step_time_bias,
    conv_x,
    conv_bc,
):
    tokens, width = x_in.shape
    seq_size, head_size = lax.axis_size("seq"), lax.axis_size("head")
    z_size = seq_size // 2
    seq_place, head = lax.axis_index("seq"), lax.axis_index("head")
    z, y = seq_place // 2, seq_place % 2
    x_bit, c_bit = head // 2, head % 2
    inner_count = width * head_size
    pair_tokens = 2 * tokens
    state_width = bc_in.shape[1] // 2
    block = w_out.shape[1]
    half = width // 2
    per_head = z_size // head_size
    first = y == 0
    line = z_size == 4 and per_head == 1

    share = w_in_bc.shape[1] // head_size
    bc_weight = lax.dynamic_slice_in_dim(w_in_bc, head * share, share, 1)
    small = share + w_in_dt.shape[1]
    if line:
        below = jnp.concatenate([bc_weight, w_in_dt], axis=1).T
        below = jnp.concatenate([below, jnp.zeros((-small % 32, block), BF16)], axis=0)
        below = below.reshape(2, below.shape[0] // 2, block)
        below = jnp.concatenate([below[0], below[1]], axis=1)
        out_blocks = z_line(w_out)
        in_blocks = z_line(jnp.concatenate([w_in_x, below], axis=0))
    else:
        w_in = jnp.concatenate([w_in_x, bc_weight, w_in_dt], axis=1)
        out_blocks, in_blocks = z_whole(w_out), z_whole(w_in)

    def parity(array, which):
        if per_head == 1:
            return lax.dynamic_slice_in_dim(array, which * block, block, 1)
        parts = array.reshape(tokens, per_head, 2, block)
        return lax.dynamic_index_in_dim(parts, which, 2, False).reshape(tokens, half)

    resid_own = parity(resid_in, y)
    resid_far = y_swap(parity(resid_in, 1 - y))

    code_one, rate_one = decay_code[0], decay_rate[0][None, :]
    first_one, end_one, payload_one = chunk_states(
        x_in, bc_in[:, :state_width], step_in, code_one, rate_one
    )
    within_one = within_blocks(x_in, bc_in, step_in, code_one, rate_one, skip_gain[0][None, :])
    carried_one = exchange_states(end_one, payload_one, y)
    scaled, square_own = whole_call(
        gated_kernel,
        [shape((tokens, width), BF16), shape((1, tokens), F32)],
        4 * x_in.size * state_width,
        *carried_one,
        first_one,
        within_one,
        bc_in[:, state_width:],
        code_one,
        rate_one,
        gate_in,
        norm_gain[None, :],
    )
    scaled_far = y_swap(scaled)
    square_own = square_own + c_swap(square_own)
    square_own = square_own + x_swap(square_own)
    square_far = y_swap(square_own)
    square_one = jnp.concatenate(
        [jnp.where(first, square_own, square_far), jnp.where(first, square_far, square_own)], axis=1
    )[0]
    resid = jnp.concatenate(
        [jnp.where(first, resid_own, resid_far), jnp.where(first, resid_far, resid_own)], axis=0
    ).astype(F32)

    keep_heads = [2 * (x_bit ^ i) + c_bit for i in range(2)]
    send_heads = [2 * (x_bit ^ i) + (1 - c_bit) for i in range(2)]
    if line:
        where = lambda heads: jnp.stack([y] + [z - h for h in heads]).astype(jnp.int32)
        (sends,) = out_call(
            where(send_heads),
            scaled,
            scaled_far,
            out_blocks,
            [shape((2, pair_tokens, block), BF16)],
        )
        keeps = out_call(
            where(keep_heads),
            scaled,
            scaled_far,
            out_blocks,
            [shape((pair_tokens, block), F32)] * 2,
        )
    else:
        both = jnp.concatenate(
            [jnp.where(first, scaled, scaled_far), jnp.where(first, scaled_far, scaled)], axis=0
        )
        by_head = out_blocks.reshape(head_size, per_head, width, block)
        by_head = by_head.transpose(0, 2, 1, 3).reshape(head_size, width, half)
        product = lambda h: jnp.dot(both, pick(by_head, h), preferred_element_type=F32)
        sends = jnp.stack([product(h) for h in send_heads]).astype(BF16)
        keeps = [product(h) for h in keep_heads]
    received = c_swap(sends)
    crossing = x_swap((keeps[1] + received[1].astype(F32)).astype(BF16))
    partial_share = keeps[0] + received[0].astype(F32) + crossing.astype(F32)
    resid_new = (
        resid + partial_share * lax.rsqrt(square_one / inner_count + 1e-05)[:, None]
    ).astype(BF16)

    resid_back = y_swap(lax.dynamic_slice_in_dim(resid_new, (1 - y) * tokens, tokens, 0))
    resid_mine = lax.dynamic_slice_in_dim(resid_new, y * tokens, tokens, 0)
    both = [jnp.where(first, resid_mine, resid_back), jnp.where(first, resid_back, resid_mine)]
    if per_head == 1:
        resid_out = jnp.concatenate(both, axis=1)
    else:
        both = [a.reshape(tokens, per_head, block) for a in both]
        resid_out = jnp.stack(both, axis=2).reshape(tokens, width)

    gains = resid_gain.reshape(z_size, 2, block)
    gain = lax.dynamic_slice_in_dim(
        lax.dynamic_index_in_dim(gains, y, 1, False), head * per_head, per_head, 0
    ).reshape(half)
    hidden_wide = resid_new.astype(F32)
    hidden = (hidden_wide * gain[None, :]).astype(BF16)
    pair = jnp.stack([hidden, x_swap(hidden)])
    other = c_swap(pair)
    square_two = jnp.sum(hidden_wide * hidden_wide, axis=1)
    square_two = square_two + x_swap(square_two)
    square_two = square_two + c_swap(square_two)
    square_two = square_two + y_swap(square_two)
    all_hidden = jnp.stack([pair[0], other[0], pair[1], other[1]])
    halo_hidden = z_shift(all_hidden[:, pair_tokens - HALO :], 1)
    halo_square = z_shift(square_two[pair_tokens - HALO :], 1)
    all_hidden = jnp.concatenate([halo_hidden, all_hidden], axis=1)
    scale_two = lax.rsqrt(jnp.concatenate([halo_square, square_two]) / inner_count + 1e-05)

    reach = tokens + HALO
    keep_start = jnp.where(first, 0, tokens)
    send_start = tokens - keep_start
    columns = (half + small, half)
    if line:
        spots = [z - (head ^ k) for k in range(4)]
        where = lambda start: jnp.stack([start] + spots).astype(jnp.int32)
        project = lambda place, start, kind: in_call(
            place, where(start), all_hidden, in_blocks, reach, columns[place], kind
        )
        theirs = [project(0, send_start, BF16), project(1, send_start, BF16)]
        mine = [project(0, keep_start, F32), project(1, keep_start, F32)]
    else:
        wide = jnp.concatenate([pick(all_hidden, head ^ i) for i in range(head_size)], axis=1)
        total = jnp.dot(
            wide, in_blocks.reshape(z_size * block, w_in.shape[1]), preferred_element_type=F32
        )
        total = [jnp.concatenate([total[:, :half], total[:, width:]], axis=1), total[:, half:width]]
        mine = [lax.dynamic_slice_in_dim(t, keep_start, reach, 0) for t in total]
        theirs = [lax.dynamic_slice_in_dim(t, send_start, reach, 0).astype(BF16) for t in total]
    scale_mine = lax.dynamic_slice_in_dim(scale_two, keep_start, reach, 0)[:, None]
    bc_taps = lax.dynamic_slice_in_dim(conv_bc, head * share, share, 1)
    taps = jnp.concatenate([conv_x[:, :half], bc_taps], axis=1).astype(F32)
    head_half = decay_code.shape[2] // 2
    far_a = y_swap(theirs[0])
    x_a, bc_share, step_a, step_b = conv_call(
        [
            shape((tokens, half), BF16),
            shape((tokens, share), BF16),
            shape((tokens, head_half), F32),
            shape((tokens, head_half), F32),
        ],
        mine[0],
        far_a,
        scale_mine,
        taps,
        step_time_bias[None, :],
    )
    (x_b,) = conv_call(
        [shape((tokens, half), BF16)],
        mine[1],
        y_swap(theirs[1]),
        scale_mine,
        conv_x[:, half:].astype(F32),
    )
    bc_pair = jnp.stack([bc_share, x_swap(bc_share)])
    bc_other = c_swap(bc_pair)
    bc_stack = jnp.stack([bc_pair[0], bc_other[0], bc_pair[1], bc_other[1]])
    bc_two = jnp.concatenate([pick(bc_stack, head ^ i) for i in range(head_size)], axis=1)

    mixed, squares = [], []
    for x, step, picked in (
        (x_a, step_a, slice(0, head_half)), (x_b, step_b, slice(head_half, None))
    ):
        code, rate = decay_code[1][:, picked], decay_rate[1][None, picked]
        first_two, end, payload = chunk_states(x, bc_two[:, :state_width], step, code, rate)
        within = within_blocks(x, bc_two, step, code, rate, skip_gain[1][None, picked])
        part, square = whole_call(
            last_kernel,
            [shape((tokens, half), F32), shape((1, tokens), F32)],
            4 * x.size * state_width,
            *exchange_states(end, payload, y),
            first_two,
            within,
            bc_two[:, state_width:],
            code,
            rate,
        )
        mixed.append(part)
        squares.append(square[0])
    square_last = lax.psum(squares[0] + squares[1], "head")
    scale_last = lax.rsqrt(square_last / inner_count + 1e-05)[:, None]
    mixer_out = jnp.concatenate([(part * scale_last).astype(BF16) for part in mixed], axis=1)
    return (resid_out, mixer_out)


def solution(mesh):
    in_specs = (
        P("seq", "head"),
        P("seq", "head"),
        P("seq", None),
        P("seq", "head"),
        P(None, "seq", "head"),
        P(None, "head"),
        P(None, "head"),
        P("head"),
        P("head", "seq"),
        P("seq", "head"),
        P(),
        P("seq", "head"),
        P("seq", None),
        P("seq", "head"),
        P("head"),
        P(None, "head"),
        P(),
    )
    out_specs = (P("seq", "head"), P("seq", "head"))

    return jax.shard_map(
        on_device, mesh=mesh, in_specs=in_specs, out_specs=out_specs, check_vma=False
    )
```

```python
import functools
import jax
import jax.numpy as jnp
from jax import lax
from jax.experimental import pallas as pl
from jax.experimental.pallas import tpu as pltpu
from jax.sharding import PartitionSpec as P

HEAD_CHANNELS = 64
GROUP = 256
HALO = 16
ROWS = 256
F32 = jnp.float32
BF16 = jnp.bfloat16


def z_shift(value, by):
    n = lax.axis_size("seq")
    pairs = [(i, i + 2 * by) for i in range(n) if 0 <= i + 2 * by < n]
    return lax.ppermute(value, "seq", pairs)


def flip(value, axis, bit):
    n = lax.axis_size(axis)
    return lax.ppermute(value, axis, [(i, i ^ bit) for i in range(n)])


def y_swap(value):
    return flip(value, "seq", 1)


def x_swap(value):
    return flip(value, "head", 2)


def c_swap(value):
    return flip(value, "head", 1)


def z_line(value, place):
    ups, downs = [value], [value]
    for _ in range(1, 4):
        ups.append(z_shift(ups[-1], 1))
        downs.append(z_shift(downs[-1], -1))
    early, low, high = place >= 1, place == 0, place == 3
    blocks = [
        value,
        jnp.where(early, ups[1], downs[1]),
        jnp.where(place >= 2, ups[2], downs[2]),
        jnp.where(low, downs[3], jnp.where(high, ups[3], downs[1])),
    ]
    places = [
        place,
        jnp.where(early, place - 1, 1),
        (place + 2) % 4,
        jnp.where(low, 3, jnp.where(high, 0, place + 1)),
    ]
    return blocks, places


def z_whole(value):
    size = lax.axis_size("seq") // 2
    groups = [[2 * i + y for i in range(size)] for y in range(2)]
    return lax.all_gather(value, "seq", axis_index_groups=groups)


HIGHEST = lax.Precision.HIGHEST
LOW = -1e30


def spread(heads):
    channels = heads * HEAD_CHANNELS
    row = lax.broadcasted_iota(jnp.int32, (heads, channels), 0)
    column = lax.broadcasted_iota(jnp.int32, (heads, channels), 1)
    return (column // HEAD_CHANNELS == row).astype(F32)


def exact_dot(a, b):
    return jnp.dot(a, b, precision=HIGHEST, preferred_element_type=F32)


def running_decay(code, rate):
    decay = -jnp.minimum(code.astype(F32) * rate, 20.0)
    rows = code.shape[0]
    lower = (
        lax.broadcasted_iota(jnp.int32, (rows, rows), 0)
        >= lax.broadcasted_iota(jnp.int32, (rows, rows), 1)
    ).astype(F32)
    return exact_dot(lower, decay)


def state_kernel(x_ref, b_ref, step_ref, code_ref, rate_ref, first_ref, end_ref, payload_ref):
    tokens, channels = x_ref.shape
    heads = channels // HEAD_CHANNELS
    table = spread(heads)
    end = None
    decay = jnp.zeros((1, heads), F32)
    for start in range(0, tokens, GROUP):
        rows = pl.ds(start, GROUP)
        total = running_decay(code_ref[rows, :], rate_ref[...])
        last = total[GROUP - 1 :, :]
        weight = exact_dot(jnp.exp(last - total) * step_ref[rows, :], table)
        v = (x_ref[rows, :].astype(F32) * weight).astype(BF16)
        term = lax.dot_general(
            b_ref[rows, :], v, (((0,), (0,)), ((), ())), preferred_element_type=F32
        )
        if end is None:
            first_ref[...] = term
            end = term
        else:
            end = end * exact_dot(jnp.exp(last), table) + term
        decay = decay + last
    end_ref[...] = end
    put_payload(payload_ref, end, exact_dot(decay, table))


def put_payload(payload_ref, state, wide):
    width, channels = state.shape
    payload_ref[:width, :] = state.astype(BF16)
    high = wide.astype(BF16)
    rest = wide - high.astype(F32)
    middle = rest.astype(BF16)
    low = rest - middle.astype(F32)
    row = lax.broadcasted_iota(jnp.int32, (16, channels), 0)
    tail = jnp.where(
        row == 0,
        high.astype(F32),
        jnp.where(row == 1, middle.astype(F32), jnp.where(row == 2, low, 0.0)),
    )
    payload_ref[width:, :] = tail.astype(BF16)


def get_payload(payload_ref):
    width = payload_ref.shape[0] - 16
    tail = payload_ref[width:, :].astype(F32)
    return payload_ref[:width, :].astype(F32), tail[0:1] + tail[1:2] + tail[2:3]


def pair_kernel(
    y_ref, end_ref, own_ref, far_ref, window_ref, payload_ref, early_ref, early_decay_ref
):
    first = y_ref[0] == 0
    own, own_decay = end_ref[...], get_payload(own_ref)[1]
    far, far_decay = get_payload(far_ref)
    early, early_decay = jnp.where(first, own, far), jnp.where(first, own_decay, far_decay)
    late, late_decay = jnp.where(first, far, own), jnp.where(first, far_decay, own_decay)
    window = jnp.exp(late_decay) * early + late
    window_ref[...] = window
    put_payload(payload_ref, window, early_decay + late_decay)
    early_ref[...] = early
    early_decay_ref[...] = early_decay


def step_kernel(
    window_ref, own_ref, far_ref, before_ref, decay_ref, *outs
):
    window_out, payload_ref, before_out, decay_out = outs
    far, far_decay = get_payload(far_ref)
    own_decay = get_payload(own_ref)[1]
    window = jnp.exp(own_decay) * far + window_ref[...]
    window_out[...] = window
    put_payload(payload_ref, window, own_decay + far_decay)
    before_out[...] = before_ref[...] + jnp.exp(decay_ref[...]) * far
    decay_out[...] = decay_ref[...] + far_decay


def start_kernel(window_ref, own_ref, far_ref, *outs):
    window_out, payload_ref, before_out, decay_out = outs
    far, far_decay = get_payload(far_ref)
    own_decay = get_payload(own_ref)[1]
    window = jnp.exp(own_decay) * far + window_ref[...]
    window_out[...] = window
    put_payload(payload_ref, window, own_decay + far_decay)
    before_out[...] = far
    decay_out[...] = far_decay


def entering(y_ref, early_ref, early_decay_ref, before_ref, decay_ref, far_ref):
    far, _ = get_payload(far_ref)
    before = before_ref[...] + jnp.exp(decay_ref[...]) * far
    late = jnp.exp(early_decay_ref[...]) * before + early_ref[...]
    return jnp.where(y_ref[0] == 0, before, late)


def within_kernel(x_ref, bc_ref, step_ref, code_ref, rate_ref, skip_ref, out_ref):
    rows, channels = x_ref.shape
    heads = channels // HEAD_CHANNELS
    width = bc_ref.shape[1] // 2
    half = rows // 2
    total = running_decay(code_ref[...], rate_ref[...])
    across = total.T
    step = step_ref[...].T
    scores = lax.dot_general(
        bc_ref[:, width:],
        bc_ref[:, :width],
        (((1,), (1,)), ((), ())),
        preferred_element_type=F32,
    )
    skip = exact_dot(skip_ref[...], spread(heads))
    keep = lax.broadcasted_iota(jnp.int32, (half, half), 0) >= lax.broadcasted_iota(
        jnp.int32, (half, half), 1
    )
    lane = lax.broadcasted_iota(jnp.int32, (rows, 2 * HEAD_CHANNELS), 1)
    for pair in range(heads // 2):
        columns = pl.ds(pair * 2 * HEAD_CHANNELS, 2 * HEAD_CHANNELS)
        u = x_ref[:, columns]
        halves = []
        for h in (2 * pair, 2 * pair + 1):
            column = total[:, h : h + 1]
            line = across[h : h + 1, :]
            weight = step[h : h + 1, :]
            top = jnp.exp(jnp.where(keep, column[:half] - line[:, :half], LOW))
            top = (top * scores[:half, :half] * weight[:, :half]).astype(BF16)
            left = jnp.exp(column[half:] - line[:, :half])
            left = (left * scores[half:, :half] * weight[:, :half]).astype(BF16)
            right = jnp.exp(jnp.where(keep, column[half:] - line[:, half:], LOW))
            right = (right * scores[half:, half:] * weight[:, half:]).astype(BF16)
            upper = jnp.dot(top, u[:half], preferred_element_type=F32)
            lower = jnp.dot(
                jnp.concatenate([left, right], axis=1), u, preferred_element_type=F32
            )
            halves.append(jnp.concatenate([upper, lower], axis=0))
        mixed = jnp.where(lane < HEAD_CHANNELS, halves[0], halves[1])
        out_ref[:, columns] = mixed + skip[:, pair * 128 : pair * 128 + 128] * u.astype(F32)


def finish_group(start, state, within_ref, c_ref, code_ref, rate_ref, table):
    rows = pl.ds(start, GROUP)
    total = running_decay(code_ref[rows, :], rate_ref[...])
    c = c_ref[rows, :]
    high = state.astype(BF16)
    low = (state - high.astype(F32)).astype(BF16)
    carried = jnp.dot(
        jnp.concatenate([c, c], axis=1),
        jnp.concatenate([high, low], axis=0),
        preferred_element_type=F32,
    )
    mixed = within_ref[rows, :] + carried * exact_dot(jnp.exp(total), table)
    return mixed, exact_dot(jnp.exp(total[GROUP - 1 :, :]), table)


def gated_kernel(
    y_ref,
    early_ref,
    early_decay_ref,
    before_ref,
    decay_ref,
    far_ref,
    first_ref,
    within_ref,
    c_ref,
    code_ref,
    rate_ref,
    gate_ref,
    gain_ref,
    out_ref,
    square_ref,
):
    tokens, channels = within_ref.shape
    table = spread(channels // HEAD_CHANNELS)
    state = entering(y_ref, early_ref, early_decay_ref, before_ref, decay_ref, far_ref)
    for start in range(0, tokens, GROUP):
        mixed, decay = finish_group(start, state, within_ref, c_ref, code_ref, rate_ref, table)
        state = state * decay + first_ref[...]
        gate = gate_ref[pl.ds(start, GROUP), :].astype(F32)
        gated = mixed * (gate / (1.0 + jnp.exp(-gate)))
        out_ref[pl.ds(start, GROUP), :] = (gated * gain_ref[...]).astype(BF16)
        square_ref[:, pl.ds(start, GROUP)] = jnp.sum(gated * gated, axis=1, keepdims=True).T


def last_kernel(
    y_ref,
    early_ref,
    early_decay_ref,
    before_ref,
    decay_ref,
    far_ref,
    first_ref,
    within_ref,
    c_ref,
    code_ref,
    rate_ref,
    out_ref,
    square_ref,
):
    tokens, channels = within_ref.shape
    table = spread(channels // HEAD_CHANNELS)
    state = entering(y_ref, early_ref, early_decay_ref, before_ref, decay_ref, far_ref)
    for start in range(0, tokens, GROUP):
        mixed, decay = finish_group(start, state, within_ref, c_ref, code_ref, rate_ref, table)
        state = state * decay + first_ref[...]
        out_ref[pl.ds(start, GROUP), :] = mixed
        square_ref[:, pl.ds(start, GROUP)] = jnp.sum(mixed * mixed, axis=1, keepdims=True).T


VMEM_SPEC = pl.BlockSpec(memory_space=pltpu.VMEM)
SMEM_SPEC = pl.BlockSpec(memory_space=pltpu.SMEM)


def whole_call(kernel, outs, flops, *args):
    moved = sum(a.size * a.dtype.itemsize for a in args)
    moved += sum(o.size * o.dtype.itemsize for o in outs)
    return pl.pallas_call(
        kernel,
        out_shape=outs,
        in_specs=[SMEM_SPEC if a.shape == (1,) else VMEM_SPEC for a in args],
        out_specs=[VMEM_SPEC] * len(outs),
        cost_estimate=pl.CostEstimate(flops=flops, bytes_accessed=moved, transcendentals=0),
        compiler_params=pltpu.CompilerParams(vmem_limit_bytes=16 * 2**20),
    )(*args)


def shape(dims, kind):
    return jax.ShapeDtypeStruct(dims, kind)


def chunk_states(x, b, step, code, rate):
    width, channels = b.shape[1], x.shape[1]
    return whole_call(
        state_kernel,
        [
            shape((width, channels), F32),
            shape((width, channels), F32),
            shape((width + 16, channels), BF16),
        ],
        4 * x.size * width,
        x,
        b,
        step,
        code,
        rate,
    )


def within_blocks(x, bc, step, code, rate, skip):
    tokens, channels = x.shape
    heads = step.shape[1]
    row = lambda cols: pl.BlockSpec((GROUP, cols), lambda i: (i, 0))
    one = pl.BlockSpec((1, heads), lambda i: (0, 0))
    return pl.pallas_call(
        within_kernel,
        name="within",
        grid=(tokens // GROUP,),
        out_shape=shape((tokens, channels), F32),
        in_specs=[row(channels), row(bc.shape[1]), row(heads), row(heads), one, one],
        out_specs=row(channels),
        cost_estimate=pl.CostEstimate(
            flops=16 * x.size * GROUP, bytes_accessed=8 * x.size, transcendentals=0
        ),
        compiler_params=pltpu.CompilerParams(vmem_limit_bytes=12 * 2**20),
    )(x, bc, step, code, rate, skip)


def convolved(mine_ref, far_ref, scale, taps_ref, pre_ref, start, size, tokens):
    rows, count = mine_ref.shape[0], taps_ref.shape[0]
    columns = pl.ds(start, size)
    pre = (mine_ref[:, columns] + far_ref[:, columns].astype(F32)) * scale
    pre_ref[:, :size] = pre.astype(BF16).astype(F32)
    total = None
    for tap in range(count):
        first = rows - tokens - count + 1 + tap
        part = pre_ref[pl.ds(first, tokens), :size] * taps_ref[tap : tap + 1, columns]
        total = part if total is None else total + part
    return (total / (1.0 + jnp.exp(-total))).astype(BF16)


def conv_kernel(mine_ref, far_ref, scale_ref, taps_ref, *refs):
    if len(refs) == 2:
        x_ref, pre_ref = refs
    else:
        bias_ref, x_ref, bc_ref, step_ref, late_ref, pre_ref = refs
    tokens, width = x_ref.shape
    scale = scale_ref[...]

    @pl.loop(0, width, step=128)
    def _(start):
        start = pl.multiple_of(start, 128)
        x_ref[:, pl.ds(start, 128)] = convolved(
            mine_ref, far_ref, scale, taps_ref, pre_ref, start, 128, tokens
        )

    if len(refs) > 2:
        share, heads = bc_ref.shape[1], step_ref.shape[1]
        bc_ref[...] = convolved(mine_ref, far_ref, scale, taps_ref, pre_ref, width, share, tokens)
        columns = pl.ds(width + share, 2 * heads)
        raw = (mine_ref[:, columns] + far_ref[:, columns].astype(F32)) * scale
        raw = raw[mine_ref.shape[0] - tokens :] + bias_ref[...]
        steps = jnp.maximum(raw, 0.0) + jnp.log1p(jnp.exp(-jnp.abs(raw)))
        step_ref[...] = steps[:, :heads]
        late_ref[...] = steps[:, heads:]


def conv_call(outs, mine, *args):
    return pl.pallas_call(
        conv_kernel,
        out_shape=outs,
        in_specs=[VMEM_SPEC] * (1 + len(args)),
        out_specs=[VMEM_SPEC] * len(outs),
        scratch_shapes=[pltpu.VMEM((mine.shape[0], 128), F32)],
        cost_estimate=pl.CostEstimate(
            flops=16 * mine.size, bytes_accessed=8 * mine.size, transcendentals=mine.size
        ),
        compiler_params=pltpu.CompilerParams(vmem_limit_bytes=12 * 2**20),
    )(mine, *args)


def out_kernel(where_ref, own_ref, far_ref, *refs):
    blocks, (send_ref, keep_ref) = refs[:4], refs[4:]
    tokens = own_ref.shape[0]
    own_start = pl.multiple_of(where_ref[0] * tokens, tokens)
    far_start = pl.multiple_of((1 - where_ref[0]) * tokens, tokens)
    for i, block_ref in enumerate(blocks):
        kept, spot = where_ref[2 * i + 1], where_ref[2 * i + 2]
        for ref, start in ((own_ref, own_start), (far_ref, far_start)):

            @pl.loop(0, tokens, step=ROWS)
            def _(row):
                row = pl.multiple_of(row, ROWS)
                product = jnp.dot(
                    ref[pl.ds(row, ROWS), :], block_ref[...], preferred_element_type=F32
                )

                @pl.when(kept == 1)
                def _():
                    keep_ref[spot, pl.ds(start + row, ROWS), :] = product

                @pl.when(kept == 0)
                def _():
                    send_ref[spot, pl.ds(start + row, ROWS), :] = product.astype(BF16)


def in_kernel(place, where_ref, hidden_ref, *refs):
    blocks, out_ref = refs[:4], refs[4]
    rows, columns = out_ref.shape
    depth = hidden_ref.shape[2]
    wide = blocks[0].shape[1] // 2

    @pl.loop(0, rows, step=rows // 3)
    def _(row):
        here = pl.ds(pl.multiple_of(row, HALO), rows // 3)
        there = pl.ds(pl.multiple_of(where_ref[0] + row, HALO), rows // 3)
        large, small = None, None
        for i, block_ref in enumerate(blocks):
            hidden = hidden_ref[where_ref[i + 1], there, :]
            weight = block_ref[:depth, place * wide : (place + 1) * wide]
            part = jnp.dot(hidden, weight, preferred_element_type=F32)
            large = part if large is None else large + part
            if columns > wide:
                packed = block_ref[depth:, :]
                part = lax.dot_general(
                    hidden,
                    jnp.concatenate([packed[:, :depth], packed[:, depth:]], axis=0),
                    (((1,), (1,)), ((), ())),
                    preferred_element_type=F32,
                )
                small = part if small is None else small + part
        out_ref[here, :wide] = large.astype(out_ref.dtype)
        if columns > wide:
            out_ref[here, wide:] = small[:, : columns - wide].astype(out_ref.dtype)


def out_call(where, own, far, blocks):
    tokens, depth = own.shape
    width = blocks[0].shape[1]
    return pl.pallas_call(
        out_kernel,
        name="out",
        out_shape=[shape((2, 2 * tokens, width), BF16), shape((2, 2 * tokens, width), F32)],
        in_specs=[SMEM_SPEC] + [VMEM_SPEC] * (2 + len(blocks)),
        out_specs=[VMEM_SPEC] * 2,
        cost_estimate=pl.CostEstimate(
            flops=16 * tokens * depth * width,
            bytes_accessed=4 * own.size + 8 * blocks[0].size,
            transcendentals=0,
        ),
        compiler_params=pltpu.CompilerParams(vmem_limit_bytes=16 * 2**20),
    )(where, own, far, *blocks)


def in_call(place, where, hidden, blocks, rows, columns, kind):
    count, _, depth = hidden.shape
    return pl.pallas_call(
        functools.partial(in_kernel, place),
        out_shape=shape((rows, columns), kind),
        in_specs=[SMEM_SPEC] + [VMEM_SPEC] * (1 + len(blocks)),
        out_specs=VMEM_SPEC,
        cost_estimate=pl.CostEstimate(
            flops=2 * count * rows * depth * columns,
            bytes_accessed=2 * (hidden.size + count * depth * columns),
            transcendentals=0,
        ),
        compiler_params=pltpu.CompilerParams(vmem_limit_bytes=16 * 2**20),
    )(where, hidden, *blocks)


def join_kernel(y_ref, mine_ref, back_ref, out_ref):
    first = y_ref[0] == 0
    half = mine_ref.shape[1]
    out_ref[:, :half] = jnp.where(first, mine_ref[...], back_ref[...])
    out_ref[:, half:] = jnp.where(first, back_ref[...], mine_ref[...])


def pick(stack, index):
    return lax.dynamic_index_in_dim(stack, index, 0, False)


def exchange_states(end, payload, y):
    full, packed = shape(end.shape, F32), shape(payload.shape, BF16)
    row = shape((1, end.shape[1]), F32)
    flag = y[None].astype(jnp.int32)
    far = y_swap(payload)
    window, payload, early, early_decay = whole_call(
        pair_kernel, [full, packed, full, row], end.size, flag, end, payload, far
    )
    parts = ()
    reach, size = 1, lax.axis_size("seq") // 2
    while 2 * reach < size:
        far = z_shift(payload, reach)
        window, payload, *parts = whole_call(
            step_kernel if parts else start_kernel,
            [full, packed, full, row],
            end.size,
            window,
            payload,
            far,
            *parts,
        )
        reach *= 2
    far = z_shift(payload, reach)
    return (flag, early, early_decay, *parts, far)


def on_device(
    x_in,
    gate_in,
    bc_in,
    step_in,
    decay_code,
    decay_rate,
    skip_gain,
    norm_gain,
    w_out,
    resid_in,
    resid_gain,
    w_in_x,
    w_in_bc,
    w_in_dt,
    step_time_bias,
    conv_x,
    conv_bc,
):
    tokens, width = x_in.shape
    seq_size, head_size = lax.axis_size("seq"), lax.axis_size("head")
    z_size = seq_size // 2
    seq_place, head = lax.axis_index("seq"), lax.axis_index("head")
    z, y = seq_place // 2, seq_place % 2
    x_bit, c_bit = head // 2, head % 2
    inner_count = width * head_size
    pair_tokens = 2 * tokens
    state_width = bc_in.shape[1] // 2
    block = w_out.shape[1]
    half = width // 2
    per_head = z_size // head_size
    first = y == 0
    line = z_size == 4 and per_head == 1

    share = w_in_bc.shape[1] // head_size
    bc_weight = lax.dynamic_slice_in_dim(w_in_bc, head * share, share, 1)
    small = share + w_in_dt.shape[1]
    if line:
        below = jnp.concatenate([bc_weight, w_in_dt], axis=1).T
        below = jnp.concatenate([below, jnp.zeros((-small % 32, block), BF16)], axis=0)
        below = below.reshape(2, below.shape[0] // 2, block)
        below = jnp.concatenate([below[0], below[1]], axis=1)
        out_blocks, out_places = z_line(w_out, z)
        in_blocks, in_places = z_line(jnp.concatenate([w_in_x, below], axis=0), z)
    else:
        w_in = jnp.concatenate([w_in_x, bc_weight, w_in_dt], axis=1)
        out_blocks, in_blocks = z_whole(w_out), z_whole(w_in)

    def parity(array, which):
        if per_head == 1:
            return lax.dynamic_slice_in_dim(array, which * block, block, 1)
        parts = array.reshape(tokens, per_head, 2, block)
        return lax.dynamic_index_in_dim(parts, which, 2, False).reshape(tokens, half)

    resid_own = parity(resid_in, y)
    resid_far = y_swap(parity(resid_in, 1 - y))

    code_one, rate_one = decay_code[0], decay_rate[0][None, :]
    first_one, end_one, payload_one = chunk_states(
        x_in, bc_in[:, :state_width], step_in, code_one, rate_one
    )
    within_one = within_blocks(x_in, bc_in, step_in, code_one, rate_one, skip_gain[0][None, :])
    carried_one = exchange_states(end_one, payload_one, y)
    scaled, square_own = whole_call(
        gated_kernel,
        [shape((tokens, width), BF16), shape((1, tokens), F32)],
        4 * x_in.size * state_width,
        *carried_one,
        first_one,
        within_one,
        bc_in[:, state_width:],
        code_one,
        rate_one,
        gate_in,
        norm_gain[None, :],
    )
    scaled_far = y_swap(scaled)
    square_own = square_own + c_swap(square_own)
    square_own = square_own + x_swap(square_own)
    square_far = y_swap(square_own)
    square_one = jnp.concatenate(
        [jnp.where(first, square_own, square_far), jnp.where(first, square_far, square_own)], axis=1
    )[0]
    resid = jnp.concatenate(
        [jnp.where(first, resid_own, resid_far), jnp.where(first, resid_far, resid_own)], axis=0
    ).astype(F32)

    keep_heads = [2 * (x_bit ^ i) + c_bit for i in range(2)]
    send_heads = [2 * (x_bit ^ i) + (1 - c_bit) for i in range(2)]
    if line:
        where = [y]
        for place in out_places:
            where += [(place % 2 == c_bit).astype(jnp.int32), (place // 2) ^ x_bit]
        sends, keeps = out_call(jnp.stack(where).astype(jnp.int32), scaled, scaled_far, out_blocks)
    else:
        both = jnp.concatenate(
            [jnp.where(first, scaled, scaled_far), jnp.where(first, scaled_far, scaled)], axis=0
        )
        by_head = out_blocks.reshape(head_size, per_head, width, block)
        by_head = by_head.transpose(0, 2, 1, 3).reshape(head_size, width, half)
        product = lambda h: jnp.dot(both, pick(by_head, h), preferred_element_type=F32)
        sends = jnp.stack([product(h) for h in send_heads]).astype(BF16)
        keeps = [product(h) for h in keep_heads]
    received = c_swap(sends)
    crossing = x_swap((keeps[1] + received[1].astype(F32)).astype(BF16))
    partial_share = keeps[0] + received[0].astype(F32) + crossing.astype(F32)
    resid_new = (
        resid + partial_share * lax.rsqrt(square_one / inner_count + 1e-05)[:, None]
    ).astype(BF16)

    resid_back = y_swap(lax.dynamic_slice_in_dim(resid_new, (1 - y) * tokens, tokens, 0))
    resid_mine = lax.dynamic_slice_in_dim(resid_new, y * tokens, tokens, 0)
    if per_head == 1:
        (resid_out,) = whole_call(
            join_kernel,
            [shape((tokens, width), BF16)],
            resid_in.size,
            y[None].astype(jnp.int32),
            resid_mine,
            resid_back,
        )
    else:
        both = [jnp.where(first, resid_mine, resid_back), jnp.where(first, resid_back, resid_mine)]
        both = [a.reshape(tokens, per_head, block) for a in both]
        resid_out = jnp.stack(both, axis=2).reshape(tokens, width)

    gains = resid_gain.reshape(z_size, 2, block)
    gain = lax.dynamic_slice_in_dim(
        lax.dynamic_index_in_dim(gains, y, 1, False), head * per_head, per_head, 0
    ).reshape(half)
    hidden_wide = resid_new.astype(F32)
    hidden = (hidden_wide * gain[None, :]).astype(BF16)
    pair = jnp.stack([hidden, x_swap(hidden)])
    other = c_swap(pair)
    square_two = jnp.sum(hidden_wide * hidden_wide, axis=1)
    square_two = square_two + x_swap(square_two)
    square_two = square_two + c_swap(square_two)
    square_two = square_two + y_swap(square_two)
    all_hidden = jnp.stack([pair[0], other[0], pair[1], other[1]])
    halo_hidden = z_shift(all_hidden[:, pair_tokens - HALO :], 1)
    halo_square = z_shift(square_two[pair_tokens - HALO :], 1)
    all_hidden = jnp.concatenate([halo_hidden, all_hidden], axis=1)
    scale_two = lax.rsqrt(jnp.concatenate([halo_square, square_two]) / inner_count + 1e-05)

    reach = tokens + HALO
    keep_start = jnp.where(first, 0, tokens)
    send_start = tokens - keep_start
    columns = (half + small, half)
    if line:
        spots = [place ^ head for place in in_places]
        where = lambda start: jnp.stack([start] + spots).astype(jnp.int32)
        project = lambda place, start, kind: in_call(
            place, where(start), all_hidden, in_blocks, reach, columns[place], kind
        )
        theirs = [project(0, send_start, BF16), project(1, send_start, BF16)]
        mine = [project(0, keep_start, F32), project(1, keep_start, F32)]
    else:
        wide = jnp.concatenate([pick(all_hidden, head ^ i) for i in range(head_size)], axis=1)
        total = jnp.dot(
            wide, in_blocks.reshape(z_size * block, w_in.shape[1]), preferred_element_type=F32
        )
        total = [jnp.concatenate([total[:, :half], total[:, width:]], axis=1), total[:, half:width]]
        mine = [lax.dynamic_slice_in_dim(t, keep_start, reach, 0) for t in total]
        theirs = [lax.dynamic_slice_in_dim(t, send_start, reach, 0).astype(BF16) for t in total]
    scale_mine = lax.dynamic_slice_in_dim(scale_two, keep_start, reach, 0)[:, None]
    bc_taps = lax.dynamic_slice_in_dim(conv_bc, head * share, share, 1)
    taps = jnp.concatenate([conv_x[:, :half], bc_taps], axis=1).astype(F32)
    head_half = decay_code.shape[2] // 2
    far_a = y_swap(theirs[0])
    x_a, bc_share, step_a, step_b = conv_call(
        [
            shape((tokens, half), BF16),
            shape((tokens, share), BF16),
            shape((tokens, head_half), F32),
            shape((tokens, head_half), F32),
        ],
        mine[0],
        far_a,
        scale_mine,
        taps,
        step_time_bias[None, :],
    )
    (x_b,) = conv_call(
        [shape((tokens, half), BF16)],
        mine[1],
        y_swap(theirs[1]),
        scale_mine,
        conv_x[:, half:].astype(F32),
    )
    bc_pair = jnp.stack([bc_share, x_swap(bc_share)])
    bc_other = c_swap(bc_pair)
    bc_stack = jnp.stack([bc_pair[0], bc_other[0], bc_pair[1], bc_other[1]])
    bc_two = jnp.concatenate([pick(bc_stack, head ^ i) for i in range(head_size)], axis=1)

    mixed, squares = [], []
    for x, step, picked in (
        (x_a, step_a, slice(0, head_half)), (x_b, step_b, slice(head_half, None))
    ):
        code, rate = decay_code[1][:, picked], decay_rate[1][None, picked]
        first_two, end, payload = chunk_states(x, bc_two[:, :state_width], step, code, rate)
        within = within_blocks(x, bc_two, step, code, rate, skip_gain[1][None, picked])
        part, square = whole_call(
            last_kernel,
            [shape((tokens, half), F32), shape((1, tokens), F32)],
            4 * x.size * state_width,
            *exchange_states(end, payload, y),
            first_two,
            within,
            bc_two[:, state_width:],
            code,
            rate,
        )
        mixed.append(part)
        squares.append(square[0])
    square_last = lax.psum(squares[0] + squares[1], "head")
    scale_last = lax.rsqrt(square_last / inner_count + 1e-05)[:, None]
    mixer_out = jnp.concatenate([(part * scale_last).astype(BF16) for part in mixed], axis=1)
    return (resid_out, mixer_out)


def solution(mesh):
    in_specs = (
        P("seq", "head"),
        P("seq", "head"),
        P("seq", None),
        P("seq", "head"),
        P(None, "seq", "head"),
        P(None, "head"),
        P(None, "head"),
        P("head"),
        P("head", "seq"),
        P("seq", "head"),
        P(),
        P("seq", "head"),
        P("seq", None),
        P("seq", "head"),
        P("head"),
        P(None, "head"),
        P(),
    )
    out_specs = (P("seq", "head"), P("seq", "head"))

    return jax.shard_map(
        on_device, mesh=mesh, in_specs=in_specs, out_specs=out_specs, check_vma=False
    )
```

```python
import functools
import jax
import jax.numpy as jnp
from jax import lax
from jax.experimental import pallas as pl
from jax.experimental.pallas import tpu as pltpu
from jax.sharding import PartitionSpec as P

HEAD_CHANNELS = 64
GROUP = 256
HALO = 16
ROWS = 256
F32 = jnp.float32
BF16 = jnp.bfloat16


def z_shift(value, by, hops=1):
    n = lax.axis_size("seq")
    pairs = [
        (i, i + 2 * by)
        for i in range(n)
        if 0 <= i + 2 * by < n and 0 <= i - 2 * by * (hops - 1) < n
    ]
    return lax.ppermute(value, "seq", pairs)


def flip(value, axis, bit):
    n = lax.axis_size(axis)
    return lax.ppermute(value, axis, [(i, i ^ bit) for i in range(n)])


def y_swap(value):
    return flip(value, "seq", 1)


def x_swap(value):
    return flip(value, "head", 2)


def c_swap(value):
    return flip(value, "head", 1)


def z_line(value, place):
    ups, downs = [value], [value]
    for step in range(1, 4):
        ups.append(z_shift(ups[-1], 1, step))
        downs.append(z_shift(downs[-1], -1, step))
    early, low, high = place >= 1, place == 0, place == 3
    blocks = [
        value,
        jnp.where(early, ups[1], downs[1]),
        jnp.where(place >= 2, ups[2], downs[2]),
        jnp.where(low, downs[3], jnp.where(high, ups[3], downs[1])),
    ]
    places = [
        place,
        jnp.where(early, place - 1, 1),
        (place + 2) % 4,
        jnp.where(low, 3, jnp.where(high, 0, place + 1)),
    ]
    return blocks, places


def z_whole(value):
    size = lax.axis_size("seq") // 2
    groups = [[2 * i + y for i in range(size)] for y in range(2)]
    return lax.all_gather(value, "seq", axis_index_groups=groups)


HIGHEST = lax.Precision.HIGHEST
LOW = -1e30


def spread(heads):
    channels = heads * HEAD_CHANNELS
    row = lax.broadcasted_iota(jnp.int32, (heads, channels), 0)
    column = lax.broadcasted_iota(jnp.int32, (heads, channels), 1)
    return (column // HEAD_CHANNELS == row).astype(F32)


def exact_dot(a, b):
    return jnp.dot(a, b, precision=HIGHEST, preferred_element_type=F32)


def running_decay(code, rate):
    decay = -jnp.minimum(code.astype(F32) * rate, 20.0)
    rows = code.shape[0]
    lower = (
        lax.broadcasted_iota(jnp.int32, (rows, rows), 0)
        >= lax.broadcasted_iota(jnp.int32, (rows, rows), 1)
    ).astype(F32)
    return exact_dot(lower, decay)


def state_kernel(x_ref, b_ref, step_ref, code_ref, rate_ref, first_ref, end_ref, payload_ref):
    tokens, channels = x_ref.shape
    heads = channels // HEAD_CHANNELS
    table = spread(heads)
    end = None
    decay = jnp.zeros((1, heads), F32)
    for start in range(0, tokens, GROUP):
        rows = pl.ds(start, GROUP)
        total = running_decay(code_ref[rows, :], rate_ref[...])
        last = total[GROUP - 1 :, :]
        weight = exact_dot(jnp.exp(last - total) * step_ref[rows, :], table)
        v = (x_ref[rows, :].astype(F32) * weight).astype(BF16)
        term = lax.dot_general(
            b_ref[rows, :], v, (((0,), (0,)), ((), ())), preferred_element_type=F32
        )
        if end is None:
            first_ref[...] = term
            end = term
        else:
            end = end * exact_dot(jnp.exp(last), table) + term
        decay = decay + last
    end_ref[...] = end
    put_payload(payload_ref, end, exact_dot(decay, table))


def put_payload(payload_ref, state, wide):
    width, channels = state.shape
    payload_ref[:width, :] = state.astype(BF16)
    high = wide.astype(BF16)
    rest = wide - high.astype(F32)
    middle = rest.astype(BF16)
    low = rest - middle.astype(F32)
    row = lax.broadcasted_iota(jnp.int32, (16, channels), 0)
    tail = jnp.where(
        row == 0,
        high.astype(F32),
        jnp.where(row == 1, middle.astype(F32), jnp.where(row == 2, low, 0.0)),
    )
    payload_ref[width:, :] = tail.astype(BF16)


def get_payload(payload_ref):
    width = payload_ref.shape[0] - 16
    tail = payload_ref[width:, :].astype(F32)
    return payload_ref[:width, :].astype(F32), tail[0:1] + tail[1:2] + tail[2:3]


def pair_kernel(
    y_ref, end_ref, own_ref, far_ref, window_ref, payload_ref, early_ref, early_decay_ref
):
    first = y_ref[0] == 0
    own, own_decay = end_ref[...], get_payload(own_ref)[1]
    far, far_decay = get_payload(far_ref)
    early, early_decay = jnp.where(first, own, far), jnp.where(first, own_decay, far_decay)
    late, late_decay = jnp.where(first, far, own), jnp.where(first, far_decay, own_decay)
    window = jnp.exp(late_decay) * early + late
    decay = early_decay + late_decay
    half = window_ref.shape[1]
    if half < window.shape[1]:
        window = jnp.where(first, window[:, :half], window[:, half:])
        decay = jnp.where(first, decay[:, :half], decay[:, half:])
    window_ref[...] = window
    put_payload(payload_ref, window, decay)
    early_ref[...] = early
    early_decay_ref[...] = early_decay


def step_kernel(
    window_ref, own_ref, far_ref, before_ref, decay_ref, *outs
):
    window_out, payload_ref, before_out, decay_out = outs
    far, far_decay = get_payload(far_ref)
    own_decay = get_payload(own_ref)[1]
    window = jnp.exp(own_decay) * far + window_ref[...]
    window_out[...] = window
    put_payload(payload_ref, window, own_decay + far_decay)
    before_out[...] = before_ref[...] + jnp.exp(decay_ref[...]) * far
    decay_out[...] = decay_ref[...] + far_decay


def start_kernel(window_ref, own_ref, far_ref, *outs):
    window_out, payload_ref, before_out, decay_out = outs
    far, far_decay = get_payload(far_ref)
    own_decay = get_payload(own_ref)[1]
    window = jnp.exp(own_decay) * far + window_ref[...]
    window_out[...] = window
    put_payload(payload_ref, window, own_decay + far_decay)
    before_out[...] = far
    decay_out[...] = far_decay


def close_kernel(before_ref, decay_ref, far_ref, out_ref):
    far, _ = get_payload(far_ref)
    out_ref[...] = (before_ref[...] + jnp.exp(decay_ref[...]) * far).astype(BF16)


def entering_halves(y_ref, early_ref, early_decay_ref, own_ref, other_ref):
    first = y_ref[0] == 0
    own, other = own_ref[...].astype(F32), other_ref[...].astype(F32)
    before = jnp.concatenate(
        [jnp.where(first, own, other), jnp.where(first, other, own)], axis=1
    )
    late = jnp.exp(early_decay_ref[...]) * before + early_ref[...]
    return jnp.where(first, before, late)


def entering(y_ref, early_ref, early_decay_ref, before_ref, decay_ref, far_ref):
    far, _ = get_payload(far_ref)
    before = before_ref[...] + jnp.exp(decay_ref[...]) * far
    late = jnp.exp(early_decay_ref[...]) * before + early_ref[...]
    return jnp.where(y_ref[0] == 0, before, late)


def within_kernel(x_ref, bc_ref, step_ref, code_ref, rate_ref, skip_ref, out_ref):
    rows, channels = x_ref.shape
    heads = channels // HEAD_CHANNELS
    width = bc_ref.shape[1] // 2
    half = rows // 2
    total = running_decay(code_ref[...], rate_ref[...])
    across = total.T
    step = step_ref[...].T
    scores = lax.dot_general(
        bc_ref[:, width:],
        bc_ref[:, :width],
        (((1,), (1,)), ((), ())),
        preferred_element_type=F32,
    )
    skip = exact_dot(skip_ref[...], spread(heads))
    keep = lax.broadcasted_iota(jnp.int32, (half, half), 0) >= lax.broadcasted_iota(
        jnp.int32, (half, half), 1
    )
    lane = lax.broadcasted_iota(jnp.int32, (rows, 2 * HEAD_CHANNELS), 1)
    for pair in range(heads // 2):
        columns = pl.ds(pair * 2 * HEAD_CHANNELS, 2 * HEAD_CHANNELS)
        u = x_ref[:, columns]
        halves = []
        for h in (2 * pair, 2 * pair + 1):
            column = total[:, h : h + 1]
            line = across[h : h + 1, :]
            weight = step[h : h + 1, :]
            top = jnp.exp(jnp.where(keep, column[:half] - line[:, :half], LOW))
            top = (top * scores[:half, :half] * weight[:, :half]).astype(BF16)
            left = jnp.exp(column[half:] - line[:, :half])
            left = (left * scores[half:, :half] * weight[:, :half]).astype(BF16)
            right = jnp.exp(jnp.where(keep, column[half:] - line[:, half:], LOW))
            right = (right * scores[half:, half:] * weight[:, half:]).astype(BF16)
            upper = jnp.dot(top, u[:half], preferred_element_type=F32)
            lower = jnp.dot(
                jnp.concatenate([left, right], axis=1), u, preferred_element_type=F32
            )
            halves.append(jnp.concatenate([upper, lower], axis=0))
        mixed = jnp.where(lane < HEAD_CHANNELS, halves[0], halves[1])
        out_ref[:, columns] = mixed + skip[:, pair * 128 : pair * 128 + 128] * u.astype(F32)


def finish_group(start, state, within_ref, c_ref, code_ref, rate_ref, table):
    rows = pl.ds(start, GROUP)
    total = running_decay(code_ref[rows, :], rate_ref[...])
    c = c_ref[rows, :]
    high = state.astype(BF16)
    low = (state - high.astype(F32)).astype(BF16)
    carried = jnp.dot(
        jnp.concatenate([c, c], axis=1),
        jnp.concatenate([high, low], axis=0),
        preferred_element_type=F32,
    )
    mixed = within_ref[rows, :] + carried * exact_dot(jnp.exp(total), table)
    return mixed, exact_dot(jnp.exp(total[GROUP - 1 :, :]), table)


def gated_kernel(
    y_ref,
    early_ref,
    early_decay_ref,
    own_ref,
    other_ref,
    first_ref,
    within_ref,
    c_ref,
    code_ref,
    rate_ref,
    gate_ref,
    gain_ref,
    out_ref,
    square_ref,
):
    tokens, channels = within_ref.shape
    table = spread(channels // HEAD_CHANNELS)
    state = entering_halves(y_ref, early_ref, early_decay_ref, own_ref, other_ref)
    for start in range(0, tokens, GROUP):
        mixed, decay = finish_group(start, state, within_ref, c_ref, code_ref, rate_ref, table)
        state = state * decay + first_ref[...]
        gate = gate_ref[pl.ds(start, GROUP), :].astype(F32)
        gated = mixed * (gate / (1.0 + jnp.exp(-gate)))
        out_ref[pl.ds(start, GROUP), :] = (gated * gain_ref[...]).astype(BF16)
        square_ref[:, pl.ds(start, GROUP)] = jnp.sum(gated * gated, axis=1, keepdims=True).T


def last_kernel(
    y_ref,
    early_ref,
    early_decay_ref,
    before_ref,
    decay_ref,
    far_ref,
    first_ref,
    within_ref,
    c_ref,
    code_ref,
    rate_ref,
    out_ref,
    square_ref,
):
    tokens, channels = within_ref.shape
    table = spread(channels // HEAD_CHANNELS)
    state = entering(y_ref, early_ref, early_decay_ref, before_ref, decay_ref, far_ref)
    for start in range(0, tokens, GROUP):
        mixed, decay = finish_group(start, state, within_ref, c_ref, code_ref, rate_ref, table)
        state = state * decay + first_ref[...]
        out_ref[pl.ds(start, GROUP), :] = mixed
        square_ref[:, pl.ds(start, GROUP)] = jnp.sum(mixed * mixed, axis=1, keepdims=True).T


VMEM_SPEC = pl.BlockSpec(memory_space=pltpu.VMEM)
SMEM_SPEC = pl.BlockSpec(memory_space=pltpu.SMEM)


def whole_call(kernel, outs, flops, *args):
    moved = sum(a.size * a.dtype.itemsize for a in args)
    moved += sum(o.size * o.dtype.itemsize for o in outs)
    return pl.pallas_call(
        kernel,
        out_shape=outs,
        in_specs=[SMEM_SPEC if a.shape == (1,) else VMEM_SPEC for a in args],
        out_specs=[VMEM_SPEC] * len(outs),
        cost_estimate=pl.CostEstimate(flops=flops, bytes_accessed=moved, transcendentals=0),
        compiler_params=pltpu.CompilerParams(vmem_limit_bytes=16 * 2**20),
    )(*args)


def shape(dims, kind):
    return jax.ShapeDtypeStruct(dims, kind)


def chunk_states(x, b, step, code, rate):
    width, channels = b.shape[1], x.shape[1]
    return whole_call(
        state_kernel,
        [
            shape((width, channels), F32),
            shape((width, channels), F32),
            shape((width + 16, channels), BF16),
        ],
        4 * x.size * width,
        x,
        b,
        step,
        code,
        rate,
    )


def within_blocks(x, bc, step, code, rate, skip):
    tokens, channels = x.shape
    heads = step.shape[1]
    row = lambda cols: pl.BlockSpec((GROUP, cols), lambda i: (i, 0))
    one = pl.BlockSpec((1, heads), lambda i: (0, 0))
    return pl.pallas_call(
        within_kernel,
        name="within",
        grid=(tokens // GROUP,),
        out_shape=shape((tokens, channels), F32),
        in_specs=[row(channels), row(bc.shape[1]), row(heads), row(heads), one, one],
        out_specs=row(channels),
        cost_estimate=pl.CostEstimate(
            flops=16 * x.size * GROUP, bytes_accessed=8 * x.size, transcendentals=0
        ),
        compiler_params=pltpu.CompilerParams(vmem_limit_bytes=12 * 2**20),
    )(x, bc, step, code, rate, skip)


def convolved(mine_ref, far_ref, scale, taps_ref, pre_ref, start, size, tokens):
    rows, count = mine_ref.shape[0], taps_ref.shape[0]
    columns = pl.ds(start, size)
    pre = (mine_ref[:, columns] + far_ref[:, columns].astype(F32)) * scale
    pre_ref[:, :size] = pre.astype(BF16).astype(F32)
    total = None
    for tap in range(count):
        first = rows - tokens - count + 1 + tap
        part = pre_ref[pl.ds(first, tokens), :size] * taps_ref[tap : tap + 1, columns]
        total = part if total is None else total + part
    return (total / (1.0 + jnp.exp(-total))).astype(BF16)


def conv_kernel(mine_ref, far_ref, scale_ref, taps_ref, *refs):
    if len(refs) == 2:
        x_ref, pre_ref = refs
    else:
        bias_ref, x_ref, bc_ref, step_ref, late_ref, pre_ref = refs
    tokens, width = x_ref.shape
    scale = scale_ref[...]

    @pl.loop(0, width, step=128)
    def _(start):
        start = pl.multiple_of(start, 128)
        x_ref[:, pl.ds(start, 128)] = convolved(
            mine_ref, far_ref, scale, taps_ref, pre_ref, start, 128, tokens
        )

    if len(refs) > 2:
        share, heads = bc_ref.shape[1], step_ref.shape[1]
        bc_ref[...] = convolved(mine_ref, far_ref, scale, taps_ref, pre_ref, width, share, tokens)
        columns = pl.ds(width + share, 2 * heads)
        raw = (mine_ref[:, columns] + far_ref[:, columns].astype(F32)) * scale
        raw = raw[mine_ref.shape[0] - tokens :] + bias_ref[...]
        steps = jnp.maximum(raw, 0.0) + jnp.log1p(jnp.exp(-jnp.abs(raw)))
        step_ref[...] = steps[:, :heads]
        late_ref[...] = steps[:, heads:]


def conv_call(outs, mine, *args):
    return pl.pallas_call(
        conv_kernel,
        out_shape=outs,
        in_specs=[VMEM_SPEC] * (1 + len(args)),
        out_specs=[VMEM_SPEC] * len(outs),
        scratch_shapes=[pltpu.VMEM((mine.shape[0], 128), F32)],
        cost_estimate=pl.CostEstimate(
            flops=16 * mine.size, bytes_accessed=8 * mine.size, transcendentals=mine.size
        ),
        compiler_params=pltpu.CompilerParams(vmem_limit_bytes=12 * 2**20),
    )(mine, *args)


def out_kernel(where_ref, own_ref, far_ref, *refs):
    blocks, (send_ref, keep_ref) = refs[:4], refs[4:]
    tokens = own_ref.shape[0]
    own_start = pl.multiple_of(where_ref[0] * tokens, tokens)
    far_start = pl.multiple_of((1 - where_ref[0]) * tokens, tokens)
    for i, block_ref in enumerate(blocks):
        kept, spot = where_ref[2 * i + 1], where_ref[2 * i + 2]
        for ref, start in ((own_ref, own_start), (far_ref, far_start)):

            @pl.loop(0, tokens, step=ROWS)
            def _(row):
                row = pl.multiple_of(row, ROWS)
                product = jnp.dot(
                    ref[pl.ds(row, ROWS), :], block_ref[...], preferred_element_type=F32
                )

                @pl.when(kept == 1)
                def _():
                    keep_ref[spot, pl.ds(start + row, ROWS), :] = product

                @pl.when(kept == 0)
                def _():
                    send_ref[spot, pl.ds(start + row, ROWS), :] = product.astype(BF16)


def in_kernel(place, where_ref, hidden_ref, *refs):
    blocks, out_ref = refs[:4], refs[4]
    rows, columns = out_ref.shape
    depth = hidden_ref.shape[2]
    wide = blocks[0].shape[1] // 2

    @pl.loop(0, rows, step=rows // 3)
    def _(row):
        here = pl.ds(pl.multiple_of(row, HALO), rows // 3)
        there = pl.ds(pl.multiple_of(where_ref[0] + row, HALO), rows // 3)
        large, small = None, None
        for i, block_ref in enumerate(blocks):
            hidden = hidden_ref[where_ref[i + 1], there, :]
            weight = block_ref[:depth, place * wide : (place + 1) * wide]
            part = jnp.dot(hidden, weight, preferred_element_type=F32)
            large = part if large is None else large + part
            if columns > wide:
                packed = block_ref[depth:, :]
                part = lax.dot_general(
                    hidden,
                    jnp.concatenate([packed[:, :depth], packed[:, depth:]], axis=0),
                    (((1,), (1,)), ((), ())),
                    preferred_element_type=F32,
                )
                small = part if small is None else small + part
        out_ref[here, :wide] = large.astype(out_ref.dtype)
        if columns > wide:
            out_ref[here, wide:] = small[:, : columns - wide].astype(out_ref.dtype)


def out_call(where, own, far, blocks):
    tokens, depth = own.shape
    width = blocks[0].shape[1]
    return pl.pallas_call(
        out_kernel,
        name="out",
        out_shape=[shape((2, 2 * tokens, width), BF16), shape((2, 2 * tokens, width), F32)],
        in_specs=[SMEM_SPEC] + [VMEM_SPEC] * (2 + len(blocks)),
        out_specs=[VMEM_SPEC] * 2,
        cost_estimate=pl.CostEstimate(
            flops=16 * tokens * depth * width,
            bytes_accessed=4 * own.size + 8 * blocks[0].size,
            transcendentals=0,
        ),
        compiler_params=pltpu.CompilerParams(vmem_limit_bytes=16 * 2**20),
    )(where, own, far, *blocks)


def in_call(place, where, hidden, blocks, rows, columns, kind):
    count, _, depth = hidden.shape
    return pl.pallas_call(
        functools.partial(in_kernel, place),
        out_shape=shape((rows, columns), kind),
        in_specs=[SMEM_SPEC] + [VMEM_SPEC] * (1 + len(blocks)),
        out_specs=VMEM_SPEC,
        cost_estimate=pl.CostEstimate(
            flops=2 * count * rows * depth * columns,
            bytes_accessed=2 * (hidden.size + count * depth * columns),
            transcendentals=0,
        ),
        compiler_params=pltpu.CompilerParams(vmem_limit_bytes=16 * 2**20),
    )(where, hidden, *blocks)


def join_kernel(y_ref, mine_ref, back_ref, out_ref):
    first = y_ref[0] == 0
    half = mine_ref.shape[1]
    out_ref[:, :half] = jnp.where(first, mine_ref[...], back_ref[...])
    out_ref[:, half:] = jnp.where(first, back_ref[...], mine_ref[...])


def pick(stack, index):
    return lax.dynamic_index_in_dim(stack, index, 0, False)


def exchange_states(end, payload, y, split):
    part = end.shape[1] // 2 if split else end.shape[1]
    full, row = shape(end.shape, F32), shape((1, end.shape[1]), F32)
    piece, packed = shape((end.shape[0], part), F32), shape((payload.shape[0], part), BF16)
    piece_row = shape((1, part), F32)
    flag = y[None].astype(jnp.int32)
    far = y_swap(payload)
    window, payload, early, early_decay = whole_call(
        pair_kernel, [piece, packed, full, row], end.size, flag, end, payload, far
    )
    parts = ()
    reach, size = 1, lax.axis_size("seq") // 2
    while 2 * reach < size:
        far = z_shift(payload, reach)
        window, payload, *parts = whole_call(
            step_kernel if parts else start_kernel,
            [piece, packed, piece, piece_row],
            end.size,
            window,
            payload,
            far,
            *parts,
        )
        reach *= 2
    far = z_shift(payload, reach)
    if split:
        (own,) = whole_call(close_kernel, [shape(piece.shape, BF16)], end.size, *parts, far)
        return (flag, early, early_decay, own, y_swap(own))
    return (flag, early, early_decay, *parts, far)


def on_device(
    x_in,
    gate_in,
    bc_in,
    step_in,
    decay_code,
    decay_rate,
    skip_gain,
    norm_gain,
    w_out,
    resid_in,
    resid_gain,
    w_in_x,
    w_in_bc,
    w_in_dt,
    step_time_bias,
    conv_x,
    conv_bc,
):
    tokens, width = x_in.shape
    seq_size, head_size = lax.axis_size("seq"), lax.axis_size("head")
    z_size = seq_size // 2
    seq_place, head = lax.axis_index("seq"), lax.axis_index("head")
    z, y = seq_place // 2, seq_place % 2
    x_bit, c_bit = head // 2, head % 2
    inner_count = width * head_size
    pair_tokens = 2 * tokens
    state_width = bc_in.shape[1] // 2
    block = w_out.shape[1]
    half = width // 2
    per_head = z_size // head_size
    first = y == 0
    line = z_size == 4 and per_head == 1

    share = w_in_bc.shape[1] // head_size
    bc_weight = lax.dynamic_slice_in_dim(w_in_bc, head * share, share, 1)
    small = share + w_in_dt.shape[1]
    if line:
        below = jnp.concatenate([bc_weight, w_in_dt], axis=1).T
        below = jnp.concatenate([below, jnp.zeros((-small % 32, block), BF16)], axis=0)
        below = below.reshape(2, below.shape[0] // 2, block)
        below = jnp.concatenate([below[0], below[1]], axis=1)
        out_blocks, out_places = z_line(w_out, z)
        in_blocks, in_places = z_line(jnp.concatenate([w_in_x, below], axis=0), z)
    else:
        w_in = jnp.concatenate([w_in_x, bc_weight, w_in_dt], axis=1)
        out_blocks, in_blocks = z_whole(w_out), z_whole(w_in)

    def parity(array, which):
        if per_head == 1:
            return lax.dynamic_slice_in_dim(array, which * block, block, 1)
        parts = array.reshape(tokens, per_head, 2, block)
        return lax.dynamic_index_in_dim(parts, which, 2, False).reshape(tokens, half)

    resid_own = parity(resid_in, y)
    resid_far = y_swap(parity(resid_in, 1 - y))

    code_one, rate_one = decay_code[0], decay_rate[0][None, :]
    first_one, end_one, payload_one = chunk_states(
        x_in, bc_in[:, :state_width], step_in, code_one, rate_one
    )
    within_one = within_blocks(x_in, bc_in, step_in, code_one, rate_one, skip_gain[0][None, :])
    carried_one = exchange_states(end_one, payload_one, y, True)
    scaled, square_own = whole_call(
        gated_kernel,
        [shape((tokens, width), BF16), shape((1, tokens), F32)],
        4 * x_in.size * state_width,
        *carried_one,
        first_one,
        within_one,
        bc_in[:, state_width:],
        code_one,
        rate_one,
        gate_in,
        norm_gain[None, :],
    )
    scaled_far = y_swap(scaled)
    square_own = square_own + c_swap(square_own)
    square_own = square_own + x_swap(square_own)
    square_far = y_swap(square_own)
    square_one = jnp.concatenate(
        [jnp.where(first, square_own, square_far), jnp.where(first, square_far, square_own)], axis=1
    )[0]
    resid = jnp.concatenate(
        [jnp.where(first, resid_own, resid_far), jnp.where(first, resid_far, resid_own)], axis=0
    ).astype(F32)

    keep_heads = [2 * (x_bit ^ i) + c_bit for i in range(2)]
    send_heads = [2 * (x_bit ^ i) + (1 - c_bit) for i in range(2)]
    if line:
        where = [y]
        for place in out_places:
            where += [(place % 2 == c_bit).astype(jnp.int32), (place // 2) ^ x_bit]
        sends, keeps = out_call(jnp.stack(where).astype(jnp.int32), scaled, scaled_far, out_blocks)
    else:
        both = jnp.concatenate(
            [jnp.where(first, scaled, scaled_far), jnp.where(first, scaled_far, scaled)], axis=0
        )
        by_head = out_blocks.reshape(head_size, per_head, width, block)
        by_head = by_head.transpose(0, 2, 1, 3).reshape(head_size, width, half)
        product = lambda h: jnp.dot(both, pick(by_head, h), preferred_element_type=F32)
        sends = jnp.stack([product(h) for h in send_heads]).astype(BF16)
        keeps = [product(h) for h in keep_heads]
    received = c_swap(sends)
    crossing = x_swap((keeps[1] + received[1].astype(F32)).astype(BF16))
    partial_share = keeps[0] + received[0].astype(F32) + crossing.astype(F32)
    resid_new = (
        resid + partial_share * lax.rsqrt(square_one / inner_count + 1e-05)[:, None]
    ).astype(BF16)

    resid_back = y_swap(lax.dynamic_slice_in_dim(resid_new, (1 - y) * tokens, tokens, 0))
    resid_mine = lax.dynamic_slice_in_dim(resid_new, y * tokens, tokens, 0)
    if per_head == 1:
        (resid_out,) = whole_call(
            join_kernel,
            [shape((tokens, width), BF16)],
            resid_in.size,
            y[None].astype(jnp.int32),
            resid_mine,
            resid_back,
        )
    else:
        both = [jnp.where(first, resid_mine, resid_back), jnp.where(first, resid_back, resid_mine)]
        both = [a.reshape(tokens, per_head, block) for a in both]
        resid_out = jnp.stack(both, axis=2).reshape(tokens, width)

    gains = resid_gain.reshape(z_size, 2, block)
    gain = lax.dynamic_slice_in_dim(
        lax.dynamic_index_in_dim(gains, y, 1, False), head * per_head, per_head, 0
    ).reshape(half)
    hidden_wide = resid_new.astype(F32)
    hidden = (hidden_wide * gain[None, :]).astype(BF16)
    pair = jnp.stack([hidden, x_swap(hidden)])
    other = c_swap(pair)
    square_two = jnp.sum(hidden_wide * hidden_wide, axis=1)
    square_two = square_two + x_swap(square_two)
    square_two = square_two + c_swap(square_two)
    square_two = square_two + y_swap(square_two)
    all_hidden = jnp.stack([pair[0], other[0], pair[1], other[1]])
    halo_hidden = z_shift(all_hidden[:, pair_tokens - HALO :], 1)
    halo_square = z_shift(square_two[pair_tokens - HALO :], 1)
    all_hidden = jnp.concatenate([halo_hidden, all_hidden], axis=1)
    scale_two = lax.rsqrt(jnp.concatenate([halo_square, square_two]) / inner_count + 1e-05)

    reach = tokens + HALO
    keep_start = jnp.where(first, 0, tokens)
    send_start = tokens - keep_start
    columns = (half + small, half)
    if line:
        spots = [place ^ head for place in in_places]
        where = lambda start: jnp.stack([start] + spots).astype(jnp.int32)
        project = lambda place, start, kind: in_call(
            place, where(start), all_hidden, in_blocks, reach, columns[place], kind
        )
        theirs = [project(0, send_start, BF16), project(1, send_start, BF16)]
        mine = [project(0, keep_start, F32), project(1, keep_start, F32)]
    else:
        wide = jnp.concatenate([pick(all_hidden, head ^ i) for i in range(head_size)], axis=1)
        total = jnp.dot(
            wide, in_blocks.reshape(z_size * block, w_in.shape[1]), preferred_element_type=F32
        )
        total = [jnp.concatenate([total[:, :half], total[:, width:]], axis=1), total[:, half:width]]
        mine = [lax.dynamic_slice_in_dim(t, keep_start, reach, 0) for t in total]
        theirs = [lax.dynamic_slice_in_dim(t, send_start, reach, 0).astype(BF16) for t in total]
    scale_mine = lax.dynamic_slice_in_dim(scale_two, keep_start, reach, 0)[:, None]
    bc_taps = lax.dynamic_slice_in_dim(conv_bc, head * share, share, 1)
    taps = jnp.concatenate([conv_x[:, :half], bc_taps], axis=1).astype(F32)
    head_half = decay_code.shape[2] // 2
    far_a = y_swap(theirs[0])
    x_a, bc_share, step_a, step_b = conv_call(
        [
            shape((tokens, half), BF16),
            shape((tokens, share), BF16),
            shape((tokens, head_half), F32),
            shape((tokens, head_half), F32),
        ],
        mine[0],
        far_a,
        scale_mine,
        taps,
        step_time_bias[None, :],
    )
    (x_b,) = conv_call(
        [shape((tokens, half), BF16)],
        mine[1],
        y_swap(theirs[1]),
        scale_mine,
        conv_x[:, half:].astype(F32),
    )
    bc_pair = jnp.stack([bc_share, x_swap(bc_share)])
    bc_other = c_swap(bc_pair)
    bc_stack = jnp.stack([bc_pair[0], bc_other[0], bc_pair[1], bc_other[1]])
    bc_two = jnp.concatenate([pick(bc_stack, head ^ i) for i in range(head_size)], axis=1)

    mixed, squares = [], []
    for x, step, picked in (
        (x_a, step_a, slice(0, head_half)), (x_b, step_b, slice(head_half, None))
    ):
        code, rate = decay_code[1][:, picked], decay_rate[1][None, picked]
        first_two, end, payload = chunk_states(x, bc_two[:, :state_width], step, code, rate)
        within = within_blocks(x, bc_two, step, code, rate, skip_gain[1][None, picked])
        part, square = whole_call(
            last_kernel,
            [shape((tokens, half), F32), shape((1, tokens), F32)],
            4 * x.size * state_width,
            *exchange_states(end, payload, y, False),
            first_two,
            within,
            bc_two[:, state_width:],
            code,
            rate,
        )
        mixed.append(part)
        squares.append(square[0])
    square_last = lax.psum(squares[0] + squares[1], "head")
    scale_last = lax.rsqrt(square_last / inner_count + 1e-05)[:, None]
    mixer_out = jnp.concatenate([(part * scale_last).astype(BF16) for part in mixed], axis=1)
    return (resid_out, mixer_out)


def solution(mesh):
    in_specs = (
        P("seq", "head"),
        P("seq", "head"),
        P("seq", None),
        P("seq", "head"),
        P(None, "seq", "head"),
        P(None, "head"),
        P(None, "head"),
        P("head"),
        P("head", "seq"),
        P("seq", "head"),
        P(),
        P("seq", "head"),
        P("seq", None),
        P("seq", "head"),
        P("head"),
        P(None, "head"),
        P(),
    )
    out_specs = (P("seq", "head"), P("seq", "head"))

    return jax.shard_map(
        on_device, mesh=mesh, in_specs=in_specs, out_specs=out_specs, check_vma=False
    )
```

```python
import functools
import jax
import jax.numpy as jnp
from jax import lax
from jax.experimental import pallas as pl
from jax.experimental.pallas import tpu as pltpu
from jax.sharding import PartitionSpec as P

HEAD_CHANNELS = 64
GROUP = 256
HALO = 16
ROWS = 256
F32 = jnp.float32
BF16 = jnp.bfloat16


def z_shift(value, by, hops=1):
    n = lax.axis_size("seq")
    pairs = [
        (i, i + 2 * by)
        for i in range(n)
        if 0 <= i + 2 * by < n and 0 <= i - 2 * by * (hops - 1) < n
    ]
    return lax.ppermute(value, "seq", pairs)


def flip(value, axis, bit):
    n = lax.axis_size(axis)
    return lax.ppermute(value, axis, [(i, i ^ bit) for i in range(n)])


def y_swap(value):
    return flip(value, "seq", 1)


def x_swap(value):
    return flip(value, "head", 2)


def c_swap(value):
    return flip(value, "head", 1)


def z_line(value, place):
    ups, downs = [value], [value]
    for step in range(1, 4):
        ups.append(z_shift(ups[-1], 1, step))
        downs.append(z_shift(downs[-1], -1, step))
    early, low, high = place >= 1, place == 0, place == 3
    blocks = [
        value,
        jnp.where(early, ups[1], downs[1]),
        jnp.where(place >= 2, ups[2], downs[2]),
        jnp.where(low, downs[3], jnp.where(high, ups[3], downs[1])),
    ]
    places = [
        place,
        jnp.where(early, place - 1, 1),
        (place + 2) % 4,
        jnp.where(low, 3, jnp.where(high, 0, place + 1)),
    ]
    return blocks, places


def z_whole(value):
    size = lax.axis_size("seq") // 2
    groups = [[2 * i + y for i in range(size)] for y in range(2)]
    return lax.all_gather(value, "seq", axis_index_groups=groups)


HIGHEST = lax.Precision.HIGHEST
LOW = -1e30


def spread(heads):
    channels = heads * HEAD_CHANNELS
    row = lax.broadcasted_iota(jnp.int32, (heads, channels), 0)
    column = lax.broadcasted_iota(jnp.int32, (heads, channels), 1)
    return (column // HEAD_CHANNELS == row).astype(F32)


def exact_dot(a, b):
    return jnp.dot(a, b, precision=HIGHEST, preferred_element_type=F32)


def running_decay(code, rate):
    decay = -jnp.minimum(code.astype(F32) * rate, 20.0)
    rows = code.shape[0]
    lower = (
        lax.broadcasted_iota(jnp.int32, (rows, rows), 0)
        >= lax.broadcasted_iota(jnp.int32, (rows, rows), 1)
    ).astype(F32)
    return exact_dot(lower, decay)


def state_kernel(x_ref, b_ref, step_ref, code_ref, rate_ref, first_ref, end_ref, payload_ref):
    tokens, channels = x_ref.shape
    heads = channels // HEAD_CHANNELS
    table = spread(heads)
    end = None
    decay = jnp.zeros((1, heads), F32)
    for start in range(0, tokens, GROUP):
        rows = pl.ds(start, GROUP)
        total = running_decay(code_ref[rows, :], rate_ref[...])
        last = total[GROUP - 1 :, :]
        weight = exact_dot(jnp.exp(last - total) * step_ref[rows, :], table)
        v = (x_ref[rows, :].astype(F32) * weight).astype(BF16)
        term = lax.dot_general(
            b_ref[rows, :], v, (((0,), (0,)), ((), ())), preferred_element_type=F32
        )
        if end is None:
            first_ref[...] = term
            end = term
        else:
            end = end * exact_dot(jnp.exp(last), table) + term
        decay = decay + last
    end_ref[...] = end
    put_payload(payload_ref, end, exact_dot(decay, table))


def put_payload(payload_ref, state, wide):
    width, channels = state.shape
    payload_ref[:width, :] = state.astype(BF16)
    high = wide.astype(BF16)
    rest = wide - high.astype(F32)
    middle = rest.astype(BF16)
    low = rest - middle.astype(F32)
    row = lax.broadcasted_iota(jnp.int32, (16, channels), 0)
    tail = jnp.where(
        row == 0,
        high.astype(F32),
        jnp.where(row == 1, middle.astype(F32), jnp.where(row == 2, low, 0.0)),
    )
    payload_ref[width:, :] = tail.astype(BF16)


def get_payload(payload_ref):
    width = payload_ref.shape[0] - 16
    tail = payload_ref[width:, :].astype(F32)
    return payload_ref[:width, :].astype(F32), tail[0:1] + tail[1:2] + tail[2:3]


def pair_kernel(
    y_ref, end_ref, own_ref, far_ref, window_ref, payload_ref, early_ref, early_decay_ref
):
    first = y_ref[0] == 0
    own, own_decay = end_ref[...], get_payload(own_ref)[1]
    far, far_decay = get_payload(far_ref)
    early, early_decay = jnp.where(first, own, far), jnp.where(first, own_decay, far_decay)
    late, late_decay = jnp.where(first, far, own), jnp.where(first, far_decay, own_decay)
    window = jnp.exp(late_decay) * early + late
    decay = early_decay + late_decay
    half = window_ref.shape[1]
    if half < window.shape[1]:
        window = jnp.where(first, window[:, :half], window[:, half:])
        decay = jnp.where(first, decay[:, :half], decay[:, half:])
    window_ref[...] = window
    put_payload(payload_ref, window, decay)
    early_ref[...] = early
    early_decay_ref[...] = early_decay


def step_kernel(
    window_ref, own_ref, far_ref, before_ref, decay_ref, *outs
):
    window_out, payload_ref, before_out, decay_out = outs
    far, far_decay = get_payload(far_ref)
    own_decay = get_payload(own_ref)[1]
    window = jnp.exp(own_decay) * far + window_ref[...]
    window_out[...] = window
    put_payload(payload_ref, window, own_decay + far_decay)
    before_out[...] = before_ref[...] + jnp.exp(decay_ref[...]) * far
    decay_out[...] = decay_ref[...] + far_decay


def start_kernel(window_ref, own_ref, far_ref, *outs):
    window_out, payload_ref, before_out, decay_out = outs
    far, far_decay = get_payload(far_ref)
    own_decay = get_payload(own_ref)[1]
    window = jnp.exp(own_decay) * far + window_ref[...]
    window_out[...] = window
    put_payload(payload_ref, window, own_decay + far_decay)
    before_out[...] = far
    decay_out[...] = far_decay


def close_kernel(before_ref, decay_ref, far_ref, out_ref):
    far, _ = get_payload(far_ref)
    out_ref[...] = (before_ref[...] + jnp.exp(decay_ref[...]) * far).astype(BF16)


def entering_halves(y_ref, early_ref, early_decay_ref, own_ref, other_ref):
    first = y_ref[0] == 0
    own, other = own_ref[...].astype(F32), other_ref[...].astype(F32)
    before = jnp.concatenate(
        [jnp.where(first, own, other), jnp.where(first, other, own)], axis=1
    )
    late = jnp.exp(early_decay_ref[...]) * before + early_ref[...]
    return jnp.where(first, before, late)


def entering(y_ref, early_ref, early_decay_ref, before_ref, decay_ref, far_ref):
    far, _ = get_payload(far_ref)
    before = before_ref[...] + jnp.exp(decay_ref[...]) * far
    late = jnp.exp(early_decay_ref[...]) * before + early_ref[...]
    return jnp.where(y_ref[0] == 0, before, late)


def within_kernel(x_ref, bc_ref, step_ref, code_ref, rate_ref, skip_ref, out_ref):
    rows, channels = x_ref.shape
    heads = channels // HEAD_CHANNELS
    width = bc_ref.shape[1] // 2
    half = rows // 2
    total = running_decay(code_ref[...], rate_ref[...])
    across = total.T
    step = step_ref[...].T
    scores = lax.dot_general(
        bc_ref[:, width:],
        bc_ref[:, :width],
        (((1,), (1,)), ((), ())),
        preferred_element_type=F32,
    )
    skip = exact_dot(skip_ref[...], spread(heads))
    keep = lax.broadcasted_iota(jnp.int32, (half, half), 0) >= lax.broadcasted_iota(
        jnp.int32, (half, half), 1
    )
    lane = lax.broadcasted_iota(jnp.int32, (rows, 2 * HEAD_CHANNELS), 1)
    for pair in range(heads // 2):
        columns = pl.ds(pair * 2 * HEAD_CHANNELS, 2 * HEAD_CHANNELS)
        u = x_ref[:, columns]
        halves = []
        for h in (2 * pair, 2 * pair + 1):
            column = total[:, h : h + 1]
            line = across[h : h + 1, :]
            weight = step[h : h + 1, :]
            top = jnp.exp(jnp.where(keep, column[:half] - line[:, :half], LOW))
            top = (top * scores[:half, :half] * weight[:, :half]).astype(BF16)
            left = jnp.exp(column[half:] - line[:, :half])
            left = (left * scores[half:, :half] * weight[:, :half]).astype(BF16)
            right = jnp.exp(jnp.where(keep, column[half:] - line[:, half:], LOW))
            right = (right * scores[half:, half:] * weight[:, half:]).astype(BF16)
            upper = jnp.dot(top, u[:half], preferred_element_type=F32)
            lower = jnp.dot(
                jnp.concatenate([left, right], axis=1), u, preferred_element_type=F32
            )
            halves.append(jnp.concatenate([upper, lower], axis=0))
        mixed = jnp.where(lane < HEAD_CHANNELS, halves[0], halves[1])
        out_ref[:, columns] = mixed + skip[:, pair * 128 : pair * 128 + 128] * u.astype(F32)


def finish_group(start, state, within_ref, c_ref, code_ref, rate_ref, table):
    rows = pl.ds(start, GROUP)
    total = running_decay(code_ref[rows, :], rate_ref[...])
    c = c_ref[rows, :]
    high = state.astype(BF16)
    low = (state - high.astype(F32)).astype(BF16)
    carried = jnp.dot(
        jnp.concatenate([c, c], axis=1),
        jnp.concatenate([high, low], axis=0),
        preferred_element_type=F32,
    )
    mixed = within_ref[rows, :] + carried * exact_dot(jnp.exp(total), table)
    return mixed, exact_dot(jnp.exp(total[GROUP - 1 :, :]), table)


def gated_kernel(
    y_ref,
    early_ref,
    early_decay_ref,
    own_ref,
    other_ref,
    first_ref,
    within_ref,
    c_ref,
    code_ref,
    rate_ref,
    gate_ref,
    gain_ref,
    out_ref,
    square_ref,
):
    tokens, channels = within_ref.shape
    table = spread(channels // HEAD_CHANNELS)
    state = entering_halves(y_ref, early_ref, early_decay_ref, own_ref, other_ref)
    for start in range(0, tokens, GROUP):
        mixed, decay = finish_group(start, state, within_ref, c_ref, code_ref, rate_ref, table)
        state = state * decay + first_ref[...]
        gate = gate_ref[pl.ds(start, GROUP), :].astype(F32)
        gated = mixed * (gate / (1.0 + jnp.exp(-gate)))
        out_ref[pl.ds(start, GROUP), :] = (gated * gain_ref[...]).astype(BF16)
        square_ref[:, pl.ds(start, GROUP)] = jnp.sum(gated * gated, axis=1, keepdims=True).T


def last_kernel(
    y_ref,
    early_ref,
    early_decay_ref,
    before_ref,
    decay_ref,
    far_ref,
    first_ref,
    within_ref,
    c_ref,
    code_ref,
    rate_ref,
    out_ref,
    square_ref,
):
    tokens, channels = within_ref.shape
    table = spread(channels // HEAD_CHANNELS)
    state = entering(y_ref, early_ref, early_decay_ref, before_ref, decay_ref, far_ref)
    for start in range(0, tokens, GROUP):
        mixed, decay = finish_group(start, state, within_ref, c_ref, code_ref, rate_ref, table)
        state = state * decay + first_ref[...]
        out_ref[pl.ds(start, GROUP), :] = mixed
        square_ref[:, pl.ds(start, GROUP)] = jnp.sum(mixed * mixed, axis=1, keepdims=True).T


VMEM_SPEC = pl.BlockSpec(memory_space=pltpu.VMEM)
SMEM_SPEC = pl.BlockSpec(memory_space=pltpu.SMEM)


def whole_call(kernel, outs, flops, *args):
    moved = sum(a.size * a.dtype.itemsize for a in args)
    moved += sum(o.size * o.dtype.itemsize for o in outs)
    return pl.pallas_call(
        kernel,
        out_shape=outs,
        in_specs=[SMEM_SPEC if a.shape == (1,) else VMEM_SPEC for a in args],
        out_specs=[VMEM_SPEC] * len(outs),
        cost_estimate=pl.CostEstimate(flops=flops, bytes_accessed=moved, transcendentals=0),
        compiler_params=pltpu.CompilerParams(vmem_limit_bytes=16 * 2**20),
    )(*args)


def shape(dims, kind):
    return jax.ShapeDtypeStruct(dims, kind)


def chunk_states(x, b, step, code, rate):
    width, channels = b.shape[1], x.shape[1]
    return whole_call(
        state_kernel,
        [
            shape((width, channels), F32),
            shape((width, channels), F32),
            shape((width + 16, channels), BF16),
        ],
        4 * x.size * width,
        x,
        b,
        step,
        code,
        rate,
    )


def within_blocks(x, bc, step, code, rate, skip):
    tokens, channels = x.shape
    heads = step.shape[1]
    row = lambda cols: pl.BlockSpec((GROUP, cols), lambda i: (i, 0))
    one = pl.BlockSpec((1, heads), lambda i: (0, 0))
    return pl.pallas_call(
        within_kernel,
        name="within",
        grid=(tokens // GROUP,),
        out_shape=shape((tokens, channels), F32),
        in_specs=[row(channels), row(bc.shape[1]), row(heads), row(heads), one, one],
        out_specs=row(channels),
        cost_estimate=pl.CostEstimate(
            flops=16 * x.size * GROUP, bytes_accessed=8 * x.size, transcendentals=0
        ),
        compiler_params=pltpu.CompilerParams(vmem_limit_bytes=12 * 2**20),
    )(x, bc, step, code, rate, skip)


def convolved(mine_ref, far_ref, scale, taps_ref, pre_ref, start, size, tokens):
    rows, count = mine_ref.shape[0], taps_ref.shape[0]
    columns = pl.ds(start, size)
    pre = (mine_ref[:, columns] + far_ref[:, columns].astype(F32)) * scale
    pre_ref[:, :size] = pre.astype(BF16).astype(F32)
    total = None
    for tap in range(count):
        first = rows - tokens - count + 1 + tap
        part = pre_ref[pl.ds(first, tokens), :size] * taps_ref[tap : tap + 1, columns]
        total = part if total is None else total + part
    return (total / (1.0 + jnp.exp(-total))).astype(BF16)


def conv_kernel(mine_ref, far_ref, scale_ref, taps_ref, *refs):
    if len(refs) == 2:
        x_ref, pre_ref = refs
    else:
        bias_ref, x_ref, bc_ref, step_ref, late_ref, pre_ref = refs
    tokens, width = x_ref.shape
    scale = scale_ref[...]

    @pl.loop(0, width, step=128)
    def _(start):
        start = pl.multiple_of(start, 128)
        x_ref[:, pl.ds(start, 128)] = convolved(
            mine_ref, far_ref, scale, taps_ref, pre_ref, start, 128, tokens
        )

    if len(refs) > 2:
        share, heads = bc_ref.shape[1], step_ref.shape[1]
        bc_ref[...] = convolved(mine_ref, far_ref, scale, taps_ref, pre_ref, width, share, tokens)
        columns = pl.ds(width + share, 2 * heads)
        raw = (mine_ref[:, columns] + far_ref[:, columns].astype(F32)) * scale
        raw = raw[mine_ref.shape[0] - tokens :] + bias_ref[...]
        steps = jnp.maximum(raw, 0.0) + jnp.log1p(jnp.exp(-jnp.abs(raw)))
        step_ref[...] = steps[:, :heads]
        late_ref[...] = steps[:, heads:]


def conv_call(outs, mine, *args):
    return pl.pallas_call(
        conv_kernel,
        out_shape=outs,
        in_specs=[VMEM_SPEC] * (1 + len(args)),
        out_specs=[VMEM_SPEC] * len(outs),
        scratch_shapes=[pltpu.VMEM((mine.shape[0], 128), F32)],
        cost_estimate=pl.CostEstimate(
            flops=16 * mine.size, bytes_accessed=8 * mine.size, transcendentals=mine.size
        ),
        compiler_params=pltpu.CompilerParams(vmem_limit_bytes=12 * 2**20),
    )(mine, *args)


def out_kernel(where_ref, own_ref, far_ref, *refs):
    blocks, (send_ref, keep_ref) = refs[:4], refs[4:]
    tokens = own_ref.shape[0]
    own_start = pl.multiple_of(where_ref[0] * tokens, tokens)
    far_start = pl.multiple_of((1 - where_ref[0]) * tokens, tokens)
    for i, block_ref in enumerate(blocks):
        kept, spot = where_ref[2 * i + 1], where_ref[2 * i + 2]
        for ref, start in ((own_ref, own_start), (far_ref, far_start)):

            @pl.loop(0, tokens, step=ROWS)
            def _(row):
                row = pl.multiple_of(row, ROWS)
                product = jnp.dot(
                    ref[pl.ds(row, ROWS), :], block_ref[...], preferred_element_type=F32
                )

                @pl.when(kept == 1)
                def _():
                    keep_ref[spot, pl.ds(start + row, ROWS), :] = product

                @pl.when(kept == 0)
                def _():
                    send_ref[spot, pl.ds(start + row, ROWS), :] = product.astype(BF16)


def in_kernel(place, where_ref, hidden_ref, *refs):
    blocks, out_ref = refs[:4], refs[4]
    rows, columns = out_ref.shape
    depth = hidden_ref.shape[2]
    wide = blocks[0].shape[1] // 2

    @pl.loop(0, rows, step=rows // 3)
    def _(row):
        here = pl.ds(pl.multiple_of(row, HALO), rows // 3)
        there = pl.ds(pl.multiple_of(where_ref[0] + row, HALO), rows // 3)
        large, small = None, None
        for i, block_ref in enumerate(blocks):
            hidden = hidden_ref[where_ref[i + 1], there, :]
            weight = block_ref[:depth, place * wide : (place + 1) * wide]
            part = jnp.dot(hidden, weight, preferred_element_type=F32)
            large = part if large is None else large + part
            if columns > wide:
                packed = block_ref[depth:, :]
                part = lax.dot_general(
                    hidden,
                    jnp.concatenate([packed[:, :depth], packed[:, depth:]], axis=0),
                    (((1,), (1,)), ((), ())),
                    preferred_element_type=F32,
                )
                small = part if small is None else small + part
        out_ref[here, :wide] = large.astype(out_ref.dtype)
        if columns > wide:
            out_ref[here, wide:] = small[:, : columns - wide].astype(out_ref.dtype)


def out_call(where, own, far, blocks):
    tokens, depth = own.shape
    width = blocks[0].shape[1]
    return pl.pallas_call(
        out_kernel,
        name="out",
        out_shape=[shape((2, 2 * tokens, width), BF16), shape((2, 2 * tokens, width), F32)],
        in_specs=[SMEM_SPEC] + [VMEM_SPEC] * (2 + len(blocks)),
        out_specs=[VMEM_SPEC] * 2,
        cost_estimate=pl.CostEstimate(
            flops=16 * tokens * depth * width,
            bytes_accessed=4 * own.size + 8 * blocks[0].size,
            transcendentals=0,
        ),
        compiler_params=pltpu.CompilerParams(vmem_limit_bytes=16 * 2**20),
    )(where, own, far, *blocks)


def in_call(place, where, hidden, blocks, rows, columns, kind):
    count, _, depth = hidden.shape
    return pl.pallas_call(
        functools.partial(in_kernel, place),
        out_shape=shape((rows, columns), kind),
        in_specs=[SMEM_SPEC] + [VMEM_SPEC] * (1 + len(blocks)),
        out_specs=VMEM_SPEC,
        cost_estimate=pl.CostEstimate(
            flops=2 * count * rows * depth * columns,
            bytes_accessed=2 * (hidden.size + count * depth * columns),
            transcendentals=0,
        ),
        compiler_params=pltpu.CompilerParams(vmem_limit_bytes=16 * 2**20),
    )(where, hidden, *blocks)


def join_kernel(y_ref, mine_ref, back_ref, out_ref):
    first = y_ref[0] == 0
    half = mine_ref.shape[1]
    out_ref[:, :half] = jnp.where(first, mine_ref[...], back_ref[...])
    out_ref[:, half:] = jnp.where(first, back_ref[...], mine_ref[...])


def pick(stack, index):
    return lax.dynamic_index_in_dim(stack, index, 0, False)


def exchange_states(end, payload, y, split):
    part = end.shape[1] // 2 if split else end.shape[1]
    full, row = shape(end.shape, F32), shape((1, end.shape[1]), F32)
    piece, packed = shape((end.shape[0], part), F32), shape((payload.shape[0], part), BF16)
    piece_row = shape((1, part), F32)
    flag = y[None].astype(jnp.int32)
    far = y_swap(payload)
    window, payload, early, early_decay = whole_call(
        pair_kernel, [piece, packed, full, row], end.size, flag, end, payload, far
    )
    parts = ()
    reach, size = 1, lax.axis_size("seq") // 2
    while 2 * reach < size:
        far = z_shift(payload, reach)
        window, payload, *parts = whole_call(
            step_kernel if parts else start_kernel,
            [piece, packed, piece, piece_row],
            end.size,
            window,
            payload,
            far,
            *parts,
        )
        reach *= 2
    far = z_shift(payload, reach)
    if split:
        (own,) = whole_call(close_kernel, [shape(piece.shape, BF16)], end.size, *parts, far)
        return (flag, early, early_decay, own, y_swap(own))
    return (flag, early, early_decay, *parts, far)


def on_device(
    x_in,
    gate_in,
    bc_in,
    step_in,
    decay_code,
    decay_rate,
    skip_gain,
    norm_gain,
    w_out,
    resid_in,
    resid_gain,
    w_in_x,
    w_in_bc,
    w_in_dt,
    step_time_bias,
    conv_x,
    conv_bc,
):
    tokens, width = x_in.shape
    seq_size, head_size = lax.axis_size("seq"), lax.axis_size("head")
    z_size = seq_size // 2
    seq_place, head = lax.axis_index("seq"), lax.axis_index("head")
    z, y = seq_place // 2, seq_place % 2
    x_bit, c_bit = head // 2, head % 2
    inner_count = width * head_size
    pair_tokens = 2 * tokens
    state_width = bc_in.shape[1] // 2
    block = w_out.shape[1]
    half = width // 2
    per_head = z_size // head_size
    first = y == 0
    line = z_size == 4 and per_head == 1

    share = w_in_bc.shape[1] // head_size
    bc_weight = lax.dynamic_slice_in_dim(w_in_bc, head * share, share, 1)
    small = share + w_in_dt.shape[1]
    if line:
        below = jnp.concatenate([bc_weight, w_in_dt], axis=1).T
        below = jnp.concatenate([below, jnp.zeros((-small % 32, block), BF16)], axis=0)
        below = below.reshape(2, below.shape[0] // 2, block)
        below = jnp.concatenate([below[0], below[1]], axis=1)
        out_blocks, out_places = z_line(w_out, z)
        in_blocks, in_places = z_line(jnp.concatenate([w_in_x, below], axis=0), z)
    else:
        w_in = jnp.concatenate([w_in_x, bc_weight, w_in_dt], axis=1)
        out_blocks, in_blocks = z_whole(w_out), z_whole(w_in)

    def parity(array, which):
        if per_head == 1:
            return lax.dynamic_slice_in_dim(array, which * block, block, 1)
        parts = array.reshape(tokens, per_head, 2, block)
        return lax.dynamic_index_in_dim(parts, which, 2, False).reshape(tokens, half)

    resid_own = parity(resid_in, y)
    resid_far = y_swap(parity(resid_in, 1 - y))

    code_one, rate_one = decay_code[0], decay_rate[0][None, :]
    first_one, end_one, payload_one = chunk_states(
        x_in, bc_in[:, :state_width], step_in, code_one, rate_one
    )
    within_one = within_blocks(x_in, bc_in, step_in, code_one, rate_one, skip_gain[0][None, :])
    carried_one = exchange_states(end_one, payload_one, y, True)
    scaled, square_own = whole_call(
        gated_kernel,
        [shape((tokens, width), BF16), shape((1, tokens), F32)],
        4 * x_in.size * state_width,
        *carried_one,
        first_one,
        within_one,
        bc_in[:, state_width:],
        code_one,
        rate_one,
        gate_in,
        norm_gain[None, :],
    )
    scaled_far = y_swap(scaled)
    square_own = square_own + c_swap(square_own)
    square_own = square_own + x_swap(square_own)
    square_far = y_swap(square_own)
    square_one = jnp.concatenate(
        [jnp.where(first, square_own, square_far), jnp.where(first, square_far, square_own)], axis=1
    )[0]
    resid = jnp.concatenate(
        [jnp.where(first, resid_own, resid_far), jnp.where(first, resid_far, resid_own)], axis=0
    ).astype(F32)

    keep_heads = [2 * (x_bit ^ i) + c_bit for i in range(2)]
    send_heads = [2 * (x_bit ^ i) + (1 - c_bit) for i in range(2)]
    if line:
        where = [y]
        for place in out_places:
            where += [(place % 2 == c_bit).astype(jnp.int32), (place // 2) ^ x_bit]
        sends, keeps = out_call(jnp.stack(where).astype(jnp.int32), scaled, scaled_far, out_blocks)
    else:
        both = jnp.concatenate(
            [jnp.where(first, scaled, scaled_far), jnp.where(first, scaled_far, scaled)], axis=0
        )
        by_head = out_blocks.reshape(head_size, per_head, width, block)
        by_head = by_head.transpose(0, 2, 1, 3).reshape(head_size, width, half)
        product = lambda h: jnp.dot(both, pick(by_head, h), preferred_element_type=F32)
        sends = jnp.stack([product(h) for h in send_heads]).astype(BF16)
        keeps = [product(h) for h in keep_heads]
    received = c_swap(sends)
    crossing = x_swap((keeps[1] + received[1].astype(F32)).astype(BF16))
    partial_share = keeps[0] + received[0].astype(F32) + crossing.astype(F32)
    resid_new = (
        resid + partial_share * lax.rsqrt(square_one / inner_count + 1e-05)[:, None]
    ).astype(BF16)

    resid_back = y_swap(lax.dynamic_slice_in_dim(resid_new, (1 - y) * tokens, tokens, 0))
    resid_mine = lax.dynamic_slice_in_dim(resid_new, y * tokens, tokens, 0)
    if per_head == 1:
        (resid_out,) = whole_call(
            join_kernel,
            [shape((tokens, width), BF16)],
            resid_in.size,
            y[None].astype(jnp.int32),
            resid_mine,
            resid_back,
        )
    else:
        both = [jnp.where(first, resid_mine, resid_back), jnp.where(first, resid_back, resid_mine)]
        both = [a.reshape(tokens, per_head, block) for a in both]
        resid_out = jnp.stack(both, axis=2).reshape(tokens, width)

    gains = resid_gain.reshape(z_size, 2, block)
    gain = lax.dynamic_slice_in_dim(
        lax.dynamic_index_in_dim(gains, y, 1, False), head * per_head, per_head, 0
    ).reshape(half)
    hidden_wide = resid_new.astype(F32)
    hidden = (hidden_wide * gain[None, :]).astype(BF16)
    pair = jnp.stack([hidden, x_swap(hidden)])
    other = c_swap(pair)
    square_two = jnp.sum(hidden_wide * hidden_wide, axis=1)
    square_two = square_two + x_swap(square_two)
    square_two = square_two + c_swap(square_two)
    square_two = square_two + y_swap(square_two)
    all_hidden = jnp.stack([pair[0], other[0], pair[1], other[1]])
    halo = z_shift(hidden[pair_tokens - HALO :], 1)
    halo_pair = jnp.stack([halo, x_swap(halo)])
    halo_other = c_swap(halo_pair)
    halo_hidden = jnp.stack([halo_pair[0], halo_other[0], halo_pair[1], halo_other[1]])
    halo_square = z_shift(square_two[pair_tokens - HALO :], 1)
    all_hidden = jnp.concatenate([halo_hidden, all_hidden], axis=1)
    scale_two = lax.rsqrt(jnp.concatenate([halo_square, square_two]) / inner_count + 1e-05)

    reach = tokens + HALO
    keep_start = jnp.where(first, 0, tokens)
    send_start = tokens - keep_start
    columns = (half + small, half)
    if line:
        spots = [place ^ head for place in in_places]
        where = lambda start: jnp.stack([start] + spots).astype(jnp.int32)
        project = lambda place, start, kind: in_call(
            place, where(start), all_hidden, in_blocks, reach, columns[place], kind
        )
        theirs = [project(0, send_start, BF16), project(1, send_start, BF16)]
        mine = [project(0, keep_start, F32), project(1, keep_start, F32)]
    else:
        wide = jnp.concatenate([pick(all_hidden, head ^ i) for i in range(head_size)], axis=1)
        total = jnp.dot(
            wide, in_blocks.reshape(z_size * block, w_in.shape[1]), preferred_element_type=F32
        )
        total = [jnp.concatenate([total[:, :half], total[:, width:]], axis=1), total[:, half:width]]
        mine = [lax.dynamic_slice_in_dim(t, keep_start, reach, 0) for t in total]
        theirs = [lax.dynamic_slice_in_dim(t, send_start, reach, 0).astype(BF16) for t in total]
    scale_mine = lax.dynamic_slice_in_dim(scale_two, keep_start, reach, 0)[:, None]
    bc_taps = lax.dynamic_slice_in_dim(conv_bc, head * share, share, 1)
    taps = jnp.concatenate([conv_x[:, :half], bc_taps], axis=1).astype(F32)
    head_half = decay_code.shape[2] // 2
    far_a = y_swap(theirs[0])
    x_a, bc_share, step_a, step_b = conv_call(
        [
            shape((tokens, half), BF16),
            shape((tokens, share), BF16),
            shape((tokens, head_half), F32),
            shape((tokens, head_half), F32),
        ],
        mine[0],
        far_a,
        scale_mine,
        taps,
        step_time_bias[None, :],
    )
    (x_b,) = conv_call(
        [shape((tokens, half), BF16)],
        mine[1],
        y_swap(theirs[1]),
        scale_mine,
        conv_x[:, half:].astype(F32),
    )
    bc_pair = jnp.stack([bc_share, x_swap(bc_share)])
    bc_other = c_swap(bc_pair)
    bc_stack = jnp.stack([bc_pair[0], bc_other[0], bc_pair[1], bc_other[1]])
    bc_two = jnp.concatenate([pick(bc_stack, head ^ i) for i in range(head_size)], axis=1)

    mixed, squares = [], []
    for x, step, picked in (
        (x_a, step_a, slice(0, head_half)), (x_b, step_b, slice(head_half, None))
    ):
        code, rate = decay_code[1][:, picked], decay_rate[1][None, picked]
        first_two, end, payload = chunk_states(x, bc_two[:, :state_width], step, code, rate)
        within = within_blocks(x, bc_two, step, code, rate, skip_gain[1][None, picked])
        part, square = whole_call(
            last_kernel,
            [shape((tokens, half), F32), shape((1, tokens), F32)],
            4 * x.size * state_width,
            *exchange_states(end, payload, y, False),
            first_two,
            within,
            bc_two[:, state_width:],
            code,
            rate,
        )
        mixed.append(part)
        squares.append(square[0])
    square_last = lax.psum(squares[0] + squares[1], "head")
    scale_last = lax.rsqrt(square_last / inner_count + 1e-05)[:, None]
    mixer_out = jnp.concatenate([(part * scale_last).astype(BF16) for part in mixed], axis=1)
    return (resid_out, mixer_out)


def solution(mesh):
    in_specs = (
        P("seq", "head"),
        P("seq", "head"),
        P("seq", None),
        P("seq", "head"),
        P(None, "seq", "head"),
        P(None, "head"),
        P(None, "head"),
        P("head"),
        P("head", "seq"),
        P("seq", "head"),
        P(),
        P("seq", "head"),
        P("seq", None),
        P("seq", "head"),
        P("head"),
        P(None, "head"),
        P(),
    )
    out_specs = (P("seq", "head"), P("seq", "head"))

    return jax.shard_map(
        on_device, mesh=mesh, in_specs=in_specs, out_specs=out_specs, check_vma=False
    )
```
